32 devices in a mesh: dev: 32 (over z, y, x, core).
Axes of the slice: x: 2, y: 2, z: 4, core: 2. Of those that a mesh axis runs over, the one named last changes fastest.
Arguments:
- tokens: bfloat16 [32768, 1024], P('dev'), may hold values from -6 to 6
- cotangent: bfloat16 [32768, 1024], P('dev'), may hold values from -6 to 6
- padding: int32 [32768], P('dev'), may hold values from 0 to 1, as said below
- image_ident: int32 [32768], P('dev'), may hold values from 0 to 48, as said below
- ln1_gain: bfloat16 [1024], P('dev'), may hold values from 0.5 to 1.5
- ln1_bias: bfloat16 [1024], P('dev'), may hold values from -3 to 3
- w_qkv: bfloat16 [1024, 3072], P('dev'), may hold values from -0.1875 to 0.1875
- b_qv: bfloat16 [2048], P('dev'), may hold values from -0.59765625 to 0.59765625
- w_out: bfloat16 [1024, 1024], P('dev'), may hold values from -2.5 to 2.5
- b_out: bfloat16 [1024], P('dev'), may hold values from -3 to 3
- ln2_gain: bfloat16 [1024], P('dev'), may hold values from 0.5 to 1.5
- ln2_bias: bfloat16 [1024], P('dev'), may hold values from -3 to 3
- w_fc: bfloat16 [4096, 1024], P('dev'), may hold values from -0.1875 to 0.1875
- b_fc: bfloat16 [4096], P('dev'), may hold values from -3 to 3
- w_proj: bfloat16 [4096, 1024], P('dev'), may hold values from -0.09375 to 0.09375
- b_proj: bfloat16 [1024], P('dev'), may hold values from -3 to 3
Outputs:
- output: bfloat16 [32768, 1024], P('dev')
- grad_tokens: bfloat16 [32768, 1024], P('dev')
- grad_ln1_gain: float32 [1024], P('dev')
- grad_ln1_bias: float32 [1024], P('dev')
- grad_w_qkv: float32 [1024, 3072], P('dev')
- grad_b_qv: float32 [2048], P('dev')
- grad_w_out: float32 [1024, 1024], P('dev')
- grad_b_out: float32 [1024], P('dev')
- grad_ln2_gain: float32 [1024], P('dev')
- grad_ln2_bias: float32 [1024], P('dev')
- grad_w_fc: float32 [4096, 1024], P('dev')
- grad_b_fc: float32 [4096], P('dev')
- grad_w_proj: float32 [4096, 1024], P('dev')
- grad_b_proj: float32 [1024], P('dev')
The draws below stay inside these ranges and needn't reach their ends.
Inputs may be any that keep to these rules, and one draw needn't show every extreme that they name: The stream holds 49 images of exactly 577 consecutive tokens, in the order of their ids, with padding tokens between, before and after them. `image_ident`: each image's id is shared by its 577 tokens and by no other image token; a padding token carries the id of the last image before it, or 0 before the first.
All inputs are finite; a program needn't handle non-finite values.
Results may differ from the reference program's by a relative error of at most 0.012.
Values may be sent and summed in bfloat16 or wider, within the bound.
No kernel may reach another device: no remote copies, remote signals or barrier semaphores. Data moves between devices by JAX's collectives and lax.ppermute only.
A program may use at most 448 MiB of HBM per device.

```python
from functools import partial
import jax
import jax.numpy as jnp
from jax import lax

HEADS = 16
HEAD_DIM = 64
D = 1024
FF = 4096
IMG = 577
TOK_DEV = 1024
TOKENS = 32768
IMAGES = 49


def stream_layout(key):
    gap_count = IMAGES + 1
    spare_tokens = TOKENS - IMAGES * IMG
    gap_choice = jax.random.randint(jax.random.fold_in(key, 11), (spare_tokens,), 0, gap_count)
    gap_sizes = jnp.zeros((gap_count,), jnp.int32).at[gap_choice].add(1)
    pads_before = jnp.cumsum(gap_sizes)[:IMAGES]
    image_starts = jnp.arange(IMAGES, dtype=jnp.int32) * IMG + pads_before
    places = jnp.arange(TOKENS, dtype=jnp.int32)
    owner_index = jnp.searchsorted(image_starts, places, side='right').astype(jnp.int32) - 1
    clipped = jnp.maximum(owner_index, 0)
    inside = (owner_index >= 0) & (places < jnp.take(image_starts, clipped) + IMG)
    return (inside.astype(jnp.int32), clipped.astype(jnp.int32))


def draw_padding(key, part):
    return stream_layout(key)[0]


def draw_image_ident(key, part):
    return stream_layout(key)[1]


def strengthened(drawn, stream_key, source, target, parts, factor):
    owner, partner = [(jnp.arange(drawn.shape[dim]) // (drawn.shape[dim] // parts)).reshape([-1 if axis == dim else 1 for axis in range(drawn.ndim)]) for dim in (source, target)]
    chosen = jax.random.permutation(stream_key, parts)[partner]
    strong = (owner == chosen) | (owner == (partner + parts // 2) % parts)
    return jnp.where(strong, factor * drawn, drawn)


def block_levels(stream_key, dims, pieces, smallest, high):
    def one(position, blocks):
        draws = jax.random.uniform(jax.random.fold_in(jax.random.fold_in(stream_key, 6), position), (blocks,), jnp.float32, smallest / len(pieces), high / len(pieces))
        return jnp.repeat(jnp.exp(draws), dims[position] // blocks).reshape((-1,) + (1,) * (len(dims) - position - 1))

    factor_of = one(*pieces[0])
    for cut in pieces[1:]:
        factor_of = factor_of * one(*cut)
    return factor_of


def gaussian(own_key, shape, scale, bound, split=(), kind=jnp.bfloat16):
    loudness = block_levels(own_key, shape, split, -0.22, 0.18) if split else 1.0
    entries = jax.random.normal(own_key, shape, jnp.float32) * scale * loudness
    return jnp.minimum(jnp.maximum(entries, -bound), bound).astype(kind)


def heavy_noise(stream_key, extent, scale, bound, shards, heavy, kind=jnp.bfloat16):
    values = scale * jax.random.normal(stream_key, extent, jnp.float32)
    if shards:
        values = values * block_levels(stream_key, extent, shards, -0.22, 0.18)
    return jnp.clip(strengthened(values, jax.random.fold_in(stream_key, 3), *heavy), -bound, bound).astype(kind)


def setup_inputs(seed: int = 0) -> dict:
    keys = jax.random.split(jax.random.key(seed), 17)
    tokens = heavy_noise(keys[0], (TOKENS, D), 1.0, 6.0, ((0, 32),), (0, 1, 32, 2.75))
    cotangent = gaussian(keys[1], (TOKENS, D), 1.0, 6.0, ((0, 32),))
    padding = draw_padding(jax.random.fold_in(keys[16], 71), 0)
    image_ident = draw_image_ident(jax.random.fold_in(keys[16], 71), 0)
    ln1_gain = jnp.clip(1.0 + 0.1 * jax.random.normal(keys[4], (D,), jnp.float32), 0.5, 1.5).astype(jnp.bfloat16)
    ln1_bias = gaussian(keys[5], (D,), 0.5, 3.0, ((0, 32),))
    w_qkv = gaussian(keys[6], (D, 3 * D), D ** -0.5, 0.1875, ((0, 32),))
    b_qv = gaussian(keys[7], (2 * D,), 0.1, 0.59765625, ((0, 32),))
    w_out = gaussian(keys[8], (D, D), (3 * D // IMG) ** -0.5, 2.5, ((0, 32),))
    b_out = gaussian(keys[9], (D,), 0.5, 3.0, ((0, 32),))
    ln2_gain = jnp.clip(1.0 + 0.1 * jax.random.normal(keys[10], (D,), jnp.float32), 0.5, 1.5).astype(jnp.bfloat16)
    ln2_bias = gaussian(keys[11], (D,), 0.5, 3.0, ((0, 32),))
    w_fc = gaussian(keys[12], (FF, D), D ** -0.5, 0.1875, ((0, 32),))
    b_fc = gaussian(keys[13], (FF,), 0.5, 3.0, ((0, 32),))
    w_proj = gaussian(keys[14], (FF, D), FF ** -0.5, 0.09375, ((0, 32),))
    b_proj = gaussian(keys[15], (D,), 0.5, 3.0, ((0, 32),))
    return dict(tokens=tokens, cotangent=cotangent, padding=padding, image_ident=image_ident, ln1_gain=ln1_gain, ln1_bias=ln1_bias, w_qkv=w_qkv, b_qv=b_qv, w_out=w_out, b_out=b_out, ln2_gain=ln2_gain, ln2_bias=ln2_bias, w_fc=w_fc, b_fc=b_fc, w_proj=w_proj, b_proj=b_proj)


@jax.custom_vjp
def low(v):
    return lax.optimization_barrier(v.astype(jnp.bfloat16)).astype(jnp.float32)

@jax.custom_vjp
def low_back(v):
    return v

def low_keep(v):
    return (low(v), None)

def low_pass(kept, grad):
    return (grad,)

def back_keep(v):
    return (v, None)

def back_low(kept, grad):
    return (low(grad),)
low.defvjp(low_keep, low_pass)
low_back.defvjp(back_keep, back_low)

def layer_norm(values, norm_gain, norm_shift):
    centered = values - lax.optimization_barrier(jnp.mean(values, axis=-1, keepdims=True))
    spread = lax.optimization_barrier(jnp.mean(centered * centered, axis=-1, keepdims=True))
    return centered * lax.rsqrt(spread + 1e-05) * norm_gain + norm_shift

def quick_gelu(values):
    return values * jax.nn.sigmoid(1.702 * values)

def product(matrix_one, matrix_two):
    return jnp.dot(matrix_one, matrix_two, precision=lax.Precision.HIGHEST, preferred_element_type=jnp.float32)

def forward(padding, image_ident, tokens, ln1_gain, ln1_bias, w_qkv, b_qv, w_out, b_out, ln2_gain, ln2_bias, w_fc, b_fc, w_proj, b_proj):
    model_width = HEADS * HEAD_DIM
    rim_rows = IMG - 1
    window_rows = TOK_DEV + 2 * rim_rows
    normed_one = low(layer_norm(tokens, ln1_gain, ln1_bias))
    mixed_proj = product(normed_one, w_qkv)
    queries = low(low_back(mixed_proj[:, :model_width] + b_qv[:model_width]))
    keys_all = low(low_back(mixed_proj[:, model_width:2 * model_width]))
    values_all = low(low_back(mixed_proj[:, 2 * model_width:] + b_qv[model_width:]))
    keys_padded = jnp.pad(keys_all, ((rim_rows, rim_rows), (0, 0)))
    values_padded = jnp.pad(values_all, ((rim_rows, rim_rows), (0, 0)))
    ident_padded = jnp.pad(image_ident, (rim_rows, rim_rows), constant_values=-1)
    mask_padded = jnp.pad(padding, (rim_rows, rim_rows))

    def attend(block_index):
        first_row = (block_index * TOK_DEV).astype(jnp.int32)
        query_block = lax.dynamic_slice_in_dim(queries, first_row, TOK_DEV, 0).reshape(TOK_DEV, HEADS, HEAD_DIM)
        key_block = lax.dynamic_slice_in_dim(keys_padded, first_row, window_rows, 0).reshape(window_rows, HEADS, HEAD_DIM)
        value_block = lax.dynamic_slice_in_dim(values_padded, first_row, window_rows, 0).reshape(window_rows, HEADS, HEAD_DIM)
        query_ident = lax.dynamic_slice_in_dim(image_ident, first_row, TOK_DEV, 0)
        key_ident = lax.dynamic_slice_in_dim(ident_padded, first_row, window_rows, 0)
        key_mask = lax.dynamic_slice_in_dim(mask_padded, first_row, window_rows, 0)
        allowed = (key_ident[None, :] == query_ident[:, None]) & (key_mask[None, :] == 1)
        scores = jnp.einsum('qhd,khd->hqk', query_block, key_block, precision=lax.Precision.HIGHEST) * HEAD_DIM ** (-0.5)
        scores = low_back(scores)
        scores = jnp.where(allowed[None], scores, -1e+30)
        row_peak = lax.optimization_barrier(jnp.max(scores, axis=-1, keepdims=True))
        log_total = row_peak + jnp.log(lax.optimization_barrier(jnp.sum(jnp.exp(scores - row_peak), axis=-1, keepdims=True)))
        soft_weights = low(jnp.exp(scores - log_total))
        mixed_heads = jnp.einsum('hqk,khd->qhd', soft_weights, value_block, precision=lax.Precision.HIGHEST)
        return mixed_heads.reshape(TOK_DEV, model_width)
    attended = lax.map(jax.checkpoint(attend), jnp.arange(TOKENS // TOK_DEV, dtype=jnp.int32))
    attended = low(low_back(attended.reshape(TOKENS, model_width)))
    branch = low_back(product(attended, w_out) + b_out)
    middle = tokens + branch
    normed_two = low(layer_norm(middle, ln2_gain, ln2_bias))
    hidden = low_back(jnp.dot(normed_two, w_fc.T, precision=lax.Precision.HIGHEST, preferred_element_type=jnp.float32) + b_fc)
    gelu_out = low(quick_gelu(hidden))
    result = middle + product(gelu_out, w_proj) + b_proj
    return padding[:, None].astype(jnp.float32) * result

def reference(tokens, cotangent, padding, image_ident, ln1_gain, ln1_bias, w_qkv, b_qv, w_out, b_out, ln2_gain, ln2_bias, w_fc, b_fc, w_proj, b_proj):
    float_args = (tokens.astype(jnp.float32), ln1_gain.astype(jnp.float32), ln1_bias.astype(jnp.float32), w_qkv.astype(jnp.float32), b_qv.astype(jnp.float32), w_out.astype(jnp.float32), b_out.astype(jnp.float32), ln2_gain.astype(jnp.float32), ln2_bias.astype(jnp.float32), w_fc.astype(jnp.float32), b_fc.astype(jnp.float32), w_proj.astype(jnp.float32), b_proj.astype(jnp.float32))
    output, pullback = jax.vjp(partial(forward, padding, image_ident), *float_args)
    gradients = pullback(cotangent.astype(jnp.float32))
    return (output.astype(jnp.bfloat16), gradients[0].astype(jnp.bfloat16), gradients[1], gradients[2], gradients[3], gradients[4], gradients[5], gradients[6], gradients[7], gradients[8], gradients[9], gradients[10], gradients[11], gradients[12])
```

```python
import jax
import jax.numpy as jnp
from jax import lax
from jax.experimental import pallas as pl
from jax.experimental.pallas import tpu as pltpu
from jax.sharding import PartitionSpec as P

HEAD_DIM = 64
IMG = 577
RIM = IMG - 1
TILE = 128
KEYS = 592
LANES = 256
MASKED = -1e30
NOWHERE = 1 << 20


def dot_nt(a, b):
    return lax.dot_general(a, b, (((1,), (1,)), ((), ())), preferred_element_type=jnp.float32)


def dot_tn(a, b):
    return lax.dot_general(a, b, (((0,), (0,)), ((), ())), preferred_element_type=jnp.float32)


def dot_nn(a, b):
    return lax.dot_general(a, b, (((1,), (0,)), ((), ())), preferred_element_type=jnp.float32)


def paired(block):
    first = lax.broadcasted_iota(jnp.int32, block.shape, 1) < HEAD_DIM
    none = jnp.zeros_like(block)
    return jnp.concatenate([jnp.where(first, block, none), jnp.where(first, none, block)], axis=0)


def unpaired(wide):
    both = jnp.concatenate([wide[:HEAD_DIM, :TILE], wide[HEAD_DIM:, TILE:]], axis=0)
    return both.T


def key_window(first, ext_rows):
    low = first + RIM
    start = jnp.clip((low // 16) * 16, 0, ext_rows - KEYS)
    return pl.multiple_of(start, 16), low - start


def keep_image(scores, offset):
    edge = lax.broadcasted_iota(jnp.int32, (16, scores.shape[1]), 0)
    top = jnp.where(edge >= offset, scores[:16], MASKED)
    low = jnp.where(edge + (KEYS - 16) < offset + IMG, scores[KEYS - 16 :], MASKED)
    return jnp.concatenate([top, scores[16 : KEYS - 16], low], axis=0)


def attend_body(first_ref, q_ref, k_ref, v_ref, out_ref, lse_ref):
    rows = q_ref.shape[0]
    tiles = rows // TILE

    def tile(j, carry):
        at = pl.multiple_of(j * TILE, TILE)
        here = pl.ds(at, TILE)

        def item(first, pair):
            lanes = slice(pair * 128, pair * 128 + 128)
            start, offset = key_window(first, k_ref.shape[0])
            scores = dot_nt(k_ref[pl.ds(start, KEYS), lanes], paired(q_ref[here, lanes]))
            scores = keep_image(scores, offset)
            peak = jnp.max(scores, axis=0, keepdims=True)
            weights = jnp.exp(scores - peak)
            total = jnp.sum(weights, axis=0, keepdims=True)
            mixed = dot_tn(v_ref[pl.ds(start, KEYS), lanes], weights.astype(jnp.bfloat16))
            mixed = unpaired(mixed / total)
            row = lax.broadcasted_iota(jnp.int32, (TILE, 128), 0) + at
            inside = (row >= first) & (row < first + IMG)
            return jnp.where(inside, mixed, 0.0).astype(jnp.bfloat16), peak + jnp.log(total)

        one, two = first_ref[j], first_ref[tiles + j]
        for pair in range(LANES // 128):
            mixed, lse = item(one, pair)
            out_ref[here, pair * 128 : pair * 128 + 128] = mixed
            lse_ref[0, 2 * pair : 2 * pair + 1, here] = lse[:, :TILE]
            lse_ref[0, 2 * pair + 1 : 2 * pair + 2, here] = lse[:, TILE:]

        @pl.when(two != one)
        def _():
            column = lax.broadcasted_iota(jnp.int32, (1, TILE), 1) + at
            inside = (column >= two) & (column < two + IMG)
            for pair in range(LANES // 128):
                lanes = slice(pair * 128, pair * 128 + 128)
                mixed, lse = item(two, pair)
                out_ref[here, lanes] = out_ref[here, lanes] + mixed
                for head in range(2):
                    line = slice(2 * pair + head, 2 * pair + head + 1)
                    new = lse[:, head * TILE : head * TILE + TILE]
                    lse_ref[0, line, here] = jnp.where(inside, new, lse_ref[0, line, here])

        return carry

    lax.fori_loop(0, tiles, tile, 0)


def attend_back_body(
    first_ref, q_ref, k_ref, v_ref, grad_ref, lse_ref, dq_ref, dk_ref, dv_ref, dk_sum, dv_sum
):
    rows = q_ref.shape[0]
    tiles = rows // TILE
    dk_sum[...] = jnp.zeros_like(dk_sum)
    dv_sum[...] = jnp.zeros_like(dv_sum)

    def tile(j, carry):
        at = pl.multiple_of(j * TILE, TILE)
        here = pl.ds(at, TILE)
        column = lax.broadcasted_iota(jnp.int32, (1, TILE), 1) + at

        def item(first, pair):
            lanes = slice(pair * 128, pair * 128 + 128)
            start, offset = key_window(first, k_ref.shape[0])
            window = pl.ds(start, KEYS)
            keys = k_ref[window, lanes]
            queries = paired(q_ref[here, lanes])
            grads = paired(grad_ref[here, lanes])
            inside = (column >= first) & (column < first + IMG)
            lse = jnp.concatenate(
                [
                    jnp.where(inside, lse_ref[0, 2 * pair : 2 * pair + 1, here], -MASKED),
                    jnp.where(inside, lse_ref[0, 2 * pair + 1 : 2 * pair + 2, here], -MASKED),
                ],
                axis=1,
            )
            probs = jnp.exp(keep_image(dot_nt(keys, queries), offset) - lse)
            grad_probs = dot_nt(v_ref[window, lanes], grads)
            dv_sum[window, lanes] += dot_nn(probs.astype(jnp.bfloat16), grads)
            inner = jnp.sum(grad_probs * probs, axis=0, keepdims=True)
            grad_scores = (probs * (grad_probs - inner)).astype(jnp.bfloat16)
            dk_sum[window, lanes] += dot_nn(grad_scores, queries)
            return unpaired(dot_tn(keys, grad_scores) * HEAD_DIM**-0.5).astype(jnp.bfloat16)

        one, two = first_ref[j], first_ref[tiles + j]
        for pair in range(LANES // 128):
            dq_ref[here, pair * 128 : pair * 128 + 128] = item(one, pair)

        @pl.when(two != one)
        def _():
            for pair in range(LANES // 128):
                lanes = slice(pair * 128, pair * 128 + 128)
                dq_ref[here, lanes] = dq_ref[here, lanes] + item(two, pair)

        return carry

    lax.fori_loop(0, tiles, tile, 0)
    dk_ref[...] = dk_sum[...].astype(jnp.bfloat16)
    dv_ref[...] = dv_sum[...].astype(jnp.bfloat16)


def attention_cost(rows, width, products):
    return pl.CostEstimate(
        flops=2 * products * 10 * TILE * KEYS * width,
        bytes_accessed=16 * rows * width,
        transcendentals=10 * TILE * KEYS * (width // HEAD_DIM),
    )


def attend(firsts, queries, key_vals):
    rows, width = queries.shape
    ext = key_vals.shape[0]
    groups = width // LANES
    return pl.pallas_call(
        attend_body,
        grid_spec=pltpu.PrefetchScalarGridSpec(
            num_scalar_prefetch=1,
            grid=(groups,),
            in_specs=[
                pl.BlockSpec((rows, LANES), lambda g, f: (0, g)),
                pl.BlockSpec((ext, LANES), lambda g, f: (0, g)),
                pl.BlockSpec((ext, LANES), lambda g, f: (0, g + groups)),
            ],
            out_specs=[
                pl.BlockSpec((rows, LANES), lambda g, f: (0, g)),
                pl.BlockSpec((1, LANES // HEAD_DIM, rows), lambda g, f: (g, 0, 0)),
            ],
        ),
        out_shape=[
            jax.ShapeDtypeStruct((rows, width), jnp.bfloat16),
            jax.ShapeDtypeStruct((groups, LANES // HEAD_DIM, rows), jnp.float32),
        ],
        cost_estimate=attention_cost(rows, width, 2),
        name="attend",
    )(firsts, queries, key_vals, key_vals)


def attend_back(firsts, queries, key_vals, grads, lse):
    rows, width = queries.shape
    ext = key_vals.shape[0]
    groups = width // LANES
    own = pl.BlockSpec((rows, LANES), lambda g, f: (0, g))
    wide = pl.BlockSpec((ext, LANES), lambda g, f: (0, g))
    return pl.pallas_call(
        attend_back_body,
        grid_spec=pltpu.PrefetchScalarGridSpec(
            num_scalar_prefetch=1,
            grid=(groups,),
            in_specs=[
                own,
                wide,
                pl.BlockSpec((ext, LANES), lambda g, f: (0, g + groups)),
                own,
                pl.BlockSpec((1, LANES // HEAD_DIM, rows), lambda g, f: (g, 0, 0)),
            ],
            out_specs=[own, wide, wide],
            scratch_shapes=[pltpu.VMEM((ext, LANES), jnp.float32)] * 2,
        ),
        out_shape=[
            jax.ShapeDtypeStruct((rows, width), jnp.bfloat16),
            jax.ShapeDtypeStruct((ext, width), jnp.bfloat16),
            jax.ShapeDtypeStruct((ext, width), jnp.bfloat16),
        ],
        cost_estimate=attention_cost(rows, width, 5),
        name="attend_back",
    )(firsts, queries, key_vals, key_vals, grads, lse)


def image_firsts(padding, ident):
    rows = padding.shape[0]
    tiles = rows // TILE
    real = padding == 1
    by_tile = jnp.where(real, ident, NOWHERE).reshape(tiles, TILE)
    low_id = jnp.min(by_tile, axis=1)
    high_id = jnp.max(jnp.where(real, ident, -1).reshape(tiles, TILE), axis=1)
    wanted = jnp.concatenate([low_id, high_id])
    place = jnp.arange(rows, dtype=jnp.int32)[None, :]
    mine = real[None, :] & (ident[None, :] == wanted[:, None])
    run_first = jnp.min(jnp.where(mine, place, NOWHERE), axis=1)
    run_last = jnp.max(jnp.where(mine, place, -1), axis=1)
    firsts = jnp.where(run_last < rows - 1, run_last - RIM, run_first)
    empty = jnp.concatenate([low_id, low_id]) == NOWHERE
    before = jnp.tile(jnp.arange(tiles, dtype=jnp.int32) * TILE - IMG, 2)
    return jnp.where(empty, before, firsts)


def normed_parts(values):
    centered = values - jnp.mean(values, axis=-1, keepdims=True)
    spread = jnp.mean(centered * centered, axis=-1, keepdims=True)
    scale = lax.rsqrt(spread + 1e-05)
    return centered * scale, scale


def norm_back(unit, scale, gain, grads):
    scaled = grads * gain
    return scale * (
        scaled
        - jnp.mean(scaled, axis=-1, keepdims=True)
        - unit * jnp.mean(scaled * unit, axis=-1, keepdims=True)
    )


def quick_gelu(values):
    return values * jax.nn.sigmoid(1.702 * values)


def shifted(value, by):
    size = lax.axis_size("dev")
    pairs = [(i, i + by) for i in range(size) if 0 <= i + by < size]
    return lax.ppermute(value, "dev", pairs)


def shards(
    tokens,
    cotangent,
    padding,
    image_ident,
    ln1_gain,
    ln1_bias,
    w_qkv,
    b_qv,
    w_out,
    b_out,
    ln2_gain,
    ln2_bias,
    w_fc,
    b_fc,
    w_proj,
    b_proj,
):
    low = jnp.bfloat16
    wide = jnp.float32
    size = lax.axis_size("dev")
    width = w_out.shape[1]
    rows = tokens.shape[0]
    feat_rows = w_qkv.shape[0]
    smalls = (ln1_gain, ln1_bias, b_qv, b_out, ln2_gain, ln2_bias, b_fc, b_proj)
    small_all = jnp.concatenate(smalls)
    extra = 128 * -(-small_all.shape[0] // (128 * feat_rows))
    side = jnp.pad(small_all, (0, feat_rows * extra - small_all.shape[0])).reshape(feat_rows, extra)
    qkv_side = lax.all_gather(
        jnp.concatenate([w_qkv, side], axis=1), "dev", axis=0, tiled=True
    )
    full_out = lax.all_gather(w_out, "dev", axis=0, tiled=True)
    full_fc = lax.all_gather(w_fc, "dev", axis=0, tiled=True)
    full_proj = lax.all_gather(w_proj, "dev", axis=0, tiled=True)
    full_qkv = qkv_side[:, : 3 * width]
    side_all = qkv_side[:, 3 * width :].reshape(size, feat_rows * extra).astype(wide)
    vectors = []
    place = 0
    for small in smalls:
        vectors.append(side_all[:, place : place + small.shape[0]].reshape(-1))
        place += small.shape[0]
    gain_one, bias_one, bias_qv, bias_out, gain_two, bias_two, bias_fc, bias_proj = vectors

    firsts = image_firsts(padding, image_ident)
    ext_tokens = jnp.concatenate(
        [shifted(tokens[rows - RIM :], 1), tokens, shifted(tokens[:RIM], -1)], axis=0
    )
    unit_one, scale_one = normed_parts(ext_tokens.astype(wide))
    normed_one = (unit_one * gain_one + bias_one).astype(low)
    normed_own = normed_one[RIM : RIM + rows]
    queries = (
        (dot_nn(normed_own, full_qkv[:, :width]) + bias_qv[:width]).astype(low)
        * HEAD_DIM**-0.5
    ).astype(low)
    kv_bias = jnp.concatenate([jnp.zeros((width,), wide), bias_qv[width:]])
    key_vals = (dot_nn(normed_one, full_qkv[:, width:]) + kv_bias).astype(low)
    attended, lse = attend(firsts, queries, key_vals)

    middle = tokens.astype(wide) + (dot_nn(attended, full_out) + bias_out)
    unit_two, scale_two = normed_parts(middle)
    normed_two = (unit_two * gain_two + bias_two).astype(low)
    hidden = dot_nt(normed_two, full_fc) + bias_fc
    gelu_out, gelu_pull = jax.vjp(quick_gelu, hidden)
    gelu_low = gelu_out.astype(low)
    keep = padding.astype(wide)[:, None]
    output = (keep * (middle + dot_nn(gelu_low, full_proj) + bias_proj)).astype(low)

    grad_result = keep * cotangent.astype(wide)
    grad_result_low = grad_result.astype(low)
    grad_hidden = gelu_pull(dot_nt(grad_result_low, full_proj))[0].astype(low)
    mlp_grads = lax.psum_scatter(
        jnp.concatenate([dot_tn(grad_hidden, normed_two), dot_tn(gelu_low, grad_result_low)], axis=1),
        "dev",
        scatter_dimension=0,
        tiled=True,
    )
    grad_norm_two = dot_nn(grad_hidden, full_fc)
    grad_middle = grad_result + norm_back(unit_two, scale_two, gain_two, grad_norm_two)
    grad_branch = grad_middle.astype(low)
    grad_attended = dot_nt(grad_branch, full_out).astype(low)
    grad_q, grad_k, grad_v = attend_back(firsts, queries, key_vals, grad_attended, lse)

    grad_ext = dot_nt(grad_k, full_qkv[:, width : 2 * width]) + dot_nt(
        grad_v, full_qkv[:, 2 * width :]
    )
    grad_own = grad_ext[RIM : RIM + rows] + dot_nt(grad_q, full_qkv[:, :width])
    head = shifted(grad_ext[rows + RIM :].astype(low), 1).astype(wide)
    tail = shifted(grad_ext[:RIM].astype(low), -1).astype(wide)
    grad_norm_one = grad_own.at[:RIM].add(head).at[rows - RIM :].add(tail)
    unit_own = unit_one[RIM : RIM + rows]
    scale_own = scale_one[RIM : RIM + rows]
    grad_tokens = (grad_middle + norm_back(unit_own, scale_own, gain_one, grad_norm_one)).astype(low)

    def total(values):
        return jnp.sum(values.astype(wide), axis=0)

    small_grads = (
        total(grad_norm_one * unit_own),
        total(grad_norm_one),
        jnp.concatenate([total(grad_q), total(grad_v)]),
        total(grad_branch),
        total(grad_norm_two * unit_two),
        total(grad_norm_two),
        total(grad_hidden),
        total(grad_result),
    )
    small_rows = jnp.concatenate([g.reshape(size, -1) for g in small_grads], axis=1)
    side_grads = jnp.pad(
        small_rows, ((0, 0), (0, feat_rows * extra - small_rows.shape[1]))
    ).reshape(size * feat_rows, extra)
    attn_grads = lax.psum_scatter(
        jnp.concatenate(
            [
                dot_tn(normed_own, grad_q),
                dot_tn(normed_one, grad_k),
                dot_tn(normed_one, grad_v),
                dot_tn(attended, grad_branch),
                side_grads,
            ],
            axis=1,
        ),
        "dev",
        scatter_dimension=0,
        tiled=True,
    )
    side_own = attn_grads[:, 4 * width :].reshape(-1)
    outs = []
    place = 0
    for small in smalls:
        outs.append(side_own[place : place + small.shape[0]])
        place += small.shape[0]
    return (
        output,
        grad_tokens,
        outs[0],
        outs[1],
        attn_grads[:, : 3 * width],
        outs[2],
        attn_grads[:, 3 * width : 4 * width],
        outs[3],
        outs[4],
        outs[5],
        mlp_grads[:, :width],
        outs[6],
        mlp_grads[:, width:],
        outs[7],
    )


def solution(mesh):
    row = P("dev", None)
    line = P("dev")
    return jax.shard_map(
        shards,
        mesh=mesh,
        in_specs=(row, row, line, line, line, line, row, line, row, line, line, line, row, line, row, line),
        out_specs=(row, row, line, line, row, line, row, line, line, line, row, line, row, line),
        check_vma=False,
    )
```

```python
import jax
import jax.numpy as jnp
import numpy as np
from jax import lax
from jax.experimental import pallas as pl
from jax.experimental.pallas import tpu as pltpu
from jax.sharding import PartitionSpec as P

HEAD_DIM = 64
IMG = 577
RIM = IMG - 1
TILE = 128
KEYS = 592
LANES = 256
MASKED = -1e30
NOWHERE = 1 << 20


def dot_nt(a, b):
    return lax.dot_general(a, b, (((1,), (1,)), ((), ())), preferred_element_type=jnp.float32)


def dot_tn(a, b):
    return lax.dot_general(a, b, (((0,), (0,)), ((), ())), preferred_element_type=jnp.float32)


def dot_nn(a, b):
    return lax.dot_general(a, b, (((1,), (0,)), ((), ())), preferred_element_type=jnp.float32)


def paired(block):
    first = lax.broadcasted_iota(jnp.int32, block.shape, 1) < HEAD_DIM
    none = jnp.zeros_like(block)
    return jnp.concatenate([jnp.where(first, block, none), jnp.where(first, none, block)], axis=0)


def unpaired(wide):
    both = jnp.concatenate([wide[:HEAD_DIM, :TILE], wide[HEAD_DIM:, TILE:]], axis=0)
    return both.T


def key_window(first, ext_rows):
    low = first + RIM
    start = jnp.clip((low // 16) * 16, 0, ext_rows - KEYS)
    return pl.multiple_of(start, 16), low - start


def keep_image(scores, offset):
    edge = lax.broadcasted_iota(jnp.int32, (16, scores.shape[1]), 0)
    top = jnp.where(edge >= offset, scores[:16], MASKED)
    low = jnp.where(edge + (KEYS - 16) < offset + IMG, scores[KEYS - 16 :], MASKED)
    return jnp.concatenate([top, scores[16 : KEYS - 16], low], axis=0)


def attend_body(first_ref, q_ref, k_ref, v_ref, out_ref, lse_ref):
    rows = q_ref.shape[0]
    tiles = rows // TILE

    def tile(j, carry):
        at = pl.multiple_of(j * TILE, TILE)
        here = pl.ds(at, TILE)

        def item(first, pair):
            lanes = slice(pair * 128, pair * 128 + 128)
            start, offset = key_window(first, k_ref.shape[0])
            scores = dot_nt(k_ref[pl.ds(start, KEYS), lanes], paired(q_ref[here, lanes]))
            scores = keep_image(scores, offset)
            peak = jnp.max(scores, axis=0, keepdims=True)
            weights = jnp.exp(scores - peak)
            total = jnp.sum(weights, axis=0, keepdims=True)
            mixed = dot_tn(v_ref[pl.ds(start, KEYS), lanes], weights.astype(jnp.bfloat16))
            mixed = unpaired(mixed / total)
            row = lax.broadcasted_iota(jnp.int32, (TILE, 128), 0) + at
            inside = (row >= first) & (row < first + IMG)
            return jnp.where(inside, mixed, 0.0).astype(jnp.bfloat16), peak + jnp.log(total)

        one, two = first_ref[j], first_ref[tiles + j]
        for pair in range(LANES // 128):
            mixed, lse = item(one, pair)
            out_ref[here, pair * 128 : pair * 128 + 128] = mixed
            lse_ref[0, 2 * pair : 2 * pair + 1, here] = lse[:, :TILE]
            lse_ref[0, 2 * pair + 1 : 2 * pair + 2, here] = lse[:, TILE:]

        @pl.when(two != one)
        def _():
            column = lax.broadcasted_iota(jnp.int32, (1, TILE), 1) + at
            inside = (column >= two) & (column < two + IMG)
            for pair in range(LANES // 128):
                lanes = slice(pair * 128, pair * 128 + 128)
                mixed, lse = item(two, pair)
                out_ref[here, lanes] = out_ref[here, lanes] + mixed
                for head in range(2):
                    line = slice(2 * pair + head, 2 * pair + head + 1)
                    new = lse[:, head * TILE : head * TILE + TILE]
                    lse_ref[0, line, here] = jnp.where(inside, new, lse_ref[0, line, here])

        return carry

    lax.fori_loop(0, tiles, tile, 0)


def attend_back_body(
    first_ref, q_ref, k_ref, v_ref, grad_ref, lse_ref, dq_ref, dkv_ref, dk_sum, dv_sum
):
    rows = q_ref.shape[0]
    tiles = rows // TILE
    dk_sum[...] = jnp.zeros_like(dk_sum)
    dv_sum[...] = jnp.zeros_like(dv_sum)

    def tile(j, carry):
        at = pl.multiple_of(j * TILE, TILE)
        here = pl.ds(at, TILE)
        column = lax.broadcasted_iota(jnp.int32, (1, TILE), 1) + at

        def item(first, pair):
            lanes = slice(pair * 128, pair * 128 + 128)
            start, offset = key_window(first, k_ref.shape[0])
            window = pl.ds(start, KEYS)
            keys = k_ref[window, lanes]
            queries = paired(q_ref[here, lanes])
            grads = paired(grad_ref[here, lanes])
            inside = (column >= first) & (column < first + IMG)
            lse = jnp.concatenate(
                [
                    jnp.where(inside, lse_ref[0, 2 * pair : 2 * pair + 1, here], -MASKED),
                    jnp.where(inside, lse_ref[0, 2 * pair + 1 : 2 * pair + 2, here], -MASKED),
                ],
                axis=1,
            )
            probs = jnp.exp(keep_image(dot_nt(keys, queries), offset) - lse)
            grad_probs = dot_nt(v_ref[window, lanes], grads)
            dv_sum[window, lanes] += dot_nn(probs.astype(jnp.bfloat16), grads)
            inner = jnp.sum(grad_probs * probs, axis=0, keepdims=True)
            grad_scores = (probs * (grad_probs - inner)).astype(jnp.bfloat16)
            dk_sum[window, lanes] += dot_nn(grad_scores, queries)
            return unpaired(dot_tn(keys, grad_scores) * HEAD_DIM**-0.5).astype(jnp.bfloat16)

        one, two = first_ref[j], first_ref[tiles + j]
        for pair in range(LANES // 128):
            dq_ref[here, pair * 128 : pair * 128 + 128] = item(one, pair)

        @pl.when(two != one)
        def _():
            for pair in range(LANES // 128):
                lanes = slice(pair * 128, pair * 128 + 128)
                dq_ref[here, lanes] = dq_ref[here, lanes] + item(two, pair)

        return carry

    lax.fori_loop(0, tiles, tile, 0)
    dkv_ref[:, :LANES] = dk_sum[...].astype(jnp.bfloat16)
    dkv_ref[:, LANES:] = dv_sum[...].astype(jnp.bfloat16)


def attention_cost(rows, width, products):
    return pl.CostEstimate(
        flops=2 * products * 10 * TILE * KEYS * width * 8,
        bytes_accessed=16 * rows * width,
        transcendentals=10 * TILE * KEYS * (width // HEAD_DIM),
    )


def attend(firsts, queries, key_vals):
    rows, width = queries.shape
    ext = key_vals.shape[0]
    groups = width // LANES
    return pl.pallas_call(
        attend_body,
        grid_spec=pltpu.PrefetchScalarGridSpec(
            num_scalar_prefetch=1,
            grid=(groups,),
            in_specs=[
                pl.BlockSpec((rows, LANES), lambda g, f: (0, g)),
                pl.BlockSpec((ext, LANES), lambda g, f: (0, 2 * g)),
                pl.BlockSpec((ext, LANES), lambda g, f: (0, 2 * g + 1)),
            ],
            out_specs=[
                pl.BlockSpec((rows, LANES), lambda g, f: (0, g)),
                pl.BlockSpec((1, LANES // HEAD_DIM, rows), lambda g, f: (g, 0, 0)),
            ],
        ),
        out_shape=[
            jax.ShapeDtypeStruct((rows, width), jnp.bfloat16),
            jax.ShapeDtypeStruct((groups, LANES // HEAD_DIM, rows), jnp.float32),
        ],
        cost_estimate=attention_cost(rows, width, 2),
        name="attend",
    )(firsts, queries, key_vals, key_vals)


def attend_back(firsts, queries, key_vals, grads, lse, part):
    rows, width = queries.shape
    ext = key_vals.shape[0]
    groups = width // LANES // 2
    base = part * groups
    own = pl.BlockSpec((rows, LANES), lambda g, f: (0, base + g))
    return pl.pallas_call(
        attend_back_body,
        grid_spec=pltpu.PrefetchScalarGridSpec(
            num_scalar_prefetch=1,
            grid=(groups,),
            in_specs=[
                own,
                pl.BlockSpec((ext, LANES), lambda g, f: (0, 2 * (base + g))),
                pl.BlockSpec((ext, LANES), lambda g, f: (0, 2 * (base + g) + 1)),
                own,
                pl.BlockSpec((1, LANES // HEAD_DIM, rows), lambda g, f: (base + g, 0, 0)),
            ],
            out_specs=[
                pl.BlockSpec((rows, LANES), lambda g, f: (0, g)),
                pl.BlockSpec((ext, 2 * LANES), lambda g, f: (0, g)),
            ],
            scratch_shapes=[pltpu.VMEM((ext, LANES), jnp.float32)] * 2,
        ),
        out_shape=[
            jax.ShapeDtypeStruct((rows, width // 2), jnp.bfloat16),
            jax.ShapeDtypeStruct((ext, width), jnp.bfloat16),
        ],
        cost_estimate=attention_cost(rows, width // 2, 5),
        name="attend_back",
    )(firsts, queries, key_vals, key_vals, grads, lse)


def by_group(keys, values):
    parts = []
    for at in range(0, keys.shape[-1], LANES):
        parts += [keys[..., at : at + LANES], values[..., at : at + LANES]]
    return parts


def image_firsts(padding, ident):
    rows = padding.shape[0]
    tiles = rows // TILE
    real = padding == 1
    by_tile = jnp.where(real, ident, NOWHERE).reshape(tiles, TILE)
    low_id = jnp.min(by_tile, axis=1)
    high_id = jnp.max(jnp.where(real, ident, -1).reshape(tiles, TILE), axis=1)
    wanted = jnp.concatenate([low_id, high_id])
    place = jnp.arange(rows, dtype=jnp.int32)[None, :]
    mine = real[None, :] & (ident[None, :] == wanted[:, None])
    run_first = jnp.min(jnp.where(mine, place, NOWHERE), axis=1)
    run_last = jnp.max(jnp.where(mine, place, -1), axis=1)
    firsts = jnp.where(run_last < rows - 1, run_last - RIM, run_first)
    empty = jnp.concatenate([low_id, low_id]) == NOWHERE
    before = jnp.tile(jnp.arange(tiles, dtype=jnp.int32) * TILE - IMG, 2)
    return jnp.where(empty, before, firsts)


def normed_parts(values):
    centered = values - jnp.mean(values, axis=-1, keepdims=True)
    spread = jnp.mean(centered * centered, axis=-1, keepdims=True)
    scale = lax.rsqrt(spread + 1e-05)
    return centered * scale, scale


def norm_back(unit, scale, gain, grads):
    scaled = grads * gain
    return scale * (
        scaled
        - jnp.mean(scaled, axis=-1, keepdims=True)
        - unit * jnp.mean(scaled * unit, axis=-1, keepdims=True)
    )


def quick_gelu(values):
    return values * jax.nn.sigmoid(1.702 * values)


def shifted(value, by):
    size = lax.axis_size("dev")
    pairs = [(i, i + by) for i in range(size) if 0 <= i + by < size]
    return lax.ppermute(value, "dev", pairs)


class Rings:
    def __init__(self, size):
        bits = size.bit_length() - 1
        self.size = size
        self.top = bits - 2
        middle = list(range(1, self.top))
        self.orders = (middle, middle[::-1])
        self.stages = len(middle)
        halves = []
        for order in self.orders:
            blocks = [(0, r) for r in range(4)]
            for bit in order:
                blocks = blocks + [(mask ^ (1 << bit), r) for mask, r in blocks]
            halves.append(blocks)
        self.blocks = [
            halves[core] + [(mask ^ 1, r) for mask, r in halves[1 - core]] for core in range(2)
        ]

    def rotated(self, device, by):
        low = device % (1 << self.top)
        return (((device >> self.top) + by) % 4 << self.top) | low

    def permute(self, value, target):
        return lax.ppermute(value, "dev", [(i, target(i)) for i in range(self.size)])

    def turn(self, value, by):
        return self.permute(value, lambda i: self.rotated(i, by))

    def pair(self, value, stage):
        return self.permute(value, lambda i: i ^ (1 << self.orders[i & 1][stage]))

    def swap(self, value):
        return self.permute(value, lambda i: i ^ 1)

    def owners(self):
        me = lax.axis_index("dev")
        lists = []
        for core in range(2):
            masks = np.array([mask for mask, _ in self.blocks[core]], np.int32)
            turns = np.array([r for _, r in self.blocks[core]], np.int32)
            low = (me ^ masks) & ((1 << self.top) - 1)
            lists.append((((me >> self.top) + turns) & 3) << self.top | low)
        return jnp.where(me & 1 == 0, lists[0], lists[1])

    def quad(self, block):
        return jnp.concatenate([block] + [self.turn(block, -r) for r in (1, 2, 3)], axis=0)

    def cut(self, total):
        at = total.shape[0] // 2
        return total[:at], total[at:].astype(jnp.bfloat16)

    def quarters(self, total):
        rows = total.shape[0] // 4
        sent = [total[r * rows : (r + 1) * rows].astype(jnp.bfloat16) for r in (1, 2, 3)]
        return total[:rows], sent

    def turned(self, parts):
        return [self.turn(part, r) for r, part in zip((1, 2, 3), parts)]


def added(kept, *received):
    for part in received:
        kept = kept + part.astype(jnp.float32)
    return kept


def after(value, *others):
    return lax.optimization_barrier((value, others))[0]


def shards(
    tokens,
    cotangent,
    padding,
    image_ident,
    ln1_gain,
    ln1_bias,
    w_qkv,
    b_qv,
    w_out,
    b_out,
    ln2_gain,
    ln2_bias,
    w_fc,
    b_fc,
    w_proj,
    b_proj,
):
    low = jnp.bfloat16
    wide = jnp.float32
    size = lax.axis_size("dev")
    width = w_out.shape[1]
    rows = tokens.shape[0]
    feat_rows = w_qkv.shape[0]
    smalls = (ln1_gain, ln1_bias, b_qv, b_out, ln2_gain, ln2_bias, b_fc, b_proj)
    extra = 128
    rings = Rings(size)
    owners = rings.owners()
    side = jnp.concatenate(smalls)
    side = jnp.pad(side, (0, feat_rows * extra - side.shape[0])).reshape(feat_rows, extra)
    qkv_side = lax.all_gather(
        jnp.concatenate(
            [w_qkv[:, :width]]
            + by_group(w_qkv[:, width : 2 * width], w_qkv[:, 2 * width :])
            + [side],
            axis=1,
        ),
        "dev", axis=0, tiled=True
    )
    full_out = lax.all_gather(w_out, "dev", axis=0, tiled=True)
    halves = [rings.quad(w_fc), rings.quad(w_proj)]
    last = rings.stages - 1
    for stage in range(last):
        halves = [jnp.concatenate([h, rings.pair(h, stage)], axis=0) for h in halves]
    halves = [(h, rings.pair(h, last)) for h in halves]
    full_qkv = qkv_side[:, : 3 * width]
    side_all = qkv_side[:, 3 * width :].reshape(size, feat_rows * extra).astype(wide)
    vectors = []
    place = 0
    for small in smalls:
        vectors.append(side_all[:, place : place + small.shape[0]])
        place += small.shape[0]
    chosen = (owners[:, None] == jnp.arange(size, dtype=jnp.int32)[None, :])[:, :, None]
    vectors[6] = jnp.sum(jnp.where(chosen, vectors[6][None], 0.0), axis=1)
    vectors = [v.reshape(-1) for v in vectors]
    gain_one, bias_one, bias_qv, bias_out, gain_two, bias_two, bias_fc, bias_proj = vectors

    firsts = image_firsts(padding, image_ident)
    ext_tokens = jnp.concatenate(
        [shifted(tokens[rows - RIM :], 1), tokens, shifted(tokens[:RIM], -1)], axis=0
    )
    unit_one, scale_one = normed_parts(ext_tokens.astype(wide))
    normed_one = (unit_one * gain_one + bias_one).astype(low)
    normed_own = normed_one[RIM : RIM + rows]
    queries = (
        (dot_nn(normed_own, full_qkv[:, :width]) + bias_qv[:width]).astype(low)
        * HEAD_DIM**-0.5
    ).astype(low)
    kv_bias = jnp.concatenate(by_group(jnp.zeros((width,), wide), bias_qv[width:]))
    key_vals = (dot_nn(normed_one, full_qkv[:, width:]) + kv_bias).astype(low)
    feature = jnp.arange(width, dtype=jnp.int32)
    wanted = (owners[:, None] * feat_rows + jnp.arange(feat_rows, dtype=jnp.int32)).reshape(-1)
    reorder = (feature[:, None] == wanted[None, :]).astype(low)
    normed_turned = dot_nn(normed_one, reorder).astype(low)
    key_vals, halves = lax.optimization_barrier((key_vals, halves))
    halves = [jnp.concatenate(h, axis=0) for h in halves]
    queries, halves = lax.optimization_barrier((queries, halves))
    (fc_own, proj_own), (fc_other, proj_other) = halves, [rings.swap(h) for h in halves]
    attended, lse = attend(firsts, queries, key_vals)

    middle = tokens.astype(wide) + (dot_nn(attended, full_out) + bias_out)
    unit_two, scale_two = normed_parts(middle)
    normed_two = (unit_two * gain_two + bias_two).astype(low)
    keep = padding.astype(wide)[:, None]
    grad_result = keep * cotangent.astype(wide)
    grad_result_low = grad_result.astype(low)
    half = fc_own.shape[0]

    def up(fc_part, proj_part, bias_part):
        hidden, pull = jax.vjp(quick_gelu, dot_nt(normed_two, fc_part) + bias_part)
        return hidden.astype(low), pull

    def down(pull, proj_part):
        return pull(dot_nt(grad_result_low, proj_part))[0].astype(low)

    gelu_own, pull_own = up(fc_own, proj_own, bias_fc[:half])
    gelu_other, pull_other = up(fc_other, proj_other, bias_fc[half:])
    proj_sent = rings.swap(dot_tn(gelu_other, grad_result_low).astype(low))
    proj_kept = dot_tn(gelu_own, grad_result_low)
    grad_hidden_own = down(pull_own, proj_own)
    grad_hidden_other = down(pull_other, proj_other)
    fc_sent = rings.swap(dot_tn(grad_hidden_other, normed_two).astype(low))
    fc_kept = dot_tn(grad_hidden_own, normed_two)
    proj_kept, proj_cut = rings.cut(added(proj_kept, proj_sent))
    proj_sent = rings.pair(proj_cut, last)
    up_own, up_other = dot_nn(gelu_own, proj_own), dot_nn(gelu_other, proj_other)
    output = (keep * (middle + up_own + up_other + bias_proj)).astype(low)
    down_own, down_other = dot_nn(grad_hidden_own, fc_own), dot_nn(grad_hidden_other, fc_other)
    fc_kept, fc_cut = rings.cut(added(fc_kept, fc_sent))
    grad_norm_two = down_own + down_other
    grad_middle = grad_result + norm_back(unit_two, scale_two, gain_two, grad_norm_two)
    grad_branch = grad_middle.astype(low)
    grad_attended = dot_nt(grad_branch, full_out).astype(low)

    def total(values):
        return jnp.sum(values.astype(wide), axis=0)

    hidden_sums = jnp.concatenate([total(grad_hidden_own), total(grad_hidden_other)])
    hidden_sums = jnp.sum(jnp.where(chosen, hidden_sums.reshape(size, 1, -1), 0.0), axis=0)
    def sided(vectors):
        lines = jnp.concatenate([g.reshape(size, -1) for g in vectors], axis=1)
        lines = jnp.pad(lines, ((0, 0), (0, feat_rows * extra - lines.shape[1])))
        return lines.reshape(width, extra)

    def unsided(flat, vectors):
        parts = []
        at = 0
        for vector in vectors:
            parts.append(flat[at : at + vector.shape[0]])
            at += vector.shape[0]
        return parts

    def scattered(values):
        return lax.psum_scatter(values, "dev", scatter_dimension=0, tiled=True)

    turned_own = normed_turned[RIM : RIM + rows]
    near, far = slice(0, width // 2), slice(width // 2, width)

    def products(lines, grad_q, grad_kv):
        return jnp.concatenate(
            [dot_tn(turned_own[:, lines], grad_q), dot_tn(normed_turned[:, lines], grad_kv)], axis=1
        )

    out_product = dot_tn(attended, grad_branch)
    grad_attended = after(grad_attended, output, fc_cut, proj_cut, out_product)
    fc_sent = rings.pair(fc_cut, last)
    grad_out = scattered(out_product)
    first_q, first_kv = attend_back(firsts, queries, key_vals, grad_attended, lse, 0)

    first_kv, fc_sent, proj_sent = lax.optimization_barrier((first_kv, fc_sent, proj_sent))
    for stage in reversed(range(last)):
        fc_kept, fc_cut = rings.cut(added(fc_kept, fc_sent))
        proj_kept, proj_cut = rings.cut(added(proj_kept, proj_sent))
        fc_sent, proj_sent = rings.pair(fc_cut, stage), rings.pair(proj_cut, stage)
    first_cut = products(far, first_q, first_kv).astype(low)
    first_sent = rings.swap(first_cut)
    first_kept = products(near, first_q, first_kv)
    grad_attended = after(grad_attended, first_kept, first_cut, fc_cut, proj_cut)
    second_q, second_kv = attend_back(firsts, queries, key_vals, grad_attended, lse, 1)

    second_kv, fc_sent, proj_sent, first_sent, grad_out = lax.optimization_barrier(
        (second_kv, fc_sent, proj_sent, first_sent, grad_out)
    )
    fc_kept, fc_cut = rings.quarters(added(fc_kept, fc_sent))
    proj_kept, proj_cut = rings.quarters(added(proj_kept, proj_sent))
    first_kept, first_cut = rings.cut(added(first_kept, first_sent))
    first_sent = rings.pair(first_cut, last)
    fc_sent, proj_sent = rings.turned(fc_cut), rings.turned(proj_cut)
    second_kv = after(second_kv, fc_cut, proj_cut, first_cut)
    second_cut = products(far, second_q, second_kv).astype(low)
    second_sent = rings.swap(second_cut)
    second_kept = products(near, second_q, after(second_kv, second_cut))
    second_sent, first_sent, second_kept = lax.optimization_barrier(
        (second_sent, first_sent, second_kept)
    )
    second_kept, second_cut = rings.cut(added(second_kept, second_sent))
    second_sent = rings.pair(second_cut, last)
    for stage in reversed(range(last)):
        first_kept, first_cut = rings.cut(added(first_kept, first_sent))
        first_sent = rings.pair(first_cut, stage)
    w_kv = full_qkv[:, width:]
    grad_ext = dot_nt(after(first_kv, second_cut, first_cut), w_kv[:, :width])
    grad_ext, first_sent, second_sent = lax.optimization_barrier((grad_ext, first_sent, second_sent))
    for stage in reversed(range(last)):
        second_kept, second_cut = rings.cut(added(second_kept, second_sent))
        second_sent = rings.pair(second_cut, stage)
    first_kept, first_cut = rings.quarters(added(first_kept, first_sent))
    first_sent = rings.turned(first_cut)
    grad_ext = grad_ext + dot_nt(after(second_kv, second_cut, first_cut), w_kv[:, width:])
    grad_q = jnp.concatenate([first_q, second_q], axis=1)
    grad_by_q = dot_nt(grad_q, full_qkv[:, :width])
    grad_own = grad_ext[RIM : RIM + rows] + grad_by_q
    head = shifted(grad_ext[rows + RIM :].astype(low), 1).astype(wide)
    tail = shifted(grad_ext[:RIM].astype(low), -1).astype(wide)
    grad_own, second_sent = lax.optimization_barrier((grad_own, second_sent))
    second_kept, second_cut = rings.quarters(added(second_kept, second_sent))
    second_sent = rings.turned(second_cut)
    grad_norm_one = (
        grad_own
        + jnp.pad(head, ((0, rows - RIM), (0, 0)))
        + jnp.pad(tail, ((rows - RIM, 0), (0, 0)))
    )
    unit_own = unit_one[RIM : RIM + rows]
    scale_own = scale_one[RIM : RIM + rows]
    grad_tokens = (grad_middle + norm_back(unit_own, scale_own, gain_one, grad_norm_one)).astype(low)

    grad_fc, grad_proj = added(fc_kept, *fc_sent), added(proj_kept, *proj_sent)
    grad_first, grad_second = added(first_kept, *first_sent), added(second_kept, *second_sent)
    value_sums = [total(first_kv).reshape(-1, 2, LANES), total(second_kv).reshape(-1, 2, LANES)]
    value_sums = jnp.concatenate(value_sums, axis=0)[:, 1].reshape(-1)
    side_grads = scattered(
        sided(
            (
                total(grad_ext * unit_one) + total(grad_by_q * unit_own),
                total(grad_ext) + total(grad_by_q),
                jnp.concatenate([total(grad_q), value_sums]),
                total(grad_branch),
                total(grad_norm_two * unit_two),
                total(grad_norm_two),
                hidden_sums,
                total(grad_result),
            )
        )
    )
    small_outs = unsided(side_grads.reshape(-1), smalls)
    both = (grad_first, grad_second)
    columns = [part[:, : width // 2] for part in both]
    for which in range(2):
        for part in both:
            for at in range(width // 2, part.shape[1], 2 * LANES):
                columns.append(part[:, at + which * LANES : at + which * LANES + LANES])
    return (
        output,
        grad_tokens,
        small_outs[0],
        small_outs[1],
        jnp.concatenate(columns, axis=1),
        small_outs[2],
        grad_out,
        small_outs[3],
        small_outs[4],
        small_outs[5],
        grad_fc,
        small_outs[6],
        grad_proj,
        small_outs[7],
    )


def solution(mesh):
    row = P("dev", None)
    line = P("dev")
    return jax.shard_map(
        shards,
        mesh=mesh,
        in_specs=(row, row, line, line, line, line, row, line, row, line, line, line, row, line, row, line),
        out_specs=(row, row, line, line, row, line, row, line, line, line, row, line, row, line),
        check_vma=False,
    )
```

```python
import jax
import jax.numpy as jnp
import numpy as np
from jax import lax
from jax.experimental import pallas as pl
from jax.experimental.pallas import tpu as pltpu
from jax.sharding import PartitionSpec as P

HEAD_DIM = 64
IMG = 577
RIM = IMG - 1
TILE = 128
KEYS = 592
LANES = 256
MASKED = -1e30
NOWHERE = 1 << 20


def dot_nt(a, b):
    return lax.dot_general(a, b, (((1,), (1,)), ((), ())), preferred_element_type=jnp.float32)


def dot_tn(a, b):
    return lax.dot_general(a, b, (((0,), (0,)), ((), ())), preferred_element_type=jnp.float32)


def dot_nn(a, b):
    return lax.dot_general(a, b, (((1,), (0,)), ((), ())), preferred_element_type=jnp.float32)


def paired(block):
    first = lax.broadcasted_iota(jnp.int32, block.shape, 1) < HEAD_DIM
    none = jnp.zeros_like(block)
    return jnp.concatenate([jnp.where(first, block, none), jnp.where(first, none, block)], axis=0)


def unpaired(wide):
    both = jnp.concatenate([wide[:HEAD_DIM, :TILE], wide[HEAD_DIM:, TILE:]], axis=0)
    return both.T


def key_window(first, ext_rows):
    low = first + RIM
    start = jnp.clip((low // 16) * 16, 0, ext_rows - KEYS)
    return pl.multiple_of(start, 16), low - start


def keep_image(scores, offset):
    edge = lax.broadcasted_iota(jnp.int32, (16, scores.shape[1]), 0)
    top = jnp.where(edge >= offset, scores[:16], MASKED)
    low = jnp.where(edge + (KEYS - 16) < offset + IMG, scores[KEYS - 16 :], MASKED)
    return jnp.concatenate([top, scores[16 : KEYS - 16], low], axis=0)


def attend_body(first_ref, q_ref, k_ref, v_ref, out_ref, lse_ref):
    tiles = out_ref.shape[0] // TILE

    def tile(j, carry):
        at = pl.multiple_of(j * TILE, TILE)
        here = pl.ds(at, TILE)
        asking = pl.ds(pl.multiple_of(at + RIM, 64), TILE)

        def item(first, pair):
            lanes = slice(pair * 128, pair * 128 + 128)
            start, offset = key_window(first, k_ref.shape[0])
            scores = dot_nt(k_ref[pl.ds(start, KEYS), lanes], paired(q_ref[asking, lanes]))
            scores = keep_image(scores, offset)
            peak = jnp.max(scores, axis=0, keepdims=True)
            weights = jnp.exp(scores - peak)
            total = jnp.sum(weights, axis=0, keepdims=True)
            mixed = dot_tn(v_ref[pl.ds(start, KEYS), lanes], weights.astype(jnp.bfloat16))
            mixed = unpaired(mixed / total)
            row = lax.broadcasted_iota(jnp.int32, (TILE, 128), 0) + at
            inside = (row >= first) & (row < first + IMG)
            return jnp.where(inside, mixed, 0.0).astype(jnp.bfloat16), peak + jnp.log(total)

        one, two = first_ref[j], first_ref[tiles + j]
        for pair in range(LANES // 128):
            mixed, lse = item(one, pair)
            out_ref[here, pair * 128 : pair * 128 + 128] = mixed
            lse_ref[0, 2 * pair : 2 * pair + 1, here] = lse[:, :TILE]
            lse_ref[0, 2 * pair + 1 : 2 * pair + 2, here] = lse[:, TILE:]

        @pl.when(two != one)
        def _():
            column = lax.broadcasted_iota(jnp.int32, (1, TILE), 1) + at
            inside = (column >= two) & (column < two + IMG)
            for pair in range(LANES // 128):
                lanes = slice(pair * 128, pair * 128 + 128)
                mixed, lse = item(two, pair)
                out_ref[here, lanes] = out_ref[here, lanes] + mixed
                for head in range(2):
                    line = slice(2 * pair + head, 2 * pair + head + 1)
                    new = lse[:, head * TILE : head * TILE + TILE]
                    lse_ref[0, line, here] = jnp.where(inside, new, lse_ref[0, line, here])

        return carry

    lax.fori_loop(0, tiles, tile, 0)


def attend_back_body(
    first_ref, q_ref, k_ref, v_ref, grad_ref, lse_ref, mixed_ref, dk_sum, dv_sum
):
    rows = grad_ref.shape[0]
    tiles = rows // TILE
    mixed_ref[:RIM, :LANES] = jnp.zeros((RIM, LANES), jnp.bfloat16)
    mixed_ref[RIM + rows :, :LANES] = jnp.zeros((RIM, LANES), jnp.bfloat16)
    dk_sum[...] = jnp.zeros_like(dk_sum)
    dv_sum[...] = jnp.zeros_like(dv_sum)

    def tile(j, carry):
        at = pl.multiple_of(j * TILE, TILE)
        here = pl.ds(at, TILE)
        asking = pl.ds(pl.multiple_of(at + RIM, 64), TILE)
        column = lax.broadcasted_iota(jnp.int32, (1, TILE), 1) + at

        def item(first, pair):
            lanes = slice(pair * 128, pair * 128 + 128)
            start, offset = key_window(first, k_ref.shape[0])
            window = pl.ds(start, KEYS)
            keys = k_ref[window, lanes]
            queries = paired(q_ref[asking, lanes])
            grads = paired(grad_ref[here, lanes])
            inside = (column >= first) & (column < first + IMG)
            lse = jnp.concatenate(
                [
                    jnp.where(inside, lse_ref[0, 2 * pair : 2 * pair + 1, here], -MASKED),
                    jnp.where(inside, lse_ref[0, 2 * pair + 1 : 2 * pair + 2, here], -MASKED),
                ],
                axis=1,
            )
            probs = jnp.exp(keep_image(dot_nt(keys, queries), offset) - lse)
            grad_probs = dot_nt(v_ref[window, lanes], grads)
            dv_sum[window, lanes] += dot_nn(probs.astype(jnp.bfloat16), grads)
            inner = jnp.sum(grad_probs * probs, axis=0, keepdims=True)
            grad_scores = (probs * (grad_probs - inner)).astype(jnp.bfloat16)
            dk_sum[window, lanes] += dot_nn(grad_scores, queries)
            return unpaired(dot_tn(keys, grad_scores) * HEAD_DIM**-0.5).astype(jnp.bfloat16)

        one, two = first_ref[j], first_ref[tiles + j]
        for pair in range(LANES // 128):
            mixed_ref[asking, pair * 128 : pair * 128 + 128] = item(one, pair)

        @pl.when(two != one)
        def _():
            for pair in range(LANES // 128):
                lanes = slice(pair * 128, pair * 128 + 128)
                mixed_ref[asking, lanes] = mixed_ref[asking, lanes] + item(two, pair)

        return carry

    lax.fori_loop(0, tiles, tile, 0)
    mixed_ref[:, LANES : 2 * LANES] = dk_sum[...].astype(jnp.bfloat16)
    mixed_ref[:, 2 * LANES :] = dv_sum[...].astype(jnp.bfloat16)


def attention_cost(rows, width, products):
    return pl.CostEstimate(
        flops=2 * products * 10 * TILE * KEYS * width * 8,
        bytes_accessed=16 * rows * width,
        transcendentals=10 * TILE * KEYS * (width // HEAD_DIM),
    )


def mixed_specs(ext, base):
    return [
        pl.BlockSpec((ext, LANES), lambda g, f, at=at: (0, 3 * (base + g) + at)) for at in range(3)
    ]


def attend(firsts, mixed, rows, part):
    ext, width = mixed.shape[0], mixed.shape[1] // 3
    groups = width // LANES // 2
    return pl.pallas_call(
        attend_body,
        grid_spec=pltpu.PrefetchScalarGridSpec(
            num_scalar_prefetch=1,
            grid=(groups,),
            in_specs=mixed_specs(ext, part * groups),
            out_specs=[
                pl.BlockSpec((rows, LANES), lambda g, f: (0, g)),
                pl.BlockSpec((1, LANES // HEAD_DIM, rows), lambda g, f: (g, 0, 0)),
            ],
        ),
        out_shape=[
            jax.ShapeDtypeStruct((rows, width // 2), jnp.bfloat16),
            jax.ShapeDtypeStruct((groups, LANES // HEAD_DIM, rows), jnp.float32),
        ],
        cost_estimate=attention_cost(rows, width // 2, 3),
        name="attend",
    )(firsts, mixed, mixed, mixed)


def attend_back(firsts, mixed, grads, lse, part):
    ext, width = mixed.shape[0], mixed.shape[1] // 3
    rows = grads.shape[0]
    groups = width // LANES // 2
    base = part * groups
    return pl.pallas_call(
        attend_back_body,
        grid_spec=pltpu.PrefetchScalarGridSpec(
            num_scalar_prefetch=1,
            grid=(groups,),
            in_specs=mixed_specs(ext, base)
            + [
                pl.BlockSpec((rows, LANES), lambda g, f: (0, base + g)),
                pl.BlockSpec((1, LANES // HEAD_DIM, rows), lambda g, f: (g, 0, 0)),
            ],
            out_specs=pl.BlockSpec((ext, 3 * LANES), lambda g, f: (0, g)),
            scratch_shapes=[pltpu.VMEM((ext, LANES), jnp.float32)] * 2,
        ),
        out_shape=jax.ShapeDtypeStruct((ext, 3 * width // 2), jnp.bfloat16),
        cost_estimate=attention_cost(rows, width // 2, 5),
        name="attend_back",
    )(firsts, mixed, mixed, mixed, grads, lse)


def into_norm_body(first_ref, second_ref, w_ref, tokens_ref, out_ref, sums_ref, mixed_sums_ref):
    cut = first_ref.shape[1]
    grads = dot_nt(first_ref[...], w_ref[:, :cut]) + dot_nt(
        second_ref[...], w_ref[:, cut : 2 * cut]
    )
    out_ref[...] = grads.astype(jnp.bfloat16)
    unit = normed_parts(tokens_ref[...].astype(jnp.float32))[0]
    lines = jnp.concatenate(
        [jnp.sum(grads * unit, axis=0, keepdims=True), jnp.sum(grads, axis=0, keepdims=True)],
        axis=0,
    )
    sides = [
        jnp.sum(ref[...].astype(jnp.float32), axis=0, keepdims=True)
        for ref in (first_ref, second_ref)
    ]

    @pl.when(pl.program_id(0) == 0)
    def _():
        sums_ref[...] = jnp.zeros_like(sums_ref)
        mixed_sums_ref[...] = jnp.zeros_like(mixed_sums_ref)

    sums_ref[...] += lines
    mixed_sums_ref[:, :cut] += sides[0]
    mixed_sums_ref[:, cut:] += sides[1]


def into_norm(first, second, w_mixed, tokens):
    ext, cut = first.shape
    width = tokens.shape[1]
    steps = 4
    block = ext // steps
    whole = lambda i: (0, 0)
    return pl.pallas_call(
        into_norm_body,
        grid=(steps,),
        in_specs=[
            pl.BlockSpec((block, cut), lambda i: (i, 0)),
            pl.BlockSpec((block, cut), lambda i: (i, 0)),
            pl.BlockSpec(w_mixed.shape, whole, pipeline_mode=pl.Buffered(1)),
            pl.BlockSpec((block, width), lambda i: (i, 0)),
        ],
        out_specs=[
            pl.BlockSpec((block, width), lambda i: (i, 0)),
            pl.BlockSpec((2, width), whole),
            pl.BlockSpec((1, 2 * cut), whole),
        ],
        out_shape=[
            jax.ShapeDtypeStruct((ext, width), jnp.bfloat16),
            jax.ShapeDtypeStruct((2, width), jnp.float32),
            jax.ShapeDtypeStruct((1, 2 * cut), jnp.float32),
        ],
        cost_estimate=pl.CostEstimate(
            flops=4 * ext * cut * width, bytes_accessed=8 * ext * cut, transcendentals=0
        ),
        name="into_norm",
    )(first, second, w_mixed, tokens)


def grouped(queries, keys, values):
    parts = []
    for at in range(0, keys.shape[-1], LANES):
        parts += [part[..., at : at + LANES] for part in (queries, keys, values)]
    return parts


def ungrouped(columns, which):
    width = columns.shape[-1]
    return [
        columns[..., at : at + LANES] for at in range(which * LANES, width, 3 * LANES)
    ]


def image_firsts(padding, ident):
    rows = padding.shape[0]
    tiles = rows // TILE
    real = padding == 1
    by_tile = jnp.where(real, ident, NOWHERE).reshape(tiles, TILE)
    low_id = jnp.min(by_tile, axis=1)
    high_id = jnp.max(jnp.where(real, ident, -1).reshape(tiles, TILE), axis=1)
    wanted = jnp.concatenate([low_id, high_id])
    place = jnp.arange(rows, dtype=jnp.int32)[None, :]
    mine = real[None, :] & (ident[None, :] == wanted[:, None])
    run_first = jnp.min(jnp.where(mine, place, NOWHERE), axis=1)
    run_last = jnp.max(jnp.where(mine, place, -1), axis=1)
    firsts = jnp.where(run_last < rows - 1, run_last - RIM, run_first)
    empty = jnp.concatenate([low_id, low_id]) == NOWHERE
    before = jnp.tile(jnp.arange(tiles, dtype=jnp.int32) * TILE - IMG, 2)
    return jnp.where(empty, before, firsts)


def normed_parts(values):
    centered = values - jnp.mean(values, axis=-1, keepdims=True)
    spread = jnp.mean(centered * centered, axis=-1, keepdims=True)
    scale = lax.rsqrt(spread + 1e-05)
    return centered * scale, scale


def norm_back(unit, scale, gain, grads):
    scaled = grads * gain
    return scale * (
        scaled
        - jnp.mean(scaled, axis=-1, keepdims=True)
        - unit * jnp.mean(scaled * unit, axis=-1, keepdims=True)
    )


def quick_gelu(values):
    return values * jax.nn.sigmoid(1.702 * values)


def shifted(value, by):
    size = lax.axis_size("dev")
    pairs = [(i, i + by) for i in range(size) if 0 <= i + by < size]
    return lax.ppermute(value, "dev", pairs)


class Rings:
    def __init__(self, size):
        bits = size.bit_length() - 1
        self.size = size
        self.top = bits - 2
        middle = list(range(1, self.top))
        self.orders = (middle, middle[::-1])
        self.stages = len(middle)
        halves = []
        for order in self.orders:
            blocks = [(0, r) for r in range(4)]
            for bit in order:
                blocks = blocks + [(mask ^ (1 << bit), r) for mask, r in blocks]
            halves.append(blocks)
        self.blocks = [
            halves[core] + [(mask ^ 1, r) for mask, r in halves[1 - core]] for core in range(2)
        ]

    def rotated(self, device, by):
        low = device % (1 << self.top)
        return (((device >> self.top) + by) % 4 << self.top) | low

    def permute(self, value, target):
        return lax.ppermute(value, "dev", [(i, target(i)) for i in range(self.size)])

    def turn(self, value, by):
        return self.permute(value, lambda i: self.rotated(i, by))

    def pair(self, value, stage):
        return self.permute(value, lambda i: i ^ (1 << self.orders[i & 1][stage]))

    def pairs(self, values, stage):
        return [self.pair(value, stage) for value in values]

    def swap(self, value):
        return self.permute(value, lambda i: i ^ 1)

    def owners(self):
        me = lax.axis_index("dev")
        lists = []
        for core in range(2):
            masks = np.array([mask for mask, _ in self.blocks[core]], np.int32)
            turns = np.array([r for _, r in self.blocks[core]], np.int32)
            low = (me ^ masks) & ((1 << self.top) - 1)
            lists.append((((me >> self.top) + turns) & 3) << self.top | low)
        return jnp.where(me & 1 == 0, lists[0], lists[1])

    def quad(self, block):
        return jnp.concatenate([block] + [self.turn(block, -r) for r in (1, 2, 3)], axis=0)

    def cut(self, totals):
        at = totals[0].shape[0] // 2
        sent = [total[at:].astype(jnp.bfloat16) for total in totals]
        return [total[:at] for total in totals], sent

    def quarters(self, totals):
        rows = totals[0].shape[0] // 4
        sent = []
        for r in (1, 2, 3):
            here = slice(r * rows, (r + 1) * rows)
            sent.append(jnp.concatenate([t[here].astype(jnp.bfloat16) for t in totals], axis=1))
        return [total[:rows] for total in totals], sent

    def turned(self, parts):
        return [self.turn(part, r) for r, part in zip((1, 2, 3), parts)]


def added(kept, received):
    return [total + part.astype(jnp.float32) for total, part in zip(kept, received)]


def quarters_added(kept, received):
    sums = []
    at = 0
    for total in kept:
        for part in received:
            total = total + part[:, at : at + total.shape[1]].astype(jnp.float32)
        sums.append(total)
        at += total.shape[1]
    return sums


def after(value, *others):
    return lax.optimization_barrier((value, others))[0]


def shards(
    tokens,
    cotangent,
    padding,
    image_ident,
    ln1_gain,
    ln1_bias,
    w_qkv,
    b_qv,
    w_out,
    b_out,
    ln2_gain,
    ln2_bias,
    w_fc,
    b_fc,
    w_proj,
    b_proj,
):
    low = jnp.bfloat16
    wide = jnp.float32
    size = lax.axis_size("dev")
    width = w_out.shape[1]
    rows = tokens.shape[0]
    feat_rows = w_qkv.shape[0]
    smalls = (ln1_gain, ln1_bias, b_qv, b_out, ln2_gain, ln2_bias, b_fc, b_proj)
    extra = 128
    rings = Rings(size)
    owners = rings.owners()
    side = jnp.concatenate(smalls)
    side = jnp.pad(side, (0, feat_rows * extra - side.shape[0])).reshape(feat_rows, extra)
    columns = grouped(w_qkv[:, :width], w_qkv[:, width : 2 * width], w_qkv[:, 2 * width :])
    w_mixed = lax.all_gather(
        jnp.concatenate(columns + [side], axis=1), "dev", axis=0, tiled=True
    )
    full_out = lax.all_gather(w_out, "dev", axis=0, tiled=True)
    side_all = w_mixed[:, 3 * width :].reshape(size, feat_rows * extra).astype(wide)
    vectors = []
    place = 0
    for small in smalls:
        vectors.append(side_all[:, place : place + small.shape[0]])
        place += small.shape[0]
    chosen = (owners[:, None] == jnp.arange(size, dtype=jnp.int32)[None, :])[:, :, None]
    vectors[6] = jnp.sum(jnp.where(chosen, vectors[6][None], 0.0), axis=1)
    vectors = [v.reshape(-1) for v in vectors]
    gain_one, bias_one, bias_qv, bias_out, gain_two, bias_two, bias_fc, bias_proj = vectors

    firsts = image_firsts(padding, image_ident)
    ext_tokens = jnp.concatenate(
        [shifted(tokens[rows - RIM :], 1), tokens, shifted(tokens[:RIM], -1)], axis=0
    )
    unit_one, scale_one = normed_parts(ext_tokens.astype(wide))
    normed_one = (unit_one * gain_one + bias_one).astype(low)
    none = jnp.zeros((width,), wide)
    bias_mixed = jnp.concatenate(grouped(bias_qv[:width], none, bias_qv[width:]))
    scale_mixed = jnp.concatenate(grouped(none + HEAD_DIM**-0.5, none + 1.0, none + 1.0))

    last = rings.stages - 1
    part_fc = rings.quad(after(w_fc, w_mixed))
    part_proj = rings.quad(after(w_proj, w_mixed))
    mixed = ((dot_nn(normed_one, w_mixed[:, : 3 * width]) + bias_mixed) * scale_mixed).astype(low)
    mixed, part_fc = lax.optimization_barrier((mixed, part_fc))
    for stage in range(last - 1):
        part_fc = jnp.concatenate([part_fc, rings.pair(part_fc, stage)], axis=0)
    pair_fc = rings.pair(part_fc, last - 1)
    first_heads, first_lse = attend(firsts, mixed, rows, 0)
    first_heads, pair_fc, part_proj = lax.optimization_barrier((first_heads, pair_fc, part_proj))
    part_fc = jnp.concatenate([part_fc, pair_fc], axis=0)
    for stage in range(last - 1):
        part_proj = jnp.concatenate([part_proj, rings.pair(part_proj, stage)], axis=0)
    mixed, part_fc, part_proj, full_out = lax.optimization_barrier(
        (mixed, part_fc, part_proj, full_out)
    )
    pair_fc, pair_proj = rings.pair(part_fc, last), rings.pair(part_proj, last - 1)
    second_heads, second_lse = attend(firsts, mixed, rows, 1)
    second_heads, pair_fc, pair_proj = lax.optimization_barrier((second_heads, pair_fc, pair_proj))
    fc_own = jnp.concatenate([part_fc, pair_fc], axis=0)
    part_proj = jnp.concatenate([part_proj, pair_proj], axis=0)
    second_heads, fc_own, part_proj = lax.optimization_barrier((second_heads, fc_own, part_proj))
    fc_other = rings.swap(fc_own)
    proj_own = jnp.concatenate([part_proj, rings.pair(part_proj, last)], axis=0)
    proj_other = rings.swap(proj_own)
    feature = jnp.arange(width, dtype=jnp.int32)
    wanted = (owners[:, None] * feat_rows + jnp.arange(feat_rows, dtype=jnp.int32)).reshape(-1)
    reorder = (feature[:, None] == wanted[None, :]).astype(low)
    attended = jnp.concatenate([first_heads, second_heads], axis=1)

    middle = tokens.astype(wide) + (dot_nn(attended, full_out) + bias_out)
    unit_two, scale_two = normed_parts(middle)
    normed_two = (unit_two * gain_two + bias_two).astype(low)
    keep = padding.astype(wide)[:, None]
    grad_result = keep * cotangent.astype(wide)
    grad_result_low = grad_result.astype(low)
    half = fc_own.shape[0]

    def up(fc_part, proj_part, bias_part):
        hidden, pull = jax.vjp(quick_gelu, dot_nt(normed_two, fc_part) + bias_part)
        return hidden.astype(low), pull

    def down(pull, proj_part):
        return pull(dot_nt(grad_result_low, proj_part))[0].astype(low)

    gelu_own, pull_own = up(fc_own, proj_own, bias_fc[:half])
    gelu_other, pull_other = up(fc_other, proj_other, bias_fc[half:])
    grad_hidden_own = down(pull_own, proj_own)
    grad_hidden_other = down(pull_other, proj_other)
    mlp_cut = [
        dot_tn(grad_hidden_other, normed_two).astype(low),
        dot_tn(gelu_other, grad_result_low).astype(low),
    ]
    mlp_sent = [rings.swap(part) for part in mlp_cut]
    gelu_own = after(gelu_own, mlp_cut)
    up_own, up_other = dot_nn(gelu_own, proj_own), dot_nn(gelu_other, proj_other)
    output = (keep * (middle + up_own + up_other + bias_proj)).astype(low)
    gelu_own, mlp_sent, output = lax.optimization_barrier((gelu_own, mlp_sent, output))
    mlp_kept = added(
        [dot_tn(grad_hidden_own, normed_two), dot_tn(gelu_own, grad_result_low)], mlp_sent
    )
    mlp_kept, mlp_cut = rings.cut(mlp_kept)
    mlp_sent = rings.pairs(mlp_cut, last)
    grad_hidden_own = after(grad_hidden_own, mlp_cut)
    normed_turned = dot_nn(normed_one, reorder).astype(low)
    down_own, down_other = dot_nn(grad_hidden_own, fc_own), dot_nn(grad_hidden_other, fc_other)
    grad_norm_two = down_own + down_other
    grad_middle = grad_result + norm_back(unit_two, scale_two, gain_two, grad_norm_two)
    grad_branch = grad_middle.astype(low)
    grad_attended = dot_nt(grad_branch, full_out).astype(low)

    def total(values):
        return jnp.sum(values.astype(wide), axis=0)

    hidden_sums = jnp.concatenate([total(grad_hidden_own), total(grad_hidden_other)])
    hidden_sums = jnp.sum(jnp.where(chosen, hidden_sums.reshape(size, 1, -1), 0.0), axis=0)
    def unsided(flat, vectors):
        parts = []
        at = 0
        for vector in vectors:
            parts.append(flat[at : at + vector.shape[0]])
            at += vector.shape[0]
        return parts

    def scattered(values):
        return lax.psum_scatter(values, "dev", scatter_dimension=0, tiled=True)

    near, far = slice(0, width // 2), slice(width // 2, width)

    def product(lines, grads):
        return dot_tn(normed_turned[:, lines], grads)

    out_product = dot_tn(attended, grad_branch)
    grad_attended, mlp_sent = lax.optimization_barrier((grad_attended, mlp_sent))
    for stage in reversed(range(last)):
        mlp_kept, mlp_cut = rings.cut(added(mlp_kept, mlp_sent))
        mlp_sent = rings.pairs(mlp_cut, stage)
    grad_attended = after(grad_attended, mlp_cut, out_product, normed_turned)
    grad_out = scattered(out_product)
    first = attend_back(firsts, mixed, grad_attended, first_lse, 0)

    first, mlp_sent = lax.optimization_barrier((first, mlp_sent))
    mlp_kept, mlp_cut = rings.quarters(added(mlp_kept, mlp_sent))
    mlp_sent = rings.turned(mlp_cut)
    first_cut = product(far, after(first, mlp_cut)).astype(low)
    first_sent = [rings.swap(first_cut)]
    first_kept = [product(near, after(first, first_cut))]
    grad_attended, first_kept = lax.optimization_barrier((grad_attended, first_kept))
    second = attend_back(firsts, mixed, grad_attended, second_lse, 1)

    second, first_sent, mlp_sent = lax.optimization_barrier((second, first_sent, mlp_sent))
    first_kept, first_cut = rings.cut(added(first_kept, first_sent))
    first_sent = rings.pairs(first_cut, last)
    second_cut = product(far, after(second, first_cut)).astype(low)
    second_sent = [rings.swap(second_cut)]
    second_kept = [product(near, after(second, second_cut))]
    second_sent, first_sent, second_kept = lax.optimization_barrier(
        (second_sent, first_sent, second_kept)
    )
    second_kept, second_cut = rings.cut(added(second_kept, second_sent))
    second_sent = rings.pairs(second_cut, last)
    for stage in reversed(range(last)):
        first_kept, first_cut = rings.cut(added(first_kept, first_sent))
        first_sent = rings.pairs(first_cut, stage)
    grad_ext, norm_sums, mixed_sums = into_norm(
        first, after(second, second_cut, first_cut), w_mixed, ext_tokens
    )
    head = shifted(grad_ext[rows + RIM :], 1).astype(wide)
    tail = shifted(grad_ext[:RIM], -1).astype(wide)
    grad_ext, first_sent, second_sent, mlp_sent, grad_out = lax.optimization_barrier(
        (grad_ext, first_sent, second_sent, mlp_sent, grad_out)
    )
    for stage in reversed(range(last)):
        second_kept, second_cut = rings.cut(added(second_kept, second_sent))
        second_sent = rings.pairs(second_cut, stage)
    first_kept, first_cut = rings.quarters(added(first_kept, first_sent))
    first_sent = rings.turned(first_cut)
    grad_fc, grad_proj = quarters_added(mlp_kept, mlp_sent)
    grad_own, grad_fc, grad_proj, second_sent = lax.optimization_barrier(
        (after(grad_ext, second_cut, first_cut)[RIM : RIM + rows], grad_fc, grad_proj, second_sent)
    )
    second_kept, second_cut = rings.quarters(added(second_kept, second_sent))
    second_sent = rings.turned(second_cut)
    grad_norm_one = (
        after(grad_own, second_cut).astype(wide)
        + jnp.pad(head, ((0, rows - RIM), (0, 0)))
        + jnp.pad(tail, ((rows - RIM, 0), (0, 0)))
    )
    unit_own, scale_own = normed_parts(tokens.astype(wide))
    grad_tokens = (grad_middle + norm_back(unit_own, scale_own, gain_one, grad_norm_one)).astype(low)

    (grad_first,) = quarters_added(first_kept, first_sent)
    (grad_second,) = quarters_added(second_kept, second_sent)
    small_sums = jnp.concatenate(
        [
            g.reshape(size, -1)
            for g in (
                norm_sums[0],
                norm_sums[1],
                jnp.concatenate(ungrouped(mixed_sums[0], 0) + ungrouped(mixed_sums[0], 2)),
                total(grad_branch),
                total(grad_norm_two * unit_two),
                total(grad_norm_two),
                hidden_sums,
                total(grad_result),
            )
        ],
        axis=1,
    )
    count = small_sums.shape[1]
    all_sums = lax.all_gather(small_sums.reshape(1, size * count), "dev", axis=0, tiled=True)
    own_sums = lax.dynamic_slice_in_dim(all_sums, lax.axis_index("dev") * count, count, axis=1)
    small_outs = unsided(jnp.sum(own_sums, axis=0), smalls)
    grad_mixed = jnp.concatenate([grad_first, grad_second], axis=1)
    columns = [part for which in range(3) for part in ungrouped(grad_mixed, which)]
    return (
        output,
        grad_tokens,
        small_outs[0],
        small_outs[1],
        jnp.concatenate(columns, axis=1),
        small_outs[2],
        grad_out,
        small_outs[3],
        small_outs[4],
        small_outs[5],
        grad_fc,
        small_outs[6],
        grad_proj,
        small_outs[7],
    )


def solution(mesh):
    row = P("dev", None)
    line = P("dev")
    return jax.shard_map(
        shards,
        mesh=mesh,
        in_specs=(row, row, line, line, line, line, row, line, row, line, line, line, row, line, row, line),
        out_specs=(row, row, line, line, row, line, row, line, line, line, row, line, row, line),
        check_vma=False,
    )
```

```python
import jax
import jax.numpy as jnp
import numpy as np
from jax import lax
from jax.experimental import pallas as pl
from jax.experimental.pallas import tpu as pltpu
from jax.sharding import PartitionSpec as P


HEAD_DIM = 64
IMG = 577
RIM = IMG - 1
TILE = 128
KEYS = 592
LANES = 256
MASKED = -1e30
NOWHERE = 1 << 20


def dot_nt(a, b):
    return lax.dot_general(a, b, (((1,), (1,)), ((), ())), preferred_element_type=jnp.float32)


def dot_tn(a, b):
    return lax.dot_general(a, b, (((0,), (0,)), ((), ())), preferred_element_type=jnp.float32)


def dot_nn(a, b):
    return lax.dot_general(a, b, (((1,), (0,)), ((), ())), preferred_element_type=jnp.float32)


def paired(block):
    first = lax.broadcasted_iota(jnp.int32, block.shape, 1) < HEAD_DIM
    none = jnp.zeros_like(block)
    return jnp.concatenate([jnp.where(first, block, none), jnp.where(first, none, block)], axis=0)


def unpaired(wide):
    both = jnp.concatenate([wide[:HEAD_DIM, :TILE], wide[HEAD_DIM:, TILE:]], axis=0)
    return both.T


def key_window(first, ext_rows):
    low = first + RIM
    start = jnp.clip((low // 16) * 16, 0, ext_rows - KEYS)
    return pl.multiple_of(start, 16), low - start


def keep_image(scores, offset):
    edge = lax.broadcasted_iota(jnp.int32, (16, scores.shape[1]), 0)
    top = jnp.where(edge >= offset, scores[:16], MASKED)
    low = jnp.where(edge + (KEYS - 16) < offset + IMG, scores[KEYS - 16 :], MASKED)
    return jnp.concatenate([top, scores[16 : KEYS - 16], low], axis=0)


def attend_body(first_ref, q_ref, k_ref, v_ref, out_ref, lse_ref):
    tiles = out_ref.shape[0] // TILE

    def both(step, carry):
        pending = [tile(2 * step + k) for k in range(2)]
        for more in pending:
            more()
        return carry

    def tile(j):
        at = pl.multiple_of(j * TILE, TILE)
        here = pl.ds(at, TILE)
        asking = pl.ds(pl.multiple_of(at + RIM, 64), TILE)

        def item(first, pair):
            lanes = slice(pair * 128, pair * 128 + 128)
            start, offset = key_window(first, k_ref.shape[0])
            scores = dot_nt(k_ref[pl.ds(start, KEYS), lanes], paired(q_ref[asking, lanes]))
            scores = keep_image(scores, offset)
            peak = jnp.max(scores, axis=0, keepdims=True)
            weights = jnp.exp(scores - peak)
            total = jnp.sum(weights, axis=0, keepdims=True)
            mixed = dot_tn(v_ref[pl.ds(start, KEYS), lanes], weights.astype(jnp.bfloat16))
            mixed = unpaired(mixed / total)
            row = lax.broadcasted_iota(jnp.int32, (TILE, 128), 0) + at
            inside = (row >= first) & (row < first + IMG)
            return jnp.where(inside, mixed, 0.0).astype(jnp.bfloat16), peak + jnp.log(total)

        one, two = first_ref[j], first_ref[tiles + j]
        for pair in range(LANES // 128):
            mixed, lse = item(one, pair)
            out_ref[here, pair * 128 : pair * 128 + 128] = mixed
            lse_ref[0, 2 * pair : 2 * pair + 1, here] = lse[:, :TILE]
            lse_ref[0, 2 * pair + 1 : 2 * pair + 2, here] = lse[:, TILE:]

        def more():
            @pl.when(two != one)
            def _():
                fill()

        def fill():
            column = lax.broadcasted_iota(jnp.int32, (1, TILE), 1) + at
            inside = (column >= two) & (column < two + IMG)
            for pair in range(LANES // 128):
                lanes = slice(pair * 128, pair * 128 + 128)
                mixed, lse = item(two, pair)
                out_ref[here, lanes] = out_ref[here, lanes] + mixed
                for head in range(2):
                    line = slice(2 * pair + head, 2 * pair + head + 1)
                    new = lse[:, head * TILE : head * TILE + TILE]
                    lse_ref[0, line, here] = jnp.where(inside, new, lse_ref[0, line, here])

        return more

    lax.fori_loop(0, tiles // 2, both, 0)


def attend_back_body(
    first_ref, q_ref, k_ref, v_ref, grad_ref, lse_ref, mixed_ref, dk_sum, dv_sum
):
    rows = grad_ref.shape[0]
    tiles = rows // TILE
    mixed_ref[:RIM, :LANES] = jnp.zeros((RIM, LANES), jnp.bfloat16)
    mixed_ref[RIM + rows :, :LANES] = jnp.zeros((RIM, LANES), jnp.bfloat16)
    dk_sum[...] = jnp.zeros_like(dk_sum)
    dv_sum[...] = jnp.zeros_like(dv_sum)

    def tile(j, carry):
        at = pl.multiple_of(j * TILE, TILE)
        here = pl.ds(at, TILE)
        asking = pl.ds(pl.multiple_of(at + RIM, 64), TILE)
        column = lax.broadcasted_iota(jnp.int32, (1, TILE), 1) + at

        def item(first, pair):
            lanes = slice(pair * 128, pair * 128 + 128)
            start, offset = key_window(first, k_ref.shape[0])
            window = pl.ds(start, KEYS)
            keys = k_ref[window, lanes]
            queries = paired(q_ref[asking, lanes])
            grads = paired(grad_ref[here, lanes])
            inside = (column >= first) & (column < first + IMG)
            lse = jnp.concatenate(
                [
                    jnp.where(inside, lse_ref[0, 2 * pair : 2 * pair + 1, here], -MASKED),
                    jnp.where(inside, lse_ref[0, 2 * pair + 1 : 2 * pair + 2, here], -MASKED),
                ],
                axis=1,
            )
            probs = jnp.exp(keep_image(dot_nt(keys, queries), offset) - lse)
            grad_probs = dot_nt(v_ref[window, lanes], grads)
            dv_sum[window, lanes] += dot_nn(probs.astype(jnp.bfloat16), grads)
            inner = jnp.sum(grad_probs * probs, axis=0, keepdims=True)
            grad_scores = (probs * (grad_probs - inner)).astype(jnp.bfloat16)
            dk_sum[window, lanes] += dot_nn(grad_scores, queries)
            return unpaired(dot_tn(keys, grad_scores) * HEAD_DIM**-0.5).astype(jnp.bfloat16)

        one, two = first_ref[j], first_ref[tiles + j]
        for pair in range(LANES // 128):
            mixed_ref[asking, pair * 128 : pair * 128 + 128] = item(one, pair)

        @pl.when(two != one)
        def _():
            for pair in range(LANES // 128):
                lanes = slice(pair * 128, pair * 128 + 128)
                mixed_ref[asking, lanes] = mixed_ref[asking, lanes] + item(two, pair)

        return carry

    lax.fori_loop(0, tiles, tile, 0)
    mixed_ref[:, LANES : 2 * LANES] = dk_sum[...].astype(jnp.bfloat16)
    mixed_ref[:, 2 * LANES :] = dv_sum[...].astype(jnp.bfloat16)


def attention_cost(rows, width, products):
    return pl.CostEstimate(
        flops=2 * products * 10 * TILE * KEYS * width * 8,
        bytes_accessed=16 * rows * width,
        transcendentals=10 * TILE * KEYS * (width // HEAD_DIM),
    )


def mixed_specs(ext, base):
    return [
        pl.BlockSpec((ext, LANES), lambda g, f, at=at: (0, 3 * (base + g) + at)) for at in range(3)
    ]


def attend(firsts, mixed, rows, part):
    ext, width = mixed.shape[0], mixed.shape[1] // 3
    groups = width // LANES // 2
    return pl.pallas_call(
        attend_body,
        grid_spec=pltpu.PrefetchScalarGridSpec(
            num_scalar_prefetch=1,
            grid=(groups,),
            in_specs=mixed_specs(ext, part * groups),
            out_specs=[
                pl.BlockSpec((rows, LANES), lambda g, f: (0, g)),
                pl.BlockSpec((1, LANES // HEAD_DIM, rows), lambda g, f: (g, 0, 0)),
            ],
        ),
        out_shape=[
            jax.ShapeDtypeStruct((rows, width // 2), jnp.bfloat16),
            jax.ShapeDtypeStruct((groups, LANES // HEAD_DIM, rows), jnp.float32),
        ],
        cost_estimate=attention_cost(rows, width // 2, 3),
        name="attend",
    )(firsts, mixed, mixed, mixed)


def attend_back(firsts, mixed, grads, lse, part):
    ext, width = mixed.shape[0], mixed.shape[1] // 3
    rows = grads.shape[0]
    groups = width // LANES // 2
    base = part * groups
    return pl.pallas_call(
        attend_back_body,
        grid_spec=pltpu.PrefetchScalarGridSpec(
            num_scalar_prefetch=1,
            grid=(groups,),
            in_specs=mixed_specs(ext, base)
            + [
                pl.BlockSpec((rows, LANES), lambda g, f: (0, base + g)),
                pl.BlockSpec((1, LANES // HEAD_DIM, rows), lambda g, f: (g, 0, 0)),
            ],
            out_specs=pl.BlockSpec((ext, 3 * LANES), lambda g, f: (0, g)),
            scratch_shapes=[pltpu.VMEM((ext, LANES), jnp.float32)] * 2,
        ),
        out_shape=jax.ShapeDtypeStruct((ext, 3 * width // 2), jnp.bfloat16),
        cost_estimate=attention_cost(rows, width // 2, 5),
        name="attend_back",
    )(firsts, mixed, mixed, mixed, grads, lse)


def into_norm_body(first_ref, second_ref, w_ref, tokens_ref, out_ref, sums_ref):
    cut = first_ref.shape[1]
    grads = dot_nt(first_ref[...], w_ref[:, :cut]) + dot_nt(
        second_ref[...], w_ref[:, cut : 2 * cut]
    )
    out_ref[...] = grads.astype(jnp.bfloat16)
    unit = normed_parts(tokens_ref[...].astype(jnp.float32))[0]
    @pl.when(pl.program_id(0) == 0)
    def _():
        sums_ref[...] = jnp.zeros_like(sums_ref)

    sums_ref[0:1, :] += jnp.sum(grads * unit, axis=0, keepdims=True)
    sums_ref[1:2, :] += jnp.sum(grads, axis=0, keepdims=True)
    groups = cut // (3 * LANES)
    for part, ref in enumerate((first_ref, second_ref)):
        line = jnp.sum(ref[...].astype(jnp.float32), axis=0, keepdims=True)
        for group in range(groups):
            to = (part * groups + group) * LANES
            at = 3 * group * LANES
            sums_ref[2:3, to : to + LANES] += line[:, at : at + LANES]
            sums_ref[3:4, to : to + LANES] += line[:, at + 2 * LANES : at + 3 * LANES]


def into_norm(first, second, w_mixed, tokens):
    ext, cut = first.shape
    width = tokens.shape[1]
    steps = 4
    block = ext // steps
    whole = lambda i: (0, 0)
    return pl.pallas_call(
        into_norm_body,
        grid=(steps,),
        in_specs=[
            pl.BlockSpec((block, cut), lambda i: (i, 0)),
            pl.BlockSpec((block, cut), lambda i: (i, 0)),
            pl.BlockSpec(w_mixed.shape, whole, pipeline_mode=pl.Buffered(1)),
            pl.BlockSpec((block, width), lambda i: (i, 0)),
        ],
        out_specs=[
            pl.BlockSpec((block, width), lambda i: (i, 0)),
            pl.BlockSpec((8, width), whole),
        ],
        out_shape=[
            jax.ShapeDtypeStruct((ext, width), jnp.bfloat16),
            jax.ShapeDtypeStruct((8, width), jnp.float32),
        ],
        cost_estimate=pl.CostEstimate(
            flops=4 * ext * cut * width, bytes_accessed=8 * ext * cut, transcendentals=0
        ),
        name="into_norm",
    )(first, second, w_mixed, tokens)


def grouped(queries, keys, values):
    parts = []
    for at in range(0, keys.shape[-1], LANES):
        parts += [part[..., at : at + LANES] for part in (queries, keys, values)]
    return parts


def ungrouped(columns, which):
    width = columns.shape[-1]
    return [
        columns[..., at : at + LANES] for at in range(which * LANES, width, 3 * LANES)
    ]


def image_firsts(padding, ident):
    rows = padding.shape[0]
    tiles = rows // TILE
    real = padding == 1
    by_tile = jnp.where(real, ident, NOWHERE).reshape(tiles, TILE)
    low_id = jnp.min(by_tile, axis=1)
    high_id = jnp.max(jnp.where(real, ident, -1).reshape(tiles, TILE), axis=1)
    wanted = jnp.concatenate([low_id, high_id])
    place = jnp.arange(rows, dtype=jnp.int32)[None, :]
    mine = real[None, :] & (ident[None, :] == wanted[:, None])
    run_first = jnp.min(jnp.where(mine, place, NOWHERE), axis=1)
    run_last = jnp.max(jnp.where(mine, place, -1), axis=1)
    firsts = jnp.where(run_last < rows - 1, run_last - RIM, run_first)
    empty = jnp.concatenate([low_id, low_id]) == NOWHERE
    before = jnp.tile(jnp.arange(tiles, dtype=jnp.int32) * TILE - IMG, 2)
    return jnp.where(empty, before, firsts)


def normed_parts(values):
    centered = values - jnp.mean(values, axis=-1, keepdims=True)
    spread = jnp.mean(centered * centered, axis=-1, keepdims=True)
    scale = lax.rsqrt(spread + 1e-05)
    return centered * scale, scale


def norm_back(unit, scale, gain, grads):
    scaled = grads * gain
    return scale * (
        scaled
        - jnp.mean(scaled, axis=-1, keepdims=True)
        - unit * jnp.mean(scaled * unit, axis=-1, keepdims=True)
    )


def quick_gelu(values):
    return values * jax.nn.sigmoid(1.702 * values)


def shifted(value, by):
    size = lax.axis_size("dev")
    pairs = [(i, i + by) for i in range(size) if 0 <= i + by < size]
    return lax.ppermute(value, "dev", pairs)


class Rings:
    def __init__(self, size):
        bits = size.bit_length() - 1
        self.size = size
        self.top = bits - 2
        middle = list(range(1, self.top))
        self.orders = (middle, middle[::-1])
        self.stages = len(middle)
        halves = []
        for order in self.orders:
            blocks = [(0, r) for r in range(4)]
            for bit in order:
                blocks = blocks + [(mask ^ (1 << bit), r) for mask, r in blocks]
            halves.append(blocks)
        self.blocks = [
            halves[core] + [(mask ^ 1, r) for mask, r in halves[1 - core]] for core in range(2)
        ]

    def rotated(self, device, by):
        low = device % (1 << self.top)
        return (((device >> self.top) + by) % 4 << self.top) | low

    def permute(self, value, target):
        return lax.ppermute(value, "dev", [(i, target(i)) for i in range(self.size)])

    def turn(self, value, by):
        return self.permute(value, lambda i: self.rotated(i, by))

    def pair(self, value, stage):
        return self.permute(value, lambda i: i ^ (1 << self.orders[i & 1][stage]))

    def pairs(self, values, stage):
        return [self.pair(value, stage) for value in values]

    def swap(self, value):
        return self.permute(value, lambda i: i ^ 1)

    def owners(self):
        me = lax.axis_index("dev")
        lists = []
        for core in range(2):
            masks = np.array([mask for mask, _ in self.blocks[core]], np.int32)
            turns = np.array([r for _, r in self.blocks[core]], np.int32)
            low = (me ^ masks) & ((1 << self.top) - 1)
            lists.append((((me >> self.top) + turns) & 3) << self.top | low)
        return jnp.where(me & 1 == 0, lists[0], lists[1])

    def quad(self, block):
        return jnp.concatenate([block] + [self.turn(block, -r) for r in (1, 2, 3)], axis=0)

    def cut(self, totals):
        at = totals[0].shape[0] // 2
        sent = [total[at:].astype(jnp.bfloat16) for total in totals]
        return [total[:at] for total in totals], sent

    def quarters(self, totals):
        rows = totals[0].shape[0] // 4
        sent = []
        for r in (1, 2, 3):
            here = slice(r * rows, (r + 1) * rows)
            sent.append(jnp.concatenate([t[here].astype(jnp.bfloat16) for t in totals], axis=1))
        return [total[:rows] for total in totals], sent

    def turned(self, parts):
        return [self.turn(part, r) for r, part in zip((1, 2, 3), parts)]


def added(kept, received):
    return [total + part.astype(jnp.float32) for total, part in zip(kept, received)]


def quarters_added(kept, received):
    sums = []
    at = 0
    for total in kept:
        for part in received:
            total = total + part[:, at : at + total.shape[1]].astype(jnp.float32)
        sums.append(total)
        at += total.shape[1]
    return sums


def joined(parts):
    return jnp.concatenate([part.astype(jnp.bfloat16) for part in parts], axis=1)


def after(value, *others):
    return lax.optimization_barrier((value, others))[0]


def shards(
    tokens,
    cotangent,
    padding,
    image_ident,
    ln1_gain,
    ln1_bias,
    w_qkv,
    b_qv,
    w_out,
    b_out,
    ln2_gain,
    ln2_bias,
    w_fc,
    b_fc,
    w_proj,
    b_proj,
):
    low = jnp.bfloat16
    wide = jnp.float32
    size = lax.axis_size("dev")
    width = w_out.shape[1]
    rows = tokens.shape[0]
    feat_rows = w_qkv.shape[0]
    smalls = (ln1_gain, ln1_bias, b_qv, b_out, ln2_gain, ln2_bias, b_fc, b_proj)
    extra = 128
    rings = Rings(size)
    owners = rings.owners()
    slots = -(-len(smalls) // feat_rows)
    slot = extra // slots
    lines = [jnp.pad(v, (0, slot - v.shape[0])) for v in smalls]
    side = []
    for at in range(0, len(lines), feat_rows):
        part = jnp.stack(lines[at : at + feat_rows])
        side.append(jnp.pad(part, ((0, feat_rows - part.shape[0]), (0, 0))))
    side = jnp.concatenate(side, axis=1)
    columns = grouped(w_qkv[:, :width], w_qkv[:, width : 2 * width], w_qkv[:, 2 * width :])
    w_mixed = lax.all_gather(
        jnp.concatenate(columns + [side], axis=1), "dev", axis=0, tiled=True
    )
    full_out = lax.all_gather(w_out, "dev", axis=0, tiled=True)
    side_all = w_mixed[:, 3 * width :].reshape(size, feat_rows, extra).astype(wide)
    vectors = []
    for at, v in enumerate(smalls):
        first = at // feat_rows * slot
        vectors.append(side_all[:, at % feat_rows, first : first + v.shape[0]])
    chosen = (owners[:, None] == jnp.arange(size, dtype=jnp.int32)[None, :])[:, :, None]
    gain_turned, bias_turned, vectors[6] = [
        jnp.sum(jnp.where(chosen, vectors[at][None], 0.0), axis=1) for at in (0, 1, 6)
    ]
    vectors = [v.reshape(-1) for v in vectors]
    gain_one, bias_one, bias_qv, bias_out, gain_two, bias_two, bias_fc, bias_proj = vectors

    firsts = image_firsts(padding, image_ident)
    ext_tokens = jnp.concatenate(
        [shifted(tokens[rows - RIM :], 1), tokens, shifted(tokens[:RIM], -1)], axis=0
    )
    feature = jnp.arange(width, dtype=jnp.int32)
    wanted = (owners[:, None] * feat_rows + jnp.arange(feat_rows, dtype=jnp.int32)).reshape(-1)
    reorder = (feature[:, None] == wanted[None, :]).astype(low)
    tokens_turned = dot_nn(ext_tokens, reorder).astype(low)
    unit_one, scale_one = normed_parts(ext_tokens.astype(wide))
    mean_one = jnp.mean(ext_tokens.astype(wide), axis=-1, keepdims=True)
    scale_one, tokens_turned = lax.optimization_barrier((scale_one, tokens_turned))
    unit_one = (ext_tokens.astype(wide) - mean_one) * scale_one
    normed_one = (unit_one * gain_one + bias_one).astype(low)
    groups = width // LANES
    bias_q, bias_v = bias_qv.reshape(2, groups, LANES)
    bias_mixed = jnp.stack([bias_q, jnp.zeros_like(bias_q), bias_v], axis=1).reshape(-1)
    scale_mixed = np.tile(np.repeat(np.array([HEAD_DIM**-0.5, 1, 1], np.float32), LANES), groups)

    last = rings.stages - 1
    part_fc = rings.quad(after(w_fc, w_mixed))
    part_proj = rings.quad(after(w_proj, w_mixed))
    centered = tokens_turned.astype(wide) - mean_one
    normed_turned = (
        centered * scale_one * gain_turned.reshape(-1) + bias_turned.reshape(-1)
    ).astype(low)
    mixed = ((dot_nn(normed_one, w_mixed[:, : 3 * width]) + bias_mixed) * scale_mixed).astype(low)
    mixed, part_fc = lax.optimization_barrier((mixed, part_fc))
    for stage in range(last - 1):
        part_fc = jnp.concatenate([part_fc, rings.pair(part_fc, stage)], axis=0)
    pair_fc = rings.pair(part_fc, last - 1)
    first_heads, first_lse = attend(firsts, mixed, rows, 0)
    first_heads, pair_fc, part_proj = lax.optimization_barrier((first_heads, pair_fc, part_proj))
    part_fc = jnp.concatenate([part_fc, pair_fc], axis=0)
    for stage in range(last - 1):
        part_proj = jnp.concatenate([part_proj, rings.pair(part_proj, stage)], axis=0)
    mixed, part_fc, part_proj, full_out, normed_turned = lax.optimization_barrier(
        (mixed, part_fc, part_proj, full_out, normed_turned)
    )
    pair_fc, pair_proj = rings.pair(part_fc, last), rings.pair(part_proj, last - 1)
    second_heads, second_lse = attend(firsts, mixed, rows, 1)
    second_heads, pair_fc, pair_proj = lax.optimization_barrier((second_heads, pair_fc, pair_proj))
    fc_own = jnp.concatenate([part_fc, pair_fc], axis=0)
    part_proj = jnp.concatenate([part_proj, pair_proj], axis=0)
    second_heads, fc_own, part_proj = lax.optimization_barrier((second_heads, fc_own, part_proj))
    fc_other = rings.swap(fc_own)
    pair_proj = rings.pair(part_proj, last)
    attended = jnp.concatenate([first_heads, second_heads], axis=1)

    middle = tokens.astype(wide) + (dot_nn(attended, full_out) + bias_out)
    unit_two, scale_two = normed_parts(middle)
    normed_two = (unit_two * gain_two + bias_two).astype(low)
    keep = padding.astype(wide)[:, None]
    grad_result = keep * cotangent.astype(wide)
    grad_result_low = grad_result.astype(low)
    half = fc_own.shape[0]

    def up(fc_part, bias_part):
        hidden, pull = jax.vjp(quick_gelu, dot_nt(normed_two, fc_part) + bias_part)
        return hidden.astype(low), pull

    def down(pull, grads, proj_part):
        return pull(dot_nt(grads, proj_part))[0].astype(low)

    gelu_own, pull_own = up(fc_own, bias_fc[:half])
    gelu_other, pull_other = up(fc_other, bias_fc[half:])
    gelu_own, gelu_other, pair_proj = lax.optimization_barrier((gelu_own, gelu_other, pair_proj))
    proj_own = jnp.concatenate([part_proj, pair_proj], axis=0)
    proj_other = rings.swap(proj_own)
    proj_cut = dot_tn(gelu_other, after(grad_result_low, proj_own)).astype(low)
    proj_sent = rings.swap(proj_cut)
    grad_hidden_own = down(pull_own, after(grad_result_low, proj_cut), proj_own)
    grad_hidden_other = down(pull_other, after(grad_result_low, grad_hidden_own), proj_other)
    fc_cut = dot_tn(grad_hidden_other, normed_two).astype(low)
    fc_sent = rings.swap(fc_cut)
    gelu_own, proj_sent = lax.optimization_barrier((after(gelu_own, fc_cut), proj_sent))
    (proj_kept,), (proj_cut,) = rings.cut(
        added([dot_tn(gelu_own, grad_result_low)], [proj_sent])
    )
    proj_sent = rings.pair(proj_cut, last)
    gelu_own = after(gelu_own, proj_cut)
    up_own, up_other = dot_nn(gelu_own, proj_own), dot_nn(gelu_other, proj_other)
    output = (keep * (middle + up_own + up_other + bias_proj)).astype(low)
    grad_hidden_own, fc_sent, output = lax.optimization_barrier((grad_hidden_own, fc_sent, output))
    (fc_kept,), (fc_cut,) = rings.cut(added([dot_tn(grad_hidden_own, normed_two)], [fc_sent]))
    fc_sent = rings.pair(fc_cut, last)
    grad_hidden_own = after(grad_hidden_own, fc_cut)
    down_own, down_other = dot_nn(grad_hidden_own, fc_own), dot_nn(grad_hidden_other, fc_other)
    down_own, proj_sent = lax.optimization_barrier((after(down_own, down_other), proj_sent))
    for stage in reversed(range(last)):
        (proj_kept,), (proj_cut,) = rings.cut(added([proj_kept], [proj_sent]))
        proj_sent = rings.pair(proj_cut, stage)
    grad_norm_two = after(down_own, proj_cut) + down_other
    grad_middle = grad_result + norm_back(unit_two, scale_two, gain_two, grad_norm_two)
    grad_branch = grad_middle.astype(low)
    grad_attended = dot_nt(grad_branch, full_out).astype(low)

    def total(values):
        return jnp.sum(values.astype(wide), axis=0)

    hidden_sums = jnp.concatenate([total(grad_hidden_own), total(grad_hidden_other)])
    hidden_sums = jnp.sum(jnp.where(chosen, hidden_sums.reshape(size, 1, -1), 0.0), axis=0)
    near, far = slice(0, width // 2), slice(width // 2, width)

    def product(lines, grads):
        return dot_tn(normed_turned[:, lines], grads)

    early_sums = jnp.concatenate(
        [
            total(grad_branch),
            total(grad_norm_two * unit_two),
            total(grad_norm_two),
            total(grad_result),
            hidden_sums.reshape(-1),
        ]
    )
    early_all = lax.all_gather(early_sums.reshape(-1, width), "dev", axis=0)
    attended_turned = dot_nn(attended, reorder).astype(low)
    grad_attended, fc_sent = lax.optimization_barrier((grad_attended, fc_sent))
    for stage in reversed(range(last)):
        (fc_kept,), (fc_cut,) = rings.cut(added([fc_kept], [fc_sent]))
        fc_sent = rings.pair(fc_cut, stage)
    mlp_kept, mlp_sent = [fc_kept, proj_kept], [fc_sent, proj_sent]
    grad_attended = after(grad_attended, fc_cut, early_sums, attended_turned)
    first = attend_back(firsts, mixed, grad_attended, first_lse, 0)

    first, mlp_sent, early_all = lax.optimization_barrier((first, mlp_sent, early_all))
    mlp_kept, mlp_cut = rings.quarters(added(mlp_kept, mlp_sent))
    mlp_sent = rings.turned(mlp_cut)
    first_cut = joined(
        [product(far, after(first, mlp_cut)), dot_tn(attended_turned[:, far], grad_branch)]
    )
    first_sent = rings.swap(first_cut)
    first_kept = [
        product(near, after(first, first_cut)),
        dot_tn(attended_turned[:, near], grad_branch),
    ]
    grad_attended, first_kept = lax.optimization_barrier((grad_attended, first_kept))
    second = attend_back(firsts, mixed, grad_attended, second_lse, 1)

    second, first_sent, mlp_sent = lax.optimization_barrier((second, first_sent, mlp_sent))
    first_kept, first_cut = rings.cut(quarters_added(first_kept, [first_sent]))
    first_cut = joined(first_cut)
    first_sent = rings.pair(first_cut, last)
    second_cut = product(far, after(second, first_cut)).astype(low)
    second_sent = [rings.swap(second_cut)]
    second_kept = [product(near, after(second, second_cut))]
    second_sent, first_sent, second_kept = lax.optimization_barrier(
        (second_sent, first_sent, second_kept)
    )
    second_kept, second_cut = rings.cut(added(second_kept, second_sent))
    second_sent = rings.pairs(second_cut, last)
    for stage in reversed(range(last)):
        first_kept, first_cut = rings.cut(quarters_added(first_kept, [first_sent]))
        first_cut = joined(first_cut)
        first_sent = rings.pair(first_cut, stage)
    grad_ext, late_sums = into_norm(
        first, after(second, second_cut, first_cut), w_mixed, ext_tokens
    )
    head = shifted(grad_ext[rows + RIM :], 1).astype(wide)
    tail = shifted(grad_ext[:RIM], -1).astype(wide)
    grad_ext, first_sent, second_sent = lax.optimization_barrier(
        (grad_ext, first_sent, second_sent)
    )
    for stage in reversed(range(last)):
        second_kept, second_cut = rings.cut(added(second_kept, second_sent))
        second_sent = rings.pairs(second_cut, stage)
    first_kept, first_cut = rings.quarters(quarters_added(first_kept, [first_sent]))
    first_sent = rings.turned(first_cut)
    grad_fc, grad_proj = quarters_added(mlp_kept, mlp_sent)
    grad_own, grad_fc, grad_proj, second_sent = lax.optimization_barrier(
        (after(grad_ext, second_cut, first_cut)[RIM : RIM + rows], grad_fc, grad_proj, second_sent)
    )
    second_kept, second_cut = rings.quarters(added(second_kept, second_sent))
    second_sent = rings.turned(second_cut)
    grad_norm_one = (
        after(grad_own, second_cut).astype(wide)
        + jnp.pad(head, ((0, rows - RIM), (0, 0)))
        + jnp.pad(tail, ((rows - RIM, 0), (0, 0)))
    )
    unit_own, scale_own = normed_parts(tokens.astype(wide))
    grad_tokens = (grad_middle + norm_back(unit_own, scale_own, gain_one, grad_norm_one)).astype(low)

    grad_first, grad_out = quarters_added(first_kept, first_sent)
    (grad_second,) = quarters_added(second_kept, second_sent)
    late_all = lax.all_gather(late_sums, "dev", axis=0)
    me = lax.axis_index("dev")

    def share(sums, at, count):
        return lax.dynamic_slice_in_dim(sums[at : at + count].reshape(-1), me * (count * feat_rows), count * feat_rows)

    late, early = jnp.sum(late_all, axis=0), jnp.sum(early_all, axis=0)
    small_outs = (
        share(late, 0, 1),
        share(late, 1, 1),
        share(late, 2, 2),
        share(early, 0, 1),
        share(early, 1, 1),
        share(early, 2, 1),
        share(early, 4, early.shape[0] - 4),
        share(early, 3, 1),
    )
    grad_mixed = jnp.concatenate([grad_first, grad_second], axis=1)
    columns = [part for which in range(3) for part in ungrouped(grad_mixed, which)]
    return (
        output,
        grad_tokens,
        small_outs[0],
        small_outs[1],
        jnp.concatenate(columns, axis=1),
        small_outs[2],
        grad_out,
        small_outs[3],
        small_outs[4],
        small_outs[5],
        grad_fc,
        small_outs[6],
        grad_proj,
        small_outs[7],
    )


def solution(mesh):
    row = P("dev", None)
    line = P("dev")
    return jax.shard_map(
        shards,
        mesh=mesh,
        in_specs=(row, row, line, line, line, line, row, line, row, line, line, line, row, line, row, line),
        out_specs=(row, row, line, line, row, line, row, line, line, line, row, line, row, line),
        check_vma=False,
    )
```

```python
import jax
import jax.numpy as jnp
import numpy as np
from jax import lax
from jax.experimental import pallas as pl
from jax.experimental.pallas import tpu as pltpu
from jax.sharding import PartitionSpec as P


HEAD_DIM = 64
IMG = 577
RIM = IMG - 1
TILE = 128
KEYS = 592
LANES = 256
MASKED = -1e30
NOWHERE = 1 << 20


def dot_nt(a, b):
    return lax.dot_general(a, b, (((1,), (1,)), ((), ())), preferred_element_type=jnp.float32)


def dot_tn(a, b):
    return lax.dot_general(a, b, (((0,), (0,)), ((), ())), preferred_element_type=jnp.float32)


def dot_nn(a, b):
    return lax.dot_general(a, b, (((1,), (0,)), ((), ())), preferred_element_type=jnp.float32)


def paired(block):
    first = lax.broadcasted_iota(jnp.int32, block.shape, 1) < HEAD_DIM
    none = jnp.zeros_like(block)
    return jnp.concatenate([jnp.where(first, block, none), jnp.where(first, none, block)], axis=0)


def unpaired(wide):
    both = jnp.concatenate([wide[:HEAD_DIM, :TILE], wide[HEAD_DIM:, TILE:]], axis=0)
    return both.T


def key_window(first, ext_rows):
    low = first + RIM
    start = jnp.clip((low // 16) * 16, 0, ext_rows - KEYS)
    return pl.multiple_of(start, 16), low - start


def keep_image(scores, offset):
    edge = lax.broadcasted_iota(jnp.int32, (16, scores.shape[1]), 0)
    top = jnp.where(edge >= offset, scores[:16], MASKED)
    low = jnp.where(edge + (KEYS - 16) < offset + IMG, scores[KEYS - 16 :], MASKED)
    return jnp.concatenate([top, scores[16 : KEYS - 16], low], axis=0)


def attend_body(first_ref, q_ref, k_ref, v_ref, out_ref, lse_ref):
    tiles = out_ref.shape[0] // TILE

    def both(step, carry):
        pending = [tile(2 * step + k) for k in range(2)]
        for more in pending:
            more()
        return carry

    def tile(j):
        at = pl.multiple_of(j * TILE, TILE)
        here = pl.ds(at, TILE)
        asking = pl.ds(pl.multiple_of(at + RIM, 64), TILE)

        def item(first, pair):
            lanes = slice(pair * 128, pair * 128 + 128)
            start, offset = key_window(first, k_ref.shape[0])
            scores = dot_nt(k_ref[pl.ds(start, KEYS), lanes], paired(q_ref[asking, lanes]))
            scores = keep_image(scores, offset)
            peak = jnp.max(scores, axis=0, keepdims=True)
            weights = jnp.exp(scores - peak)
            total = jnp.sum(weights, axis=0, keepdims=True)
            mixed = dot_tn(v_ref[pl.ds(start, KEYS), lanes], weights.astype(jnp.bfloat16))
            mixed = unpaired(mixed / total)
            row = lax.broadcasted_iota(jnp.int32, (TILE, 128), 0) + at
            inside = (row >= first) & (row < first + IMG)
            return jnp.where(inside, mixed, 0.0).astype(jnp.bfloat16), peak + jnp.log(total)

        one, two = first_ref[j], first_ref[tiles + j]
        for pair in range(LANES // 128):
            mixed, lse = item(one, pair)
            out_ref[here, pair * 128 : pair * 128 + 128] = mixed
            lse_ref[0, 2 * pair : 2 * pair + 1, here] = lse[:, :TILE]
            lse_ref[0, 2 * pair + 1 : 2 * pair + 2, here] = lse[:, TILE:]

        def more():
            @pl.when(two != one)
            def _():
                fill()

        def fill():
            column = lax.broadcasted_iota(jnp.int32, (1, TILE), 1) + at
            inside = (column >= two) & (column < two + IMG)
            for pair in range(LANES // 128):
                lanes = slice(pair * 128, pair * 128 + 128)
                mixed, lse = item(two, pair)
                out_ref[here, lanes] = out_ref[here, lanes] + mixed
                for head in range(2):
                    line = slice(2 * pair + head, 2 * pair + head + 1)
                    new = lse[:, head * TILE : head * TILE + TILE]
                    lse_ref[0, line, here] = jnp.where(inside, new, lse_ref[0, line, here])

        return more

    lax.fori_loop(0, tiles // 2, both, 0)


def attend_back_body(
    first_ref, q_ref, k_ref, v_ref, grad_ref, lse_ref, mixed_ref, dk_sum, dv_sum
):
    rows = grad_ref.shape[0]
    tiles = rows // TILE
    mixed_ref[:RIM, :LANES] = jnp.zeros((RIM, LANES), jnp.bfloat16)
    mixed_ref[RIM + rows :, :LANES] = jnp.zeros((RIM, LANES), jnp.bfloat16)
    dk_sum[...] = jnp.zeros_like(dk_sum)
    dv_sum[...] = jnp.zeros_like(dv_sum)

    def tile(j, carry):
        at = pl.multiple_of(j * TILE, TILE)
        here = pl.ds(at, TILE)
        asking = pl.ds(pl.multiple_of(at + RIM, 64), TILE)
        column = lax.broadcasted_iota(jnp.int32, (1, TILE), 1) + at

        def item(first, pair):
            lanes = slice(pair * 128, pair * 128 + 128)
            start, offset = key_window(first, k_ref.shape[0])
            window = pl.ds(start, KEYS)
            keys = k_ref[window, lanes]
            queries = paired(q_ref[asking, lanes])
            grads = paired(grad_ref[here, lanes])
            inside = (column >= first) & (column < first + IMG)
            lse = jnp.concatenate(
                [
                    jnp.where(inside, lse_ref[0, 2 * pair : 2 * pair + 1, here], -MASKED),
                    jnp.where(inside, lse_ref[0, 2 * pair + 1 : 2 * pair + 2, here], -MASKED),
                ],
                axis=1,
            )
            probs = jnp.exp(keep_image(dot_nt(keys, queries), offset) - lse)
            grad_probs = dot_nt(v_ref[window, lanes], grads)
            dv_sum[window, lanes] += dot_nn(probs.astype(jnp.bfloat16), grads)
            inner = jnp.sum(grad_probs * probs, axis=0, keepdims=True)
            grad_scores = (probs * (grad_probs - inner)).astype(jnp.bfloat16)
            dk_sum[window, lanes] += dot_nn(grad_scores, queries)
            return unpaired(dot_tn(keys, grad_scores) * HEAD_DIM**-0.5).astype(jnp.bfloat16)

        one, two = first_ref[j], first_ref[tiles + j]
        for pair in range(LANES // 128):
            mixed_ref[asking, pair * 128 : pair * 128 + 128] = item(one, pair)

        @pl.when(two != one)
        def _():
            for pair in range(LANES // 128):
                lanes = slice(pair * 128, pair * 128 + 128)
                mixed_ref[asking, lanes] = mixed_ref[asking, lanes] + item(two, pair)

        return carry

    lax.fori_loop(0, tiles, tile, 0)
    mixed_ref[:, LANES : 2 * LANES] = dk_sum[...].astype(jnp.bfloat16)
    mixed_ref[:, 2 * LANES :] = dv_sum[...].astype(jnp.bfloat16)


def attention_cost(rows, width, products):
    return pl.CostEstimate(
        flops=2 * products * 10 * TILE * KEYS * width * 8,
        bytes_accessed=16 * rows * width,
        transcendentals=10 * TILE * KEYS * (width // HEAD_DIM),
    )


def mixed_specs(ext):
    return [pl.BlockSpec((ext, LANES), lambda g, f, at=at: (0, 3 * g + at)) for at in range(3)]


def attend(firsts, mixed, rows):
    ext, width = mixed.shape[0], mixed.shape[1] // 3
    groups = width // LANES
    return pl.pallas_call(
        attend_body,
        grid_spec=pltpu.PrefetchScalarGridSpec(
            num_scalar_prefetch=1,
            grid=(groups,),
            in_specs=mixed_specs(ext),
            out_specs=[
                pl.BlockSpec((rows, LANES), lambda g, f: (0, g)),
                pl.BlockSpec((1, LANES // HEAD_DIM, rows), lambda g, f: (g, 0, 0)),
            ],
        ),
        out_shape=[
            jax.ShapeDtypeStruct((rows, width), jnp.bfloat16),
            jax.ShapeDtypeStruct((groups, LANES // HEAD_DIM, rows), jnp.float32),
        ],
        cost_estimate=attention_cost(rows, width, 3),
        name="attend",
    )(firsts, mixed, mixed, mixed)


def attend_back(firsts, mixed, grads, lse, part):
    ext, width = mixed.shape[0], mixed.shape[1] // 3
    rows = grads.shape[0]
    groups = width // LANES
    base = part * groups
    return pl.pallas_call(
        attend_back_body,
        grid_spec=pltpu.PrefetchScalarGridSpec(
            num_scalar_prefetch=1,
            grid=(groups,),
            in_specs=mixed_specs(ext)
            + [
                pl.BlockSpec((rows, LANES), lambda g, f: (0, base + g)),
                pl.BlockSpec((1, LANES // HEAD_DIM, rows), lambda g, f: (g, 0, 0)),
            ],
            out_specs=pl.BlockSpec((ext, 3 * LANES), lambda g, f: (0, g)),
            scratch_shapes=[pltpu.VMEM((ext, LANES), jnp.float32)] * 2,
        ),
        out_shape=jax.ShapeDtypeStruct((ext, 3 * width), jnp.bfloat16),
        cost_estimate=attention_cost(rows, width, 5),
        name="attend_back",
    )(firsts, mixed, mixed, mixed, grads, lse)


def into_norm_body(
    first_ref, second_ref, w_first_ref, w_second_ref, tokens_ref, out_ref, sums_ref
):
    cut = first_ref.shape[1]
    grads = dot_nt(first_ref[...], w_first_ref[...]) + dot_nt(second_ref[...], w_second_ref[...])
    out_ref[...] = grads.astype(jnp.bfloat16)
    unit = normed_parts(tokens_ref[...].astype(jnp.float32))[0]
    @pl.when(pl.program_id(0) == 0)
    def _():
        sums_ref[...] = jnp.zeros_like(sums_ref)

    sums_ref[0:1, :] += jnp.sum(grads * unit, axis=0, keepdims=True)
    sums_ref[1:2, :] += jnp.sum(grads, axis=0, keepdims=True)
    groups = cut // (3 * LANES)
    for part, ref in enumerate((first_ref, second_ref)):
        line = jnp.sum(ref[...].astype(jnp.float32), axis=0, keepdims=True)
        for group in range(groups):
            to = (part * groups + group) * LANES
            at = 3 * group * LANES
            sums_ref[2:3, to : to + LANES] += line[:, at : at + LANES]
            sums_ref[3:4, to : to + LANES] += line[:, at + 2 * LANES : at + 3 * LANES]


def into_norm(first, second, w_first, w_second, tokens):
    ext, cut = first.shape
    width = tokens.shape[1]
    steps = 4
    block = ext // steps
    whole = lambda i: (0, 0)
    return pl.pallas_call(
        into_norm_body,
        grid=(steps,),
        in_specs=[
            pl.BlockSpec((block, cut), lambda i: (i, 0)),
            pl.BlockSpec((block, cut), lambda i: (i, 0)),
            pl.BlockSpec((width, cut), whole, pipeline_mode=pl.Buffered(1)),
            pl.BlockSpec((width, cut), whole, pipeline_mode=pl.Buffered(1)),
            pl.BlockSpec((block, width), lambda i: (i, 0)),
        ],
        out_specs=[
            pl.BlockSpec((block, width), lambda i: (i, 0)),
            pl.BlockSpec((4, width), whole),
        ],
        out_shape=[
            jax.ShapeDtypeStruct((ext, width), jnp.bfloat16),
            jax.ShapeDtypeStruct((4, width), jnp.float32),
        ],
        cost_estimate=pl.CostEstimate(
            flops=4 * ext * cut * width, bytes_accessed=8 * ext * cut, transcendentals=0
        ),
        name="into_norm",
    )(first, second, w_first, w_second, tokens)


def grouped(queries, keys, values):
    parts = []
    for at in range(0, keys.shape[-1], LANES):
        parts += [part[..., at : at + LANES] for part in (queries, keys, values)]
    return parts


def ungrouped(columns, which):
    width = columns.shape[-1]
    return [
        columns[..., at : at + LANES] for at in range(which * LANES, width, 3 * LANES)
    ]


def image_firsts(padding, ident):
    rows = padding.shape[0]
    tiles = rows // TILE
    real = padding == 1
    by_tile = jnp.where(real, ident, NOWHERE).reshape(tiles, TILE)
    low_id = jnp.min(by_tile, axis=1)
    high_id = jnp.max(jnp.where(real, ident, -1).reshape(tiles, TILE), axis=1)
    wanted = jnp.concatenate([low_id, high_id])
    place = jnp.arange(rows, dtype=jnp.int32)[None, :]
    mine = real[None, :] & (ident[None, :] == wanted[:, None])
    run_first = jnp.min(jnp.where(mine, place, NOWHERE), axis=1)
    run_last = jnp.max(jnp.where(mine, place, -1), axis=1)
    firsts = jnp.where(run_last < rows - 1, run_last - RIM, run_first)
    empty = jnp.concatenate([low_id, low_id]) == NOWHERE
    before = jnp.tile(jnp.arange(tiles, dtype=jnp.int32) * TILE - IMG, 2)
    return jnp.where(empty, before, firsts)


def normed_parts(values):
    centered = values - jnp.mean(values, axis=-1, keepdims=True)
    spread = jnp.mean(centered * centered, axis=-1, keepdims=True)
    scale = lax.rsqrt(spread + 1e-05)
    return centered * scale, scale


def norm_back(unit, scale, gain, grads):
    scaled = grads * gain
    return scale * (
        scaled
        - jnp.mean(scaled, axis=-1, keepdims=True)
        - unit * jnp.mean(scaled * unit, axis=-1, keepdims=True)
    )


def quick_gelu(values):
    return values * jax.nn.sigmoid(1.702 * values)


def shifted(value, by):
    size = lax.axis_size("dev")
    pairs = [(i, i + by) for i in range(size) if 0 <= i + by < size]
    return lax.ppermute(value, "dev", pairs)


class Rings:
    def __init__(self, size):
        bits = size.bit_length() - 1
        self.size = size
        self.top = bits - 2
        middle = list(range(1, self.top))
        self.orders = (middle, middle[::-1])
        self.stages = len(middle)
        halves = []
        for order in self.orders:
            blocks = [(0, r) for r in range(4)]
            for bit in order:
                blocks = blocks + [(mask ^ (1 << bit), r) for mask, r in blocks]
            halves.append(blocks)
        self.blocks = [
            halves[core] + [(mask ^ 1, r) for mask, r in halves[1 - core]] for core in range(2)
        ]

    def rotated(self, device, by):
        low = device % (1 << self.top)
        return (((device >> self.top) + by) % 4 << self.top) | low

    def permute(self, value, target):
        return lax.ppermute(value, "dev", [(i, target(i)) for i in range(self.size)])

    def turn(self, value, by):
        return self.permute(value, lambda i: self.rotated(i, by))

    def pair(self, value, stage):
        return self.permute(value, lambda i: i ^ (1 << self.orders[i & 1][stage]))

    def pairs(self, values, stage):
        return [self.pair(value, stage) for value in values]

    def swap(self, value):
        return self.permute(value, lambda i: i ^ 1)

    def owners(self):
        me = lax.axis_index("dev")
        lists = []
        for core in range(2):
            masks = np.array([mask for mask, _ in self.blocks[core]], np.int32)
            turns = np.array([r for _, r in self.blocks[core]], np.int32)
            low = (me ^ masks) & ((1 << self.top) - 1)
            lists.append((((me >> self.top) + turns) & 3) << self.top | low)
        return jnp.where(me & 1 == 0, lists[0], lists[1])

    def quad(self, block):
        return jnp.concatenate(self.quad_parts(block), axis=0)

    def quad_parts(self, block):
        return [block] + [self.turn(block, -r) for r in (1, 2, 3)]

    def gathered(self, block):
        part = self.quad(block)
        for stage in range(self.stages):
            part = jnp.concatenate([part, self.pair(part, stage)], axis=0)
        return jnp.concatenate([part, self.swap(part)], axis=0)

    def all_sum(self, value):
        bit = 1
        while bit < self.size:
            value = value + self.permute(value, lambda i: i ^ bit)
            bit *= 2
        return value

    def cut(self, totals):
        at = totals[0].shape[0] // 2
        sent = [total[at:].astype(jnp.bfloat16) for total in totals]
        return [total[:at] for total in totals], sent

    def quarters(self, totals):
        rows = totals[0].shape[0] // 4
        sent = []
        for r in (1, 2, 3):
            here = slice(r * rows, (r + 1) * rows)
            sent.append(jnp.concatenate([t[here].astype(jnp.bfloat16) for t in totals], axis=1))
        return [total[:rows] for total in totals], sent

    def turned(self, parts):
        return [self.turn(part, r) for r, part in zip((1, 2, 3), parts)]


def added(kept, received):
    return [total + part.astype(jnp.float32) for total, part in zip(kept, received)]


def quarters_added(kept, received):
    sums = []
    at = 0
    for total in kept:
        for part in received:
            total = total + part[:, at : at + total.shape[1]].astype(jnp.float32)
        sums.append(total)
        at += total.shape[1]
    return sums


def joined(parts):
    return jnp.concatenate([part.astype(jnp.bfloat16) for part in parts], axis=1)


def after(value, *others):
    return lax.optimization_barrier((value, others))[0]


def shards(
    tokens,
    cotangent,
    padding,
    image_ident,
    ln1_gain,
    ln1_bias,
    w_qkv,
    b_qv,
    w_out,
    b_out,
    ln2_gain,
    ln2_bias,
    w_fc,
    b_fc,
    w_proj,
    b_proj,
):
    low = jnp.bfloat16
    wide = jnp.float32
    size = lax.axis_size("dev")
    width = w_out.shape[1]
    rows = tokens.shape[0]
    feat_rows = w_qkv.shape[0]
    smalls = (ln1_gain, ln1_bias, b_qv, b_out, ln2_gain, ln2_bias, b_fc, b_proj)
    extra = 128
    rings = Rings(size)
    owners = rings.owners()
    slots = -(-len(smalls) // feat_rows)
    slot = extra // slots
    lines = [jnp.pad(v, (0, slot - v.shape[0])) for v in smalls]
    side = []
    for at in range(0, len(lines), feat_rows):
        part = jnp.stack(lines[at : at + feat_rows])
        side.append(jnp.pad(part, ((0, feat_rows - part.shape[0]), (0, 0))))
    side = jnp.concatenate(side, axis=1)
    columns = grouped(w_qkv[:, :width], w_qkv[:, width : 2 * width], w_qkv[:, 2 * width :])
    half_columns = len(columns) // 2
    w_first = rings.gathered(jnp.concatenate(columns[:half_columns] + [side], axis=1))
    w_second = lax.all_gather(
        jnp.concatenate(columns[half_columns:] + [w_out], axis=1), "dev", axis=0, tiled=True
    )
    mixed_half = 3 * width // 2
    full_out = w_second[:, mixed_half:]
    chosen = (owners[:, None] == jnp.arange(size, dtype=jnp.int32)[None, :])[:, :, None]
    side_turned = w_first[:, mixed_half:].reshape(size, feat_rows, extra).astype(wide)
    used = min(len(smalls), feat_rows)
    side_turned = side_turned[:, :used].reshape(size, 1, used * extra)
    side_all = jnp.sum(jnp.where(chosen, side_turned, 0.0), axis=0).reshape(size, used, extra)
    side_turned = side_turned.reshape(size, used, extra)

    def vector(sides, at):
        first = at // feat_rows * slot
        return sides[:, at % feat_rows, first : first + smalls[at].shape[0]]

    gain_turned, bias_turned = vector(side_turned, 0), vector(side_turned, 1)
    vectors = [vector(side_turned if at == 6 else side_all, at) for at in range(len(smalls))]
    vectors = [v.reshape(-1) for v in vectors]
    gain_one, bias_one, bias_qv, bias_out, gain_two, bias_two, bias_fc, bias_proj = vectors

    firsts = image_firsts(padding, image_ident)
    ext_tokens = jnp.concatenate(
        [shifted(tokens[rows - RIM :], 1), tokens, shifted(tokens[:RIM], -1)], axis=0
    )
    feature = jnp.arange(width, dtype=jnp.int32)
    wanted = (owners[:, None] * feat_rows + jnp.arange(feat_rows, dtype=jnp.int32)).reshape(-1)
    reorder = (feature[:, None] == wanted[None, :]).astype(low)
    tokens_turned = dot_nn(ext_tokens, reorder).astype(low)
    scale_one = normed_parts(ext_tokens.astype(wide))[1]
    mean_one = jnp.mean(ext_tokens.astype(wide), axis=-1, keepdims=True)
    scale_one, tokens_turned = lax.optimization_barrier((scale_one, tokens_turned))
    groups = width // LANES
    bias_q, bias_v = bias_qv.reshape(2, groups, LANES)
    bias_mixed = jnp.stack([bias_q, jnp.zeros_like(bias_q), bias_v], axis=1).reshape(-1)
    scale_mixed = np.tile(np.repeat(np.array([HEAD_DIM**-0.5, 1, 1], np.float32), LANES), groups)

    last = rings.stages - 1
    part_fc = rings.quad(after(w_fc, w_first))
    parts_proj = rings.quad_parts(after(w_proj, w_first))
    centered = tokens_turned.astype(wide) - mean_one
    normed_turned = (
        centered * scale_one * gain_turned.reshape(-1) + bias_turned.reshape(-1)
    ).astype(low)
    normed_turned = lax.optimization_barrier(normed_turned)

    def mixed_part(rows_in, w_part, columns):
        products = dot_nn(rows_in, w_part[:, :mixed_half])
        return ((products + bias_mixed[columns]) * scale_mixed[columns]).astype(low)

    mixed_first = mixed_part(normed_turned, w_first, slice(0, mixed_half))
    mixed_first, part_fc = lax.optimization_barrier((mixed_first, part_fc))
    for stage in range(last - 1):
        part_fc = jnp.concatenate([part_fc, rings.pair(part_fc, stage)], axis=0)
    pair_fc = rings.pair(part_fc, last - 1)
    first_heads, first_lse = attend(firsts, mixed_first, rows)
    first_heads, pair_fc, parts_proj = lax.optimization_barrier((first_heads, pair_fc, parts_proj))
    part_proj = jnp.concatenate(parts_proj, axis=0)
    part_fc = jnp.concatenate([part_fc, pair_fc], axis=0)
    for stage in range(last - 1):
        part_proj = jnp.concatenate([part_proj, rings.pair(part_proj, stage)], axis=0)
    pair_fc, pair_proj = rings.pair(part_fc, last), rings.pair(part_proj, last - 1)
    scale_late = after(scale_one, part_fc, part_proj)
    normed_one = ((ext_tokens.astype(wide) - mean_one) * scale_late * gain_one + bias_one).astype(low)
    mixed_second = mixed_part(normed_one, w_second, slice(mixed_half, 2 * mixed_half))
    second_heads, second_lse = attend(firsts, mixed_second, rows)
    second_heads, pair_fc, pair_proj = lax.optimization_barrier((second_heads, pair_fc, pair_proj))
    fc_own = jnp.concatenate([part_fc, pair_fc], axis=0)
    part_proj = jnp.concatenate([part_proj, pair_proj], axis=0)
    second_heads, fc_own, part_proj = lax.optimization_barrier((second_heads, fc_own, part_proj))
    fc_other = rings.swap(fc_own)
    pair_proj = rings.pair(part_proj, last)
    attended = jnp.concatenate([first_heads, second_heads], axis=1)

    middle = tokens.astype(wide) + (dot_nn(attended, full_out) + bias_out)
    unit_two, scale_two = normed_parts(middle)
    normed_two = (unit_two * gain_two + bias_two).astype(low)
    keep = padding.astype(wide)[:, None]
    grad_result = keep * cotangent.astype(wide)
    grad_result_low = grad_result.astype(low)
    half = fc_own.shape[0]

    def up(fc_part, bias_part):
        hidden, pull = jax.vjp(quick_gelu, dot_nt(normed_two, fc_part) + bias_part)
        return hidden.astype(low), pull

    def down(pull, grads, proj_part):
        return pull(dot_nt(grads, proj_part))[0].astype(low)

    gelu_own, pull_own = up(fc_own, bias_fc[:half])
    gelu_other, pull_other = up(fc_other, bias_fc[half:])
    gelu_own, gelu_other, pair_proj = lax.optimization_barrier((gelu_own, gelu_other, pair_proj))
    proj_own = jnp.concatenate([part_proj, pair_proj], axis=0)
    proj_other = rings.swap(proj_own)
    proj_cut = dot_tn(gelu_other, after(grad_result_low, proj_own)).astype(low)
    proj_sent = rings.swap(proj_cut)
    grad_hidden_own = down(pull_own, after(grad_result_low, proj_cut), proj_own)
    grad_hidden_other = down(pull_other, after(grad_result_low, grad_hidden_own), proj_other)
    fc_cut = dot_tn(grad_hidden_other, normed_two).astype(low)
    fc_sent = rings.swap(fc_cut)
    gelu_own, proj_sent = lax.optimization_barrier((after(gelu_own, fc_cut), proj_sent))
    (proj_kept,), (proj_cut,) = rings.cut(
        added([dot_tn(gelu_own, grad_result_low)], [proj_sent])
    )
    proj_sent = rings.pair(proj_cut, last)
    gelu_own = after(gelu_own, proj_cut)
    up_own, up_other = dot_nn(gelu_own, proj_own), dot_nn(gelu_other, proj_other)
    output = (keep * (middle + up_own + up_other + bias_proj)).astype(low)
    grad_hidden_own, fc_sent, output = lax.optimization_barrier((grad_hidden_own, fc_sent, output))
    (fc_kept,), (fc_cut,) = rings.cut(added([dot_tn(grad_hidden_own, normed_two)], [fc_sent]))
    fc_sent = rings.pair(fc_cut, last)
    grad_hidden_own = after(grad_hidden_own, fc_cut)
    down_own, down_other = dot_nn(grad_hidden_own, fc_own), dot_nn(grad_hidden_other, fc_other)
    down_own, proj_sent = lax.optimization_barrier((after(down_own, down_other), proj_sent))
    for stage in reversed(range(last)):
        (proj_kept,), (proj_cut,) = rings.cut(added([proj_kept], [proj_sent]))
        proj_sent = rings.pair(proj_cut, stage)
    grad_norm_two = after(down_own, proj_cut) + down_other
    grad_middle = grad_result + norm_back(unit_two, scale_two, gain_two, grad_norm_two)
    grad_branch = grad_middle.astype(low)
    grad_attended = dot_nt(grad_branch, full_out).astype(low)

    def total(values):
        return jnp.sum(values.astype(wide), axis=0)

    hidden_sums = jnp.concatenate([total(grad_hidden_own), total(grad_hidden_other)])
    hidden_sums = jnp.sum(jnp.where(chosen, hidden_sums.reshape(size, 1, -1), 0.0), axis=0)
    near, far = slice(0, width // 2), slice(width // 2, width)
    w_restored = dot_nn(reorder, w_first[:, :mixed_half]).astype(low)

    def product(lines, grads):
        return dot_tn(normed_turned[:, lines], grads)

    early_sums = jnp.concatenate(
        [
            total(grad_branch),
            total(grad_norm_two * unit_two),
            total(grad_norm_two),
            total(grad_result),
            hidden_sums.reshape(-1),
        ]
    )
    early_all = lax.all_gather(early_sums.reshape(-1, width), "dev", axis=0)
    attended_turned = dot_nn(attended, reorder).astype(low)
    grad_attended, fc_sent = lax.optimization_barrier((grad_attended, fc_sent))
    for stage in reversed(range(last)):
        (fc_kept,), (fc_cut,) = rings.cut(added([fc_kept], [fc_sent]))
        fc_sent = rings.pair(fc_cut, stage)
    mlp_kept, mlp_sent = [fc_kept, proj_kept], [fc_sent, proj_sent]
    grad_attended = after(grad_attended, fc_cut, early_sums, attended_turned)
    first = attend_back(firsts, mixed_first, grad_attended, first_lse, 0)

    first, mlp_sent = lax.optimization_barrier((first, mlp_sent))
    mlp_kept, mlp_cut = rings.quarters(added(mlp_kept, mlp_sent))
    mlp_sent = rings.turned(mlp_cut)
    first_cut = joined(
        [product(far, after(first, mlp_cut)), dot_tn(attended_turned[:, far], grad_branch)]
    )
    first_sent = rings.swap(first_cut)
    first_kept = [
        product(near, after(first, first_cut)),
        dot_tn(attended_turned[:, near], grad_branch),
    ]
    grad_attended, first_kept = lax.optimization_barrier((grad_attended, first_kept))
    second = attend_back(firsts, mixed_second, grad_attended, second_lse, 1)

    second, first_sent, mlp_sent, early_all = lax.optimization_barrier(
        (second, first_sent, mlp_sent, early_all)
    )
    first_kept, first_cut = rings.cut(quarters_added(first_kept, [first_sent]))
    first_cut = joined(first_cut)
    first_sent = rings.pair(first_cut, last)
    second_cut = product(far, after(second, first_cut)).astype(low)
    second_sent = [rings.swap(second_cut)]
    second_kept = [product(near, after(second, second_cut))]
    second_sent, first_sent, second_kept = lax.optimization_barrier(
        (second_sent, first_sent, second_kept)
    )
    second_kept, second_cut = rings.cut(added(second_kept, second_sent))
    second_sent = rings.pairs(second_cut, last)
    for stage in reversed(range(last)):
        first_kept, first_cut = rings.cut(quarters_added(first_kept, [first_sent]))
        first_cut = joined(first_cut)
        first_sent = rings.pair(first_cut, stage)
    grad_ext, late_sums = into_norm(
        first, after(second, second_cut, first_cut), w_restored, w_second, ext_tokens
    )
    grad_ext, first_sent, second_sent, late_sums = lax.optimization_barrier(
        (grad_ext, first_sent, second_sent, late_sums)
    )
    ends = (grad_ext[rows + RIM :], grad_ext[:RIM])
    late_sums, ends = lax.optimization_barrier((late_sums, ends))
    head = shifted(ends[0], 1).astype(wide)
    tail = shifted(ends[1], -1).astype(wide)
    for stage in reversed(range(last)):
        second_kept, second_cut = rings.cut(added(second_kept, second_sent))
        second_sent = rings.pairs(second_cut, stage)
    first_kept, first_cut = rings.quarters(quarters_added(first_kept, [first_sent]))
    first_sent = rings.turned(first_cut)
    grad_fc, grad_proj = quarters_added(mlp_kept, mlp_sent)
    grad_own, grad_fc, grad_proj, second_sent = lax.optimization_barrier(
        (after(grad_ext, second_cut, first_cut)[RIM : RIM + rows], grad_fc, grad_proj, second_sent)
    )
    second_kept, second_cut = rings.quarters(added(second_kept, second_sent))
    second_sent = rings.turned(second_cut)
    grad_norm_one = (
        after(grad_own, second_cut).astype(wide)
        + jnp.pad(head, ((0, rows - RIM), (0, 0)))
        + jnp.pad(tail, ((rows - RIM, 0), (0, 0)))
    )
    unit_own, scale_own = normed_parts(tokens.astype(wide))
    grad_tokens = (grad_middle + norm_back(unit_own, scale_own, gain_one, grad_norm_one)).astype(low)

    grad_tokens, second_sent = lax.optimization_barrier((grad_tokens, second_sent))
    grad_first, grad_out = quarters_added(first_kept, first_sent)
    (grad_second,) = quarters_added(second_kept, second_sent)
    me = lax.axis_index("dev")

    def share(sums, at, count):
        return lax.dynamic_slice_in_dim(sums[at : at + count].reshape(-1), me * (count * feat_rows), count * feat_rows)

    late, early = rings.all_sum(late_sums), jnp.sum(early_all, axis=0)
    small_outs = (
        share(late, 0, 1),
        share(late, 1, 1),
        share(late, 2, 2),
        share(early, 0, 1),
        share(early, 1, 1),
        share(early, 2, 1),
        share(early, 4, early.shape[0] - 4),
        share(early, 3, 1),
    )
    grad_mixed = jnp.concatenate([grad_first, grad_second], axis=1)
    columns = [part for which in range(3) for part in ungrouped(grad_mixed, which)]
    return (
        output,
        grad_tokens,
        small_outs[0],
        small_outs[1],
        jnp.concatenate(columns, axis=1),
        small_outs[2],
        grad_out,
        small_outs[3],
        small_outs[4],
        small_outs[5],
        grad_fc,
        small_outs[6],
        grad_proj,
        small_outs[7],
    )


def solution(mesh):
    row = P("dev", None)
    line = P("dev")
    return jax.shard_map(
        shards,
        mesh=mesh,
        in_specs=(row, row, line, line, line, line, row, line, row, line, line, line, row, line, row, line),
        out_specs=(row, row, line, line, row, line, row, line, line, line, row, line, row, line),
        check_vma=False,
    )
```

```python
import jax
import jax.numpy as jnp
import numpy as np
from jax import lax
from jax.experimental import pallas as pl
from jax.experimental.pallas import tpu as pltpu
from jax.sharding import PartitionSpec as P


HEAD_DIM = 64
IMG = 577
RIM = IMG - 1
TILE = 128
KEYS = 592
LANES = 256
MASKED = -1e30
NOWHERE = 1 << 20


def dot_nt(a, b):
    return lax.dot_general(a, b, (((1,), (1,)), ((), ())), preferred_element_type=jnp.float32)


def dot_tn(a, b):
    return lax.dot_general(a, b, (((0,), (0,)), ((), ())), preferred_element_type=jnp.float32)


def dot_nn(a, b):
    return lax.dot_general(a, b, (((1,), (0,)), ((), ())), preferred_element_type=jnp.float32)


def paired(block):
    first = lax.broadcasted_iota(jnp.int32, block.shape, 1) < HEAD_DIM
    none = jnp.zeros_like(block)
    return jnp.concatenate([jnp.where(first, block, none), jnp.where(first, none, block)], axis=0)


def unpaired(wide):
    both = jnp.concatenate([wide[:HEAD_DIM, :TILE], wide[HEAD_DIM:, TILE:]], axis=0)
    return both.T


def key_window(first, ext_rows):
    low = first + RIM
    start = jnp.clip((low // 16) * 16, 0, ext_rows - KEYS)
    return pl.multiple_of(start, 16), low - start


def keep_image(scores, offset):
    edge = lax.broadcasted_iota(jnp.int32, (16, scores.shape[1]), 0)
    top = jnp.where(edge >= offset, scores[:16], MASKED)
    low = jnp.where(edge + (KEYS - 16) < offset + IMG, scores[KEYS - 16 :], MASKED)
    return jnp.concatenate([top, scores[16 : KEYS - 16], low], axis=0)


def attend_body(first_ref, q_ref, k_ref, v_ref, out_ref, lse_ref):
    tiles = out_ref.shape[0] // TILE

    def both(step, carry):
        pending = [tile(2 * step + k) for k in range(2)]
        for more in pending:
            more()
        return carry

    def tile(j):
        at = pl.multiple_of(j * TILE, TILE)
        here = pl.ds(at, TILE)
        asking = pl.ds(pl.multiple_of(at + RIM, 64), TILE)

        def item(first, pair):
            lanes = slice(pair * 128, pair * 128 + 128)
            start, offset = key_window(first, k_ref.shape[0])
            scores = dot_nt(k_ref[pl.ds(start, KEYS), lanes], paired(q_ref[asking, lanes]))
            scores = keep_image(scores, offset)
            peak = jnp.max(scores, axis=0, keepdims=True)
            weights = jnp.exp(scores - peak)
            total = jnp.sum(weights, axis=0, keepdims=True)
            mixed = dot_tn(v_ref[pl.ds(start, KEYS), lanes], weights.astype(jnp.bfloat16))
            mixed = unpaired(mixed / total)
            row = lax.broadcasted_iota(jnp.int32, (TILE, 128), 0) + at
            inside = (row >= first) & (row < first + IMG)
            return jnp.where(inside, mixed, 0.0).astype(jnp.bfloat16), peak + jnp.log(total)

        one, two = first_ref[j], first_ref[tiles + j]
        for pair in range(LANES // 128):
            mixed, lse = item(one, pair)
            out_ref[here, pair * 128 : pair * 128 + 128] = mixed
            lse_ref[0, 2 * pair : 2 * pair + 1, here] = lse[:, :TILE]
            lse_ref[0, 2 * pair + 1 : 2 * pair + 2, here] = lse[:, TILE:]

        def more():
            @pl.when(two != one)
            def _():
                fill()

        def fill():
            column = lax.broadcasted_iota(jnp.int32, (1, TILE), 1) + at
            inside = (column >= two) & (column < two + IMG)
            for pair in range(LANES // 128):
                lanes = slice(pair * 128, pair * 128 + 128)
                mixed, lse = item(two, pair)
                out_ref[here, lanes] = out_ref[here, lanes] + mixed
                for head in range(2):
                    line = slice(2 * pair + head, 2 * pair + head + 1)
                    new = lse[:, head * TILE : head * TILE + TILE]
                    lse_ref[0, line, here] = jnp.where(inside, new, lse_ref[0, line, here])

        return more

    lax.fori_loop(0, tiles // 2, both, 0)


def attend_back_body(
    first_ref, q_ref, k_ref, v_ref, grad_ref, lse_ref, mixed_ref, dk_sum, dv_sum
):
    rows = grad_ref.shape[0]
    tiles = rows // TILE
    mixed_ref[:RIM, :LANES] = jnp.zeros((RIM, LANES), jnp.bfloat16)
    mixed_ref[RIM + rows :, :LANES] = jnp.zeros((RIM, LANES), jnp.bfloat16)
    dk_sum[...] = jnp.zeros_like(dk_sum)
    dv_sum[...] = jnp.zeros_like(dv_sum)

    def tile(j, carry):
        at = pl.multiple_of(j * TILE, TILE)
        here = pl.ds(at, TILE)
        asking = pl.ds(pl.multiple_of(at + RIM, 64), TILE)
        column = lax.broadcasted_iota(jnp.int32, (1, TILE), 1) + at

        def item(first, pair):
            lanes = slice(pair * 128, pair * 128 + 128)
            start, offset = key_window(first, k_ref.shape[0])
            window = pl.ds(start, KEYS)
            keys = k_ref[window, lanes]
            queries = paired(q_ref[asking, lanes])
            grads = paired(grad_ref[here, lanes])
            inside = (column >= first) & (column < first + IMG)
            lse = jnp.concatenate(
                [
                    jnp.where(inside, lse_ref[0, 2 * pair : 2 * pair + 1, here], -MASKED),
                    jnp.where(inside, lse_ref[0, 2 * pair + 1 : 2 * pair + 2, here], -MASKED),
                ],
                axis=1,
            )
            probs = jnp.exp(keep_image(dot_nt(keys, queries), offset) - lse)
            grad_probs = dot_nt(v_ref[window, lanes], grads)
            dv_sum[window, lanes] += dot_nn(probs.astype(jnp.bfloat16), grads)
            inner = jnp.sum(grad_probs * probs, axis=0, keepdims=True)
            grad_scores = (probs * (grad_probs - inner)).astype(jnp.bfloat16)
            dk_sum[window, lanes] += dot_nn(grad_scores, queries)
            return unpaired(dot_tn(keys, grad_scores) * HEAD_DIM**-0.5).astype(jnp.bfloat16)

        one, two = first_ref[j], first_ref[tiles + j]
        for pair in range(LANES // 128):
            mixed_ref[asking, pair * 128 : pair * 128 + 128] = item(one, pair)

        @pl.when(two != one)
        def _():
            for pair in range(LANES // 128):
                lanes = slice(pair * 128, pair * 128 + 128)
                mixed_ref[asking, lanes] = mixed_ref[asking, lanes] + item(two, pair)

        return carry

    lax.fori_loop(0, tiles, tile, 0)
    mixed_ref[:, LANES : 2 * LANES] = dk_sum[...].astype(jnp.bfloat16)
    mixed_ref[:, 2 * LANES :] = dv_sum[...].astype(jnp.bfloat16)


def attention_cost(rows, width, products):
    return pl.CostEstimate(
        flops=2 * products * 10 * TILE * KEYS * width * 8,
        bytes_accessed=16 * rows * width,
        transcendentals=10 * TILE * KEYS * (width // HEAD_DIM),
    )


def mixed_specs(ext):
    return [pl.BlockSpec((ext, LANES), lambda g, f, at=at: (0, 3 * g + at)) for at in range(3)]


def attend(firsts, mixed, rows):
    ext, width = mixed.shape[0], mixed.shape[1] // 3
    groups = width // LANES
    return pl.pallas_call(
        attend_body,
        grid_spec=pltpu.PrefetchScalarGridSpec(
            num_scalar_prefetch=1,
            grid=(groups,),
            in_specs=mixed_specs(ext),
            out_specs=[
                pl.BlockSpec((rows, LANES), lambda g, f: (0, g)),
                pl.BlockSpec((1, LANES // HEAD_DIM, rows), lambda g, f: (g, 0, 0)),
            ],
        ),
        out_shape=[
            jax.ShapeDtypeStruct((rows, width), jnp.bfloat16),
            jax.ShapeDtypeStruct((groups, LANES // HEAD_DIM, rows), jnp.float32),
        ],
        cost_estimate=attention_cost(rows, width, 3),
        name="attend",
    )(firsts, mixed, mixed, mixed)


def attend_back(firsts, mixed, grads, lse, part):
    ext, width = mixed.shape[0], mixed.shape[1] // 3
    rows = grads.shape[0]
    groups = width // LANES
    base = part * groups
    return pl.pallas_call(
        attend_back_body,
        grid_spec=pltpu.PrefetchScalarGridSpec(
            num_scalar_prefetch=1,
            grid=(groups,),
            in_specs=mixed_specs(ext)
            + [
                pl.BlockSpec((rows, LANES), lambda g, f: (0, base + g)),
                pl.BlockSpec((1, LANES // HEAD_DIM, rows), lambda g, f: (g, 0, 0)),
            ],
            out_specs=pl.BlockSpec((ext, 3 * LANES), lambda g, f: (0, g)),
            scratch_shapes=[pltpu.VMEM((ext, LANES), jnp.float32)] * 2,
        ),
        out_shape=jax.ShapeDtypeStruct((ext, 3 * width), jnp.bfloat16),
        cost_estimate=attention_cost(rows, width, 5),
        name="attend_back",
    )(firsts, mixed, mixed, mixed, grads, lse)


def into_norm_body(
    first_ref, second_ref, w_first_ref, w_second_ref, tokens_ref, out_ref, sums_ref
):
    cut = first_ref.shape[1]
    grads = dot_nt(first_ref[...], w_first_ref[...]) + dot_nt(second_ref[...], w_second_ref[...])
    out_ref[...] = grads.astype(jnp.bfloat16)
    unit = normed_parts(tokens_ref[...].astype(jnp.float32))[0]
    @pl.when(pl.program_id(0) == 0)
    def _():
        sums_ref[...] = jnp.zeros_like(sums_ref)

    sums_ref[0:1, :] += jnp.sum(grads * unit, axis=0, keepdims=True)
    sums_ref[1:2, :] += jnp.sum(grads, axis=0, keepdims=True)
    groups = cut // (3 * LANES)
    for part, ref in enumerate((first_ref, second_ref)):
        line = jnp.sum(ref[...].astype(jnp.float32), axis=0, keepdims=True)
        for group in range(groups):
            to = (part * groups + group) * LANES
            at = 3 * group * LANES
            sums_ref[2:3, to : to + LANES] += line[:, at : at + LANES]
            sums_ref[3:4, to : to + LANES] += line[:, at + 2 * LANES : at + 3 * LANES]


def into_norm(first, second, w_first, w_second, tokens):
    ext, cut = first.shape
    width = tokens.shape[1]
    steps = 4
    block = ext // steps
    whole = lambda i: (0, 0)
    return pl.pallas_call(
        into_norm_body,
        grid=(steps,),
        in_specs=[
            pl.BlockSpec((block, cut), lambda i: (i, 0)),
            pl.BlockSpec((block, cut), lambda i: (i, 0)),
            pl.BlockSpec((width, cut), whole, pipeline_mode=pl.Buffered(1)),
            pl.BlockSpec((width, cut), whole, pipeline_mode=pl.Buffered(1)),
            pl.BlockSpec((block, width), lambda i: (i, 0)),
        ],
        out_specs=[
            pl.BlockSpec((block, width), lambda i: (i, 0)),
            pl.BlockSpec((4, width), whole),
        ],
        out_shape=[
            jax.ShapeDtypeStruct((ext, width), jnp.bfloat16),
            jax.ShapeDtypeStruct((4, width), jnp.float32),
        ],
        cost_estimate=pl.CostEstimate(
            flops=4 * ext * cut * width, bytes_accessed=8 * ext * cut, transcendentals=0
        ),
        name="into_norm",
    )(first, second, w_first, w_second, tokens)


def pack_body(w_qkv_ref, w_out_ref, side_ref, first_ref, second_ref):
    width = w_out_ref.shape[1]
    groups = width // LANES // 2
    for half, ref in enumerate((first_ref, second_ref)):
        for group in range(groups):
            for which in range(3):
                at = which * width + (half * groups + group) * LANES
                to = (3 * group + which) * LANES
                ref[:, to : to + LANES] = w_qkv_ref[:, at : at + LANES]
    first_ref[:, 3 * width // 2 :] = side_ref[...]
    second_ref[:, 3 * width // 2 :] = w_out_ref[...]


def pack(w_qkv, w_out, side):
    rows, width = w_out.shape
    half = 3 * width // 2
    return pl.pallas_call(
        pack_body,
        out_shape=[
            jax.ShapeDtypeStruct((rows, half + side.shape[1]), jnp.bfloat16),
            jax.ShapeDtypeStruct((rows, half + width), jnp.bfloat16),
        ],
        name="pack",
    )(w_qkv, w_out, side)


def ungrouped(columns, which):
    width = columns.shape[-1]
    return [
        columns[..., at : at + LANES] for at in range(which * LANES, width, 3 * LANES)
    ]


def image_firsts(padding, ident):
    rows = padding.shape[0]
    tiles = rows // TILE
    real = padding == 1
    by_tile = jnp.where(real, ident, NOWHERE).reshape(tiles, TILE)
    low_id = jnp.min(by_tile, axis=1)
    high_id = jnp.max(jnp.where(real, ident, -1).reshape(tiles, TILE), axis=1)
    wanted = jnp.concatenate([low_id, high_id])
    place = jnp.arange(rows, dtype=jnp.int32)[None, :]
    mine = real[None, :] & (ident[None, :] == wanted[:, None])
    run_first = jnp.min(jnp.where(mine, place, NOWHERE), axis=1)
    run_last = jnp.max(jnp.where(mine, place, -1), axis=1)
    firsts = jnp.where(run_last < rows - 1, run_last - RIM, run_first)
    empty = jnp.concatenate([low_id, low_id]) == NOWHERE
    before = jnp.tile(jnp.arange(tiles, dtype=jnp.int32) * TILE - IMG, 2)
    return jnp.where(empty, before, firsts)


def normed_parts(values):
    centered = values - jnp.mean(values, axis=-1, keepdims=True)
    spread = jnp.mean(centered * centered, axis=-1, keepdims=True)
    scale = lax.rsqrt(spread + 1e-05)
    return centered * scale, scale


def norm_back(unit, scale, gain, grads):
    scaled = grads * gain
    return scale * (
        scaled
        - jnp.mean(scaled, axis=-1, keepdims=True)
        - unit * jnp.mean(scaled * unit, axis=-1, keepdims=True)
    )


def quick_gelu(values):
    return values * jax.nn.sigmoid(1.702 * values)


def shifted(value, by):
    size = lax.axis_size("dev")
    pairs = [(i, i + by) for i in range(size) if 0 <= i + by < size]
    return lax.ppermute(value, "dev", pairs)


class Rings:
    def __init__(self, size):
        bits = size.bit_length() - 1
        self.size = size
        self.top = bits - 2
        middle = list(range(1, self.top))
        self.orders = (middle, middle[::-1])
        self.stages = len(middle)
        halves = []
        for order in self.orders:
            blocks = [(0, r) for r in range(4)]
            for bit in order:
                blocks = blocks + [(mask ^ (1 << bit), r) for mask, r in blocks]
            halves.append(blocks)
        self.blocks = [
            halves[core] + [(mask ^ 1, r) for mask, r in halves[1 - core]] for core in range(2)
        ]

    def rotated(self, device, by):
        low = device % (1 << self.top)
        return (((device >> self.top) + by) % 4 << self.top) | low

    def permute(self, value, target):
        return lax.ppermute(value, "dev", [(i, target(i)) for i in range(self.size)])

    def turn(self, value, by):
        return self.permute(value, lambda i: self.rotated(i, by))

    def pair(self, value, stage):
        return self.permute(value, lambda i: i ^ (1 << self.orders[i & 1][stage]))

    def pairs(self, values, stage):
        return [self.pair(value, stage) for value in values]

    def swap(self, value):
        return self.permute(value, lambda i: i ^ 1)

    def owners(self):
        me = lax.axis_index("dev")
        lists = []
        for core in range(2):
            masks = np.array([mask for mask, _ in self.blocks[core]], np.int32)
            turns = np.array([r for _, r in self.blocks[core]], np.int32)
            low = (me ^ masks) & ((1 << self.top) - 1)
            lists.append((((me >> self.top) + turns) & 3) << self.top | low)
        return jnp.where(me & 1 == 0, lists[0], lists[1])

    def quad(self, block):
        return jnp.concatenate(self.quad_parts(block), axis=0)

    def quad_parts(self, block):
        return [block] + [self.turn(block, -r) for r in (1, 2, 3)]

    def all_sum(self, value):
        bit = 1
        while bit < self.size:
            value = value + self.permute(value, lambda i: i ^ bit)
            bit *= 2
        return value

    def cut(self, totals):
        at = totals[0].shape[0] // 2
        sent = [total[at:].astype(jnp.bfloat16) for total in totals]
        return [total[:at] for total in totals], sent

    def quarters(self, totals):
        rows = totals[0].shape[0] // 4
        sent = []
        for r in (1, 2, 3):
            here = slice(r * rows, (r + 1) * rows)
            sent.append(jnp.concatenate([t[here].astype(jnp.bfloat16) for t in totals], axis=1))
        return [total[:rows] for total in totals], sent

    def turned(self, parts):
        return [self.turn(part, r) for r, part in zip((1, 2, 3), parts)]


def added(kept, received):
    return [total + part.astype(jnp.float32) for total, part in zip(kept, received)]


def quarters_added(kept, received):
    sums = []
    at = 0
    for total in kept:
        for part in received:
            total = total + part[:, at : at + total.shape[1]].astype(jnp.float32)
        sums.append(total)
        at += total.shape[1]
    return sums


def joined(parts):
    return jnp.concatenate([part.astype(jnp.bfloat16) for part in parts], axis=1)


def after(value, *others):
    return lax.optimization_barrier((value, others))[0]


def shards(
    tokens,
    cotangent,
    padding,
    image_ident,
    ln1_gain,
    ln1_bias,
    w_qkv,
    b_qv,
    w_out,
    b_out,
    ln2_gain,
    ln2_bias,
    w_fc,
    b_fc,
    w_proj,
    b_proj,
):
    low = jnp.bfloat16
    wide = jnp.float32
    size = lax.axis_size("dev")
    width = w_out.shape[1]
    rows = tokens.shape[0]
    feat_rows = w_qkv.shape[0]
    smalls = (ln1_gain, ln1_bias, b_qv, b_out, ln2_gain, ln2_bias, b_fc, b_proj)
    extra = 128
    rings = Rings(size)
    owners = rings.owners()
    slots = -(-len(smalls) // feat_rows)
    slot = extra // slots
    lines = [jnp.pad(v, (0, slot - v.shape[0])) for v in smalls]
    side = []
    for at in range(0, len(lines), feat_rows):
        part = jnp.stack(lines[at : at + feat_rows])
        side.append(jnp.pad(part, ((0, feat_rows - part.shape[0]), (0, 0))))
    side = jnp.concatenate(side, axis=1)
    first_block, second_block = pack(w_qkv, w_out, side)
    part = rings.quad(first_block)
    w_second = lax.all_gather(after(second_block, part), "dev", axis=0, tiled=True)
    for stage in range(rings.stages):
        part = jnp.concatenate([part, rings.pair(part, stage)], axis=0)
    w_first = jnp.concatenate([part, rings.swap(part)], axis=0)
    mixed_half = 3 * width // 2
    full_out = w_second[:, mixed_half:]
    chosen = (owners[:, None] == jnp.arange(size, dtype=jnp.int32)[None, :])[:, :, None]
    side_turned = w_first[:, mixed_half:].reshape(size, feat_rows, extra).astype(wide)
    used = min(len(smalls), feat_rows)
    side_turned = side_turned[:, :used].reshape(size, 1, used * extra)
    side_all = jnp.sum(jnp.where(chosen, side_turned, 0.0), axis=0).reshape(size, used, extra)
    side_turned = side_turned.reshape(size, used, extra)

    def vector(sides, at):
        first = at // feat_rows * slot
        return sides[:, at % feat_rows, first : first + smalls[at].shape[0]]

    gain_turned, bias_turned = vector(side_turned, 0), vector(side_turned, 1)
    vectors = [vector(side_turned if at == 6 else side_all, at) for at in range(len(smalls))]
    vectors = [v.reshape(-1) for v in vectors]
    gain_one, bias_one, bias_qv, bias_out, gain_two, bias_two, bias_fc, bias_proj = vectors

    firsts = image_firsts(padding, image_ident)
    ext_tokens = jnp.concatenate(
        [shifted(tokens[rows - RIM :], 1), tokens, shifted(tokens[:RIM], -1)], axis=0
    )
    feature = jnp.arange(width, dtype=jnp.int32)
    wanted = (owners[:, None] * feat_rows + jnp.arange(feat_rows, dtype=jnp.int32)).reshape(-1)
    reorder = (feature[:, None] == wanted[None, :]).astype(low)
    tokens_turned = dot_nn(ext_tokens, reorder).astype(low)
    scale_one = normed_parts(ext_tokens.astype(wide))[1]
    mean_one = jnp.mean(ext_tokens.astype(wide), axis=-1, keepdims=True)
    scale_one, tokens_turned = lax.optimization_barrier((scale_one, tokens_turned))
    groups = width // LANES
    bias_q, bias_v = bias_qv.reshape(2, groups, LANES)
    bias_mixed = jnp.stack([bias_q, jnp.zeros_like(bias_q), bias_v], axis=1).reshape(-1)
    scale_mixed = np.tile(np.repeat(np.array([HEAD_DIM**-0.5, 1, 1], np.float32), LANES), groups)

    last = rings.stages - 1
    part_fc = rings.quad(after(w_fc, w_first))
    parts_proj = rings.quad_parts(after(w_proj, w_first))
    centered = tokens_turned.astype(wide) - mean_one
    normed_turned = (
        centered * scale_one * gain_turned.reshape(-1) + bias_turned.reshape(-1)
    ).astype(low)
    normed_turned = lax.optimization_barrier(normed_turned)

    def mixed_part(rows_in, w_part, columns):
        products = dot_nn(rows_in, w_part[:, :mixed_half])
        return ((products + bias_mixed[columns]) * scale_mixed[columns]).astype(low)

    mixed_first = mixed_part(normed_turned, w_first, slice(0, mixed_half))
    mixed_first, part_fc = lax.optimization_barrier((mixed_first, part_fc))
    for stage in range(last - 1):
        part_fc = jnp.concatenate([part_fc, rings.pair(part_fc, stage)], axis=0)
    pair_fc = rings.pair(part_fc, last - 1)
    first_heads, first_lse = attend(firsts, mixed_first, rows)
    first_heads, pair_fc, parts_proj = lax.optimization_barrier((first_heads, pair_fc, parts_proj))
    part_proj = jnp.concatenate(parts_proj, axis=0)
    part_fc = jnp.concatenate([part_fc, pair_fc], axis=0)
    for stage in range(last - 1):
        part_proj = jnp.concatenate([part_proj, rings.pair(part_proj, stage)], axis=0)
    pair_fc, pair_proj = rings.pair(part_fc, last), rings.pair(part_proj, last - 1)
    scale_late = after(scale_one, part_fc, part_proj)
    normed_one = ((ext_tokens.astype(wide) - mean_one) * scale_late * gain_one + bias_one).astype(low)
    mixed_second = mixed_part(normed_one, w_second, slice(mixed_half, 2 * mixed_half))
    second_heads, second_lse = attend(firsts, mixed_second, rows)
    second_heads, pair_fc, pair_proj = lax.optimization_barrier((second_heads, pair_fc, pair_proj))
    fc_own = jnp.concatenate([part_fc, pair_fc], axis=0)
    part_proj = jnp.concatenate([part_proj, pair_proj], axis=0)
    second_heads, fc_own, part_proj = lax.optimization_barrier((second_heads, fc_own, part_proj))
    fc_other = rings.swap(fc_own)
    pair_proj = rings.pair(part_proj, last)
    attended = jnp.concatenate([first_heads, second_heads], axis=1)

    middle = tokens.astype(wide) + (dot_nn(attended, full_out) + bias_out)
    unit_two, scale_two = normed_parts(middle)
    normed_two = (unit_two * gain_two + bias_two).astype(low)
    keep = padding.astype(wide)[:, None]
    grad_result = keep * cotangent.astype(wide)
    grad_result_low = grad_result.astype(low)
    half = fc_own.shape[0]

    def up(fc_part, bias_part):
        hidden, pull = jax.vjp(quick_gelu, dot_nt(normed_two, fc_part) + bias_part)
        return hidden.astype(low), pull

    def down(pull, grads, proj_part):
        return pull(dot_nt(grads, proj_part))[0].astype(low)

    gelu_own, pull_own = up(fc_own, bias_fc[:half])
    gelu_other, pull_other = up(fc_other, bias_fc[half:])
    gelu_own, gelu_other, pair_proj = lax.optimization_barrier((gelu_own, gelu_other, pair_proj))
    proj_own = jnp.concatenate([part_proj, pair_proj], axis=0)
    proj_other = rings.swap(proj_own)
    proj_cut = dot_tn(gelu_other, after(grad_result_low, proj_own)).astype(low)
    proj_sent = rings.swap(proj_cut)
    grad_hidden_own = down(pull_own, after(grad_result_low, proj_cut), proj_own)
    grad_hidden_other = down(pull_other, after(grad_result_low, grad_hidden_own), proj_other)
    fc_cut = dot_tn(grad_hidden_other, normed_two).astype(low)
    fc_sent = rings.swap(fc_cut)
    gelu_own, proj_sent = lax.optimization_barrier((after(gelu_own, fc_cut), proj_sent))
    (proj_kept,), (proj_cut,) = rings.cut(
        added([dot_tn(gelu_own, grad_result_low)], [proj_sent])
    )
    proj_sent = rings.pair(proj_cut, last)
    gelu_own = after(gelu_own, proj_cut)
    up_own, up_other = dot_nn(gelu_own, proj_own), dot_nn(gelu_other, proj_other)
    output = (keep * (middle + up_own + up_other + bias_proj)).astype(low)
    grad_hidden_own, fc_sent, output = lax.optimization_barrier((grad_hidden_own, fc_sent, output))
    (fc_kept,), (fc_cut,) = rings.cut(added([dot_tn(grad_hidden_own, normed_two)], [fc_sent]))
    fc_sent = rings.pair(fc_cut, last)
    grad_hidden_own = after(grad_hidden_own, fc_cut)
    down_own, down_other = dot_nn(grad_hidden_own, fc_own), dot_nn(grad_hidden_other, fc_other)
    down_own, proj_sent = lax.optimization_barrier((after(down_own, down_other), proj_sent))
    for stage in reversed(range(last)):
        (proj_kept,), (proj_cut,) = rings.cut(added([proj_kept], [proj_sent]))
        proj_sent = rings.pair(proj_cut, stage)
    grad_norm_two = after(down_own, proj_cut) + down_other
    grad_middle = grad_result + norm_back(unit_two, scale_two, gain_two, grad_norm_two)
    grad_branch = grad_middle.astype(low)
    grad_attended = dot_nt(grad_branch, full_out).astype(low)

    def total(values):
        return jnp.sum(values.astype(wide), axis=0)

    hidden_sums = jnp.concatenate([total(grad_hidden_own), total(grad_hidden_other)])
    hidden_sums = jnp.sum(jnp.where(chosen, hidden_sums.reshape(size, 1, -1), 0.0), axis=0)
    near, far = slice(0, width // 2), slice(width // 2, width)
    w_restored = dot_nn(reorder, w_first[:, :mixed_half]).astype(low)

    def product(lines, grads):
        return dot_tn(normed_turned[:, lines], grads)

    early_sums = jnp.concatenate(
        [
            total(grad_branch),
            total(grad_norm_two * unit_two),
            total(grad_norm_two),
            total(grad_result),
            hidden_sums.reshape(-1),
        ]
    )
    early_all = lax.all_gather(early_sums.reshape(-1, width), "dev", axis=0)
    attended_turned = dot_nn(attended, reorder).astype(low)
    grad_attended, fc_sent = lax.optimization_barrier((grad_attended, fc_sent))
    for stage in reversed(range(last)):
        (fc_kept,), (fc_cut,) = rings.cut(added([fc_kept], [fc_sent]))
        fc_sent = rings.pair(fc_cut, stage)
    mlp_kept, mlp_sent = [fc_kept, proj_kept], [fc_sent, proj_sent]
    grad_attended = after(grad_attended, fc_cut, early_sums, attended_turned)
    first = attend_back(firsts, mixed_first, grad_attended, first_lse, 0)

    first, mlp_sent = lax.optimization_barrier((first, mlp_sent))
    mlp_kept, mlp_cut = rings.quarters(added(mlp_kept, mlp_sent))
    mlp_sent = rings.turned(mlp_cut)
    first_cut = joined(
        [product(far, after(first, mlp_cut)), dot_tn(attended_turned[:, far], grad_branch)]
    )
    first_sent = rings.swap(first_cut)
    first_kept = [
        product(near, after(first, first_cut)),
        dot_tn(attended_turned[:, near], grad_branch),
    ]
    grad_attended, first_kept = lax.optimization_barrier((grad_attended, first_kept))
    second = attend_back(firsts, mixed_second, grad_attended, second_lse, 1)

    second, first_sent, mlp_sent, early_all = lax.optimization_barrier(
        (second, first_sent, mlp_sent, early_all)
    )
    first_kept, first_cut = rings.cut(quarters_added(first_kept, [first_sent]))
    first_cut = joined(first_cut)
    first_sent = rings.pair(first_cut, last)
    grad_ext, late_sums = into_norm(
        first, after(second, first_cut), w_restored, w_second, ext_tokens
    )
    ends = (grad_ext[rows + RIM :], grad_ext[:RIM])
    second, ends, first_sent = lax.optimization_barrier((second, ends, first_sent))
    head, tail = shifted(ends[0], 1), shifted(ends[1], -1)
    for stage in reversed(range(last)):
        first_kept, first_cut = rings.cut(quarters_added(first_kept, [first_sent]))
        first_cut = joined(first_cut)
        first_sent = rings.pair(first_cut, stage)
    second_cut = product(far, after(second, first_cut)).astype(low)
    second_sent = [rings.swap(second_cut)]
    second_kept = [product(near, after(second, second_cut))]
    second_sent, first_sent, second_kept, late_sums = lax.optimization_barrier(
        (second_sent, first_sent, second_kept, late_sums)
    )
    second_kept, second_cut = rings.cut(added(second_kept, second_sent))
    second_sent = rings.pairs(second_cut, last)
    first_kept, first_cut = rings.quarters(quarters_added(first_kept, [first_sent]))
    first_sent = rings.turned(first_cut)
    grad_fc, grad_proj = quarters_added(mlp_kept, mlp_sent)
    grad_own = after(grad_ext, second_cut, first_cut)[RIM : RIM + rows]
    for stage in reversed(range(last)):
        second_kept, second_cut = rings.cut(added(second_kept, second_sent))
        second_sent = rings.pairs(second_cut, stage)
    grad_norm_one = (
        grad_own.astype(wide)
        + jnp.pad(head.astype(wide), ((0, rows - RIM), (0, 0)))
        + jnp.pad(tail.astype(wide), ((rows - RIM, 0), (0, 0)))
    )
    unit_own, scale_own = normed_parts(tokens.astype(wide))
    grad_tokens = (grad_middle + norm_back(unit_own, scale_own, gain_one, grad_norm_one)).astype(low)

    second_kept, second_cut = rings.quarters(added(second_kept, second_sent))
    grad_tokens = after(grad_tokens, second_cut)
    second_sent = rings.turned(second_cut)
    grad_first, grad_out = quarters_added(first_kept, first_sent)
    (grad_second,) = quarters_added(second_kept, second_sent)
    me = lax.axis_index("dev")

    def share(sums, at, count):
        return lax.dynamic_slice_in_dim(sums[at : at + count].reshape(-1), me * (count * feat_rows), count * feat_rows)

    late, early = rings.all_sum(late_sums), jnp.sum(early_all, axis=0)
    small_outs = (
        share(late, 0, 1),
        share(late, 1, 1),
        share(late, 2, 2),
        share(early, 0, 1),
        share(early, 1, 1),
        share(early, 2, 1),
        share(early, 4, early.shape[0] - 4),
        share(early, 3, 1),
    )
    grad_mixed = jnp.concatenate([grad_first, grad_second], axis=1)
    columns = [part for which in range(3) for part in ungrouped(grad_mixed, which)]
    return (
        output,
        grad_tokens,
        small_outs[0],
        small_outs[1],
        jnp.concatenate(columns, axis=1),
        small_outs[2],
        grad_out,
        small_outs[3],
        small_outs[4],
        small_outs[5],
        grad_fc,
        small_outs[6],
        grad_proj,
        small_outs[7],
    )


def solution(mesh):
    row = P("dev", None)
    line = P("dev")
    return jax.shard_map(
        shards,
        mesh=mesh,
        in_specs=(row, row, line, line, line, line, row, line, row, line, line, line, row, line, row, line),
        out_specs=(row, row, line, line, row, line, row, line, line, line, row, line, row, line),
        check_vma=False,
    )
```

```python
import jax
import jax.numpy as jnp
import numpy as np
from jax import lax
from jax.experimental import pallas as pl
from jax.experimental.pallas import tpu as pltpu
from jax.sharding import PartitionSpec as P


HEAD_DIM = 64
IMG = 577
RIM = IMG - 1
TILE = 128
KEYS = 592
LANES = 256
MASKED = -1e30
NOWHERE = 1 << 20


def dot_nt(a, b):
    return lax.dot_general(a, b, (((1,), (1,)), ((), ())), preferred_element_type=jnp.float32)


def dot_tn(a, b):
    return lax.dot_general(a, b, (((0,), (0,)), ((), ())), preferred_element_type=jnp.float32)


def dot_nn(a, b):
    return lax.dot_general(a, b, (((1,), (0,)), ((), ())), preferred_element_type=jnp.float32)


def paired(block):
    first = lax.broadcasted_iota(jnp.int32, block.shape, 1) < HEAD_DIM
    none = jnp.zeros_like(block)
    return jnp.concatenate([jnp.where(first, block, none), jnp.where(first, none, block)], axis=0)


def unpaired(wide):
    both = jnp.concatenate([wide[:HEAD_DIM, :TILE], wide[HEAD_DIM:, TILE:]], axis=0)
    return both.T


def key_window(first, ext_rows):
    low = first + RIM
    start = jnp.clip((low // 16) * 16, 0, ext_rows - KEYS)
    return pl.multiple_of(start, 16), low - start


def keep_image(scores, offset):
    edge = lax.broadcasted_iota(jnp.int32, (16, scores.shape[1]), 0)
    top = jnp.where(edge >= offset, scores[:16], MASKED)
    low = jnp.where(edge + (KEYS - 16) < offset + IMG, scores[KEYS - 16 :], MASKED)
    return jnp.concatenate([top, scores[16 : KEYS - 16], low], axis=0)


def attend_body(first_ref, q_ref, k_ref, v_ref, out_ref, lse_ref):
    tiles = out_ref.shape[0] // TILE

    def both(step, carry):
        pending = [tile(2 * step + k) for k in range(2)]
        for more in pending:
            more()
        return carry

    def tile(j):
        at = pl.multiple_of(j * TILE, TILE)
        here = pl.ds(at, TILE)
        asking = pl.ds(pl.multiple_of(at + RIM, 64), TILE)

        def item(first, pair):
            lanes = slice(pair * 128, pair * 128 + 128)
            start, offset = key_window(first, k_ref.shape[0])
            scores = dot_nt(k_ref[pl.ds(start, KEYS), lanes], paired(q_ref[asking, lanes]))
            scores = keep_image(scores, offset)
            peak = jnp.max(scores, axis=0, keepdims=True)
            weights = jnp.exp(scores - peak)
            total = jnp.sum(weights, axis=0, keepdims=True)
            mixed = dot_tn(v_ref[pl.ds(start, KEYS), lanes], weights.astype(jnp.bfloat16))
            mixed = unpaired(mixed / total)
            row = lax.broadcasted_iota(jnp.int32, (TILE, 128), 0) + at
            inside = (row >= first) & (row < first + IMG)
            return jnp.where(inside, mixed, 0.0).astype(jnp.bfloat16), peak + jnp.log(total)

        one, two = first_ref[j], first_ref[tiles + j]
        for pair in range(LANES // 128):
            mixed, lse = item(one, pair)
            out_ref[here, pair * 128 : pair * 128 + 128] = mixed
            lse_ref[0, 2 * pair : 2 * pair + 1, here] = lse[:, :TILE]
            lse_ref[0, 2 * pair + 1 : 2 * pair + 2, here] = lse[:, TILE:]

        def more():
            @pl.when(two != one)
            def _():
                fill()

        def fill():
            column = lax.broadcasted_iota(jnp.int32, (1, TILE), 1) + at
            inside = (column >= two) & (column < two + IMG)
            for pair in range(LANES // 128):
                lanes = slice(pair * 128, pair * 128 + 128)
                mixed, lse = item(two, pair)
                out_ref[here, lanes] = out_ref[here, lanes] + mixed
                for head in range(2):
                    line = slice(2 * pair + head, 2 * pair + head + 1)
                    new = lse[:, head * TILE : head * TILE + TILE]
                    lse_ref[0, line, here] = jnp.where(inside, new, lse_ref[0, line, here])

        return more

    lax.fori_loop(0, tiles // 2, both, 0)


def attend_back_body(
    first_ref, q_ref, k_ref, v_ref, grad_ref, lse_ref, mixed_ref, dk_sum, dv_sum
):
    rows = grad_ref.shape[0]
    tiles = rows // TILE
    mixed_ref[:RIM, :LANES] = jnp.zeros((RIM, LANES), jnp.bfloat16)
    mixed_ref[RIM + rows :, :LANES] = jnp.zeros((RIM, LANES), jnp.bfloat16)
    dk_sum[...] = jnp.zeros_like(dk_sum)
    dv_sum[...] = jnp.zeros_like(dv_sum)

    def tile(j, carry):
        at = pl.multiple_of(j * TILE, TILE)
        here = pl.ds(at, TILE)
        asking = pl.ds(pl.multiple_of(at + RIM, 64), TILE)
        column = lax.broadcasted_iota(jnp.int32, (1, TILE), 1) + at

        def item(first, pair):
            lanes = slice(pair * 128, pair * 128 + 128)
            start, offset = key_window(first, k_ref.shape[0])
            window = pl.ds(start, KEYS)
            keys = k_ref[window, lanes]
            queries = paired(q_ref[asking, lanes])
            grads = paired(grad_ref[here, lanes])
            inside = (column >= first) & (column < first + IMG)
            lse = jnp.concatenate(
                [
                    jnp.where(inside, lse_ref[0, 2 * pair : 2 * pair + 1, here], -MASKED),
                    jnp.where(inside, lse_ref[0, 2 * pair + 1 : 2 * pair + 2, here], -MASKED),
                ],
                axis=1,
            )
            probs = jnp.exp(keep_image(dot_nt(keys, queries), offset) - lse)
            grad_probs = dot_nt(v_ref[window, lanes], grads)
            dv_sum[window, lanes] += dot_nn(probs.astype(jnp.bfloat16), grads)
            inner = jnp.sum(grad_probs * probs, axis=0, keepdims=True)
            grad_scores = (probs * (grad_probs - inner)).astype(jnp.bfloat16)
            dk_sum[window, lanes] += dot_nn(grad_scores, queries)
            return unpaired(dot_tn(keys, grad_scores) * HEAD_DIM**-0.5).astype(jnp.bfloat16)

        one, two = first_ref[j], first_ref[tiles + j]
        for pair in range(LANES // 128):
            mixed_ref[asking, pair * 128 : pair * 128 + 128] = item(one, pair)

        @pl.when(two != one)
        def _():
            for pair in range(LANES // 128):
                lanes = slice(pair * 128, pair * 128 + 128)
                mixed_ref[asking, lanes] = mixed_ref[asking, lanes] + item(two, pair)

        return carry

    lax.fori_loop(0, tiles, tile, 0)
    mixed_ref[:, LANES : 2 * LANES] = dk_sum[...].astype(jnp.bfloat16)
    mixed_ref[:, 2 * LANES :] = dv_sum[...].astype(jnp.bfloat16)


def attention_cost(rows, width, products):
    return pl.CostEstimate(
        flops=2 * products * 10 * TILE * KEYS * width * 8,
        bytes_accessed=16 * rows * width,
        transcendentals=10 * TILE * KEYS * (width // HEAD_DIM),
    )


def mixed_specs(ext):
    return [pl.BlockSpec((ext, LANES), lambda g, f, at=at: (0, 3 * g + at)) for at in range(3)]


def attend(firsts, mixed, rows):
    ext, width = mixed.shape[0], mixed.shape[1] // 3
    groups = width // LANES
    return pl.pallas_call(
        attend_body,
        grid_spec=pltpu.PrefetchScalarGridSpec(
            num_scalar_prefetch=1,
            grid=(groups,),
            in_specs=mixed_specs(ext),
            out_specs=[
                pl.BlockSpec((rows, LANES), lambda g, f: (0, g)),
                pl.BlockSpec((1, LANES // HEAD_DIM, rows), lambda g, f: (g, 0, 0)),
            ],
        ),
        out_shape=[
            jax.ShapeDtypeStruct((rows, width), jnp.bfloat16),
            jax.ShapeDtypeStruct((groups, LANES // HEAD_DIM, rows), jnp.float32),
        ],
        cost_estimate=attention_cost(rows, width, 3),
        name="attend",
    )(firsts, mixed, mixed, mixed)


def attend_back(firsts, mixed, grads, lse, part):
    ext, width = mixed.shape[0], mixed.shape[1] // 3
    rows = grads.shape[0]
    groups = width // LANES
    base = part * groups
    return pl.pallas_call(
        attend_back_body,
        grid_spec=pltpu.PrefetchScalarGridSpec(
            num_scalar_prefetch=1,
            grid=(groups,),
            in_specs=mixed_specs(ext)
            + [
                pl.BlockSpec((rows, LANES), lambda g, f: (0, base + g)),
                pl.BlockSpec((1, LANES // HEAD_DIM, rows), lambda g, f: (g, 0, 0)),
            ],
            out_specs=pl.BlockSpec((ext, 3 * LANES), lambda g, f: (0, g)),
            scratch_shapes=[pltpu.VMEM((ext, LANES), jnp.float32)] * 2,
        ),
        out_shape=jax.ShapeDtypeStruct((ext, 3 * width), jnp.bfloat16),
        cost_estimate=attention_cost(rows, width, 5),
        name="attend_back",
    )(firsts, mixed, mixed, mixed, grads, lse)


def into_norm_body(
    first_ref, second_ref, w_first_ref, w_second_ref, tokens_ref, out_ref, sums_ref
):
    cut = first_ref.shape[1]
    grads = dot_nt(first_ref[...], w_first_ref[...]) + dot_nt(second_ref[...], w_second_ref[...])
    out_ref[...] = grads.astype(jnp.bfloat16)
    unit = normed_parts(tokens_ref[...].astype(jnp.float32))[0]
    @pl.when(pl.program_id(0) == 0)
    def _():
        sums_ref[...] = jnp.zeros_like(sums_ref)

    sums_ref[0:1, :] += jnp.sum(grads * unit, axis=0, keepdims=True)
    sums_ref[1:2, :] += jnp.sum(grads, axis=0, keepdims=True)
    groups = cut // (3 * LANES)
    for part, ref in enumerate((first_ref, second_ref)):
        line = jnp.sum(ref[...].astype(jnp.float32), axis=0, keepdims=True)
        for group in range(groups):
            to = (part * groups + group) * LANES
            at = 3 * group * LANES
            sums_ref[2:3, to : to + LANES] += line[:, at : at + LANES]
            sums_ref[3:4, to : to + LANES] += line[:, at + 2 * LANES : at + 3 * LANES]


def into_norm(first, second, w_first, w_second, tokens):
    ext, cut = first.shape
    width = tokens.shape[1]
    steps = 4
    block = ext // steps
    whole = lambda i: (0, 0)
    return pl.pallas_call(
        into_norm_body,
        grid=(steps,),
        in_specs=[
            pl.BlockSpec((block, cut), lambda i: (i, 0)),
            pl.BlockSpec((block, cut), lambda i: (i, 0)),
            pl.BlockSpec((width, cut), whole, pipeline_mode=pl.Buffered(1)),
            pl.BlockSpec((width, cut), whole, pipeline_mode=pl.Buffered(1)),
            pl.BlockSpec((block, width), lambda i: (i, 0)),
        ],
        out_specs=[
            pl.BlockSpec((block, width), lambda i: (i, 0)),
            pl.BlockSpec((4, width), whole),
        ],
        out_shape=[
            jax.ShapeDtypeStruct((ext, width), jnp.bfloat16),
            jax.ShapeDtypeStruct((4, width), jnp.float32),
        ],
        cost_estimate=pl.CostEstimate(
            flops=4 * ext * cut * width, bytes_accessed=8 * ext * cut, transcendentals=0
        ),
        name="into_norm",
    )(first, second, w_first, w_second, tokens)


def pack_body(w_qkv_ref, w_out_ref, side_ref, first_ref, second_ref):
    width = w_out_ref.shape[1]
    groups = width // LANES // 2
    for half, ref in enumerate((first_ref, second_ref)):
        for group in range(groups):
            for which in range(3):
                at = which * width + (half * groups + group) * LANES
                to = (3 * group + which) * LANES
                ref[:, to : to + LANES] = w_qkv_ref[:, at : at + LANES]
    first_ref[:, 3 * width // 2 :] = side_ref[...]
    second_ref[:, 3 * width // 2 :] = w_out_ref[...]


def pack(w_qkv, w_out, side):
    rows, width = w_out.shape
    half = 3 * width // 2
    return pl.pallas_call(
        pack_body,
        out_shape=[
            jax.ShapeDtypeStruct((rows, half + side.shape[1]), jnp.bfloat16),
            jax.ShapeDtypeStruct((rows, half + width), jnp.bfloat16),
        ],
        name="pack",
    )(w_qkv, w_out, side)


def ungrouped(columns, which):
    width = columns.shape[-1]
    return [
        columns[..., at : at + LANES] for at in range(which * LANES, width, 3 * LANES)
    ]


def image_firsts(padding, ident):
    rows = padding.shape[0]
    tiles = rows // TILE
    real = padding == 1
    by_tile = jnp.where(real, ident, NOWHERE).reshape(tiles, TILE)
    low_id = jnp.min(by_tile, axis=1)
    high_id = jnp.max(jnp.where(real, ident, -1).reshape(tiles, TILE), axis=1)
    wanted = jnp.concatenate([low_id, high_id])
    place = jnp.arange(rows, dtype=jnp.int32)[None, :]
    mine = real[None, :] & (ident[None, :] == wanted[:, None])
    run_first = jnp.min(jnp.where(mine, place, NOWHERE), axis=1)
    run_last = jnp.max(jnp.where(mine, place, -1), axis=1)
    firsts = jnp.where(run_last < rows - 1, run_last - RIM, run_first)
    empty = jnp.concatenate([low_id, low_id]) == NOWHERE
    before = jnp.tile(jnp.arange(tiles, dtype=jnp.int32) * TILE - IMG, 2)
    return jnp.where(empty, before, firsts)


def normed_parts(values):
    centered = values - jnp.mean(values, axis=-1, keepdims=True)
    spread = jnp.mean(centered * centered, axis=-1, keepdims=True)
    scale = lax.rsqrt(spread + 1e-05)
    return centered * scale, scale


def norm_back(unit, scale, gain, grads):
    scaled = grads * gain
    return scale * (
        scaled
        - jnp.mean(scaled, axis=-1, keepdims=True)
        - unit * jnp.mean(scaled * unit, axis=-1, keepdims=True)
    )


def quick_gelu(values):
    return values * jax.nn.sigmoid(1.702 * values)


def shifted(value, by):
    size = lax.axis_size("dev")
    pairs = [(i, i + by) for i in range(size) if 0 <= i + by < size]
    return lax.ppermute(value, "dev", pairs)


class Rings:
    def __init__(self, size):
        bits = size.bit_length() - 1
        self.size = size
        self.top = bits - 2
        middle = list(range(1, self.top))
        self.orders = (middle, middle[::-1])
        self.stages = len(middle)
        halves = []
        for order in self.orders:
            blocks = [(0, r) for r in range(4)]
            for bit in order:
                blocks = blocks + [(mask ^ (1 << bit), r) for mask, r in blocks]
            halves.append(blocks)
        self.blocks = [
            halves[core] + [(mask ^ 1, r) for mask, r in halves[1 - core]] for core in range(2)
        ]

    def rotated(self, device, by):
        low = device % (1 << self.top)
        return (((device >> self.top) + by) % 4 << self.top) | low

    def permute(self, value, target):
        return lax.ppermute(value, "dev", [(i, target(i)) for i in range(self.size)])

    def turn(self, value, by):
        return self.permute(value, lambda i: self.rotated(i, by))

    def pair(self, value, stage):
        return self.permute(value, lambda i: i ^ (1 << self.orders[i & 1][stage]))

    def pairs(self, values, stage):
        return [self.pair(value, stage) for value in values]

    def swap(self, value):
        return self.permute(value, lambda i: i ^ 1)

    def owners(self):
        me = lax.axis_index("dev")
        lists = []
        for core in range(2):
            masks = np.array([mask for mask, _ in self.blocks[core]], np.int32)
            turns = np.array([r for _, r in self.blocks[core]], np.int32)
            low = (me ^ masks) & ((1 << self.top) - 1)
            lists.append((((me >> self.top) + turns) & 3) << self.top | low)
        return jnp.where(me & 1 == 0, lists[0], lists[1])

    def quad(self, block):
        return jnp.concatenate(self.quad_parts(block), axis=0)

    def quad_parts(self, block):
        return [block] + [self.turn(block, -r) for r in (1, 2, 3)]

    def gathered(self, block):
        part = self.quad(block)
        for stage in range(self.stages):
            part = jnp.concatenate([part, self.pair(part, stage)], axis=0)
        return jnp.concatenate([part, self.swap(part)], axis=0)

    def all_sum(self, value):
        bit = 1
        while bit < self.size:
            value = value + self.permute(value, lambda i: i ^ bit)
            bit *= 2
        return value

    def cut(self, totals):
        at = totals[0].shape[0] // 2
        sent = [total[at:].astype(jnp.bfloat16) for total in totals]
        return [total[:at] for total in totals], sent

    def quarters(self, totals):
        rows = totals[0].shape[0] // 4
        sent = []
        for r in (1, 2, 3):
            here = slice(r * rows, (r + 1) * rows)
            sent.append(jnp.concatenate([t[here].astype(jnp.bfloat16) for t in totals], axis=1))
        return [total[:rows] for total in totals], sent

    def turned(self, parts):
        return [self.turn(part, r) for r, part in zip((1, 2, 3), parts)]


def added(kept, received):
    return [total + part.astype(jnp.float32) for total, part in zip(kept, received)]


def quarters_added(kept, received):
    sums = []
    at = 0
    for total in kept:
        for part in received:
            total = total + part[:, at : at + total.shape[1]].astype(jnp.float32)
        sums.append(total)
        at += total.shape[1]
    return sums


def joined(parts):
    return jnp.concatenate([part.astype(jnp.bfloat16) for part in parts], axis=1)


def after(value, *others):
    return lax.optimization_barrier((value, others))[0]


def shards(
    tokens,
    cotangent,
    padding,
    image_ident,
    ln1_gain,
    ln1_bias,
    w_qkv,
    b_qv,
    w_out,
    b_out,
    ln2_gain,
    ln2_bias,
    w_fc,
    b_fc,
    w_proj,
    b_proj,
):
    low = jnp.bfloat16
    wide = jnp.float32
    size = lax.axis_size("dev")
    width = w_out.shape[1]
    rows = tokens.shape[0]
    feat_rows = w_qkv.shape[0]
    smalls = (ln1_gain, ln1_bias, b_qv, b_out, ln2_gain, ln2_bias, b_fc, b_proj)
    extra = 128
    rings = Rings(size)
    owners = rings.owners()
    slots = -(-len(smalls) // feat_rows)
    slot = extra // slots
    lines = [jnp.pad(v, (0, slot - v.shape[0])) for v in smalls]
    side = []
    for at in range(0, len(lines), feat_rows):
        part = jnp.stack(lines[at : at + feat_rows])
        side.append(jnp.pad(part, ((0, feat_rows - part.shape[0]), (0, 0))))
    side = jnp.concatenate(side, axis=1)
    first_block, second_block = pack(w_qkv, w_out, side)
    w_second = lax.all_gather(second_block, "dev", axis=0, tiled=True)
    w_first = rings.gathered(first_block)
    mixed_half = 3 * width // 2
    full_out = w_second[:, mixed_half:]
    chosen = (owners[:, None] == jnp.arange(size, dtype=jnp.int32)[None, :])[:, :, None]
    side_turned = w_first[:, mixed_half:].reshape(size, feat_rows, extra).astype(wide)
    used = min(len(smalls), feat_rows)
    side_turned = side_turned[:, :used].reshape(size, 1, used * extra)
    side_all = jnp.sum(jnp.where(chosen, side_turned, 0.0), axis=0).reshape(size, used, extra)
    side_turned = side_turned.reshape(size, used, extra)

    def vector(sides, at):
        first = at // feat_rows * slot
        return sides[:, at % feat_rows, first : first + smalls[at].shape[0]]

    gain_turned, bias_turned = vector(side_turned, 0), vector(side_turned, 1)
    vectors = [vector(side_turned if at == 6 else side_all, at) for at in range(len(smalls))]
    vectors = [v.reshape(-1) for v in vectors]
    gain_one, bias_one, bias_qv, bias_out, gain_two, bias_two, bias_fc, bias_proj = vectors

    firsts = image_firsts(padding, image_ident)
    ext_tokens = jnp.concatenate(
        [shifted(tokens[rows - RIM :], 1), tokens, shifted(tokens[:RIM], -1)], axis=0
    )
    feature = jnp.arange(width, dtype=jnp.int32)
    wanted = (owners[:, None] * feat_rows + jnp.arange(feat_rows, dtype=jnp.int32)).reshape(-1)
    reorder = (feature[:, None] == wanted[None, :]).astype(low)
    tokens_turned = dot_nn(ext_tokens, reorder).astype(low)
    scale_one = normed_parts(ext_tokens.astype(wide))[1]
    mean_one = jnp.mean(ext_tokens.astype(wide), axis=-1, keepdims=True)
    scale_one, tokens_turned = lax.optimization_barrier((scale_one, tokens_turned))
    groups = width // LANES
    bias_q, bias_v = bias_qv.reshape(2, groups, LANES)
    bias_mixed = jnp.stack([bias_q, jnp.zeros_like(bias_q), bias_v], axis=1).reshape(-1)
    scale_mixed = np.tile(np.repeat(np.array([HEAD_DIM**-0.5, 1, 1], np.float32), LANES), groups)

    last = rings.stages - 1
    parts_fc = rings.quad_parts(after(w_fc, w_first))
    parts_proj = rings.quad_parts(after(w_proj, w_first))
    centered = tokens_turned.astype(wide) - mean_one
    normed_turned = (
        centered * scale_one * gain_turned.reshape(-1) + bias_turned.reshape(-1)
    ).astype(low)
    normed_turned = lax.optimization_barrier(normed_turned)

    def mixed_part(rows_in, w_part, columns):
        products = dot_nn(rows_in, w_part[:, :mixed_half])
        return ((products + bias_mixed[columns]) * scale_mixed[columns]).astype(low)

    mixed_first = mixed_part(normed_turned, w_first, slice(0, mixed_half))
    first_heads, first_lse = attend(firsts, mixed_first, rows)
    first_heads, parts_fc, parts_proj = lax.optimization_barrier(
        (first_heads, parts_fc, parts_proj)
    )
    part_fc, part_proj = jnp.concatenate(parts_fc, axis=0), jnp.concatenate(parts_proj, axis=0)
    for stage in range(last - 1):
        part_fc = jnp.concatenate([part_fc, rings.pair(part_fc, stage)], axis=0)
        part_proj = jnp.concatenate([part_proj, rings.pair(part_proj, stage)], axis=0)
    pair_fc, pair_proj = rings.pair(part_fc, last - 1), rings.pair(part_proj, last - 1)
    scale_late = after(scale_one, part_fc, part_proj)
    normed_one = ((ext_tokens.astype(wide) - mean_one) * scale_late * gain_one + bias_one).astype(low)
    mixed_second = mixed_part(normed_one, w_second, slice(mixed_half, 2 * mixed_half))
    mixed_second, pair_fc = lax.optimization_barrier((mixed_second, pair_fc))
    part_fc = jnp.concatenate([part_fc, pair_fc], axis=0)
    pair_fc = rings.pair(part_fc, last)
    second_heads, second_lse = attend(firsts, after(mixed_second, part_fc), rows)
    second_heads, pair_fc, pair_proj = lax.optimization_barrier((second_heads, pair_fc, pair_proj))
    fc_own = jnp.concatenate([part_fc, pair_fc], axis=0)
    part_proj = jnp.concatenate([part_proj, pair_proj], axis=0)
    second_heads, fc_own, part_proj = lax.optimization_barrier((second_heads, fc_own, part_proj))
    fc_other = rings.swap(fc_own)
    pair_proj = rings.pair(part_proj, last)
    attended = jnp.concatenate([first_heads, second_heads], axis=1)

    middle = tokens.astype(wide) + (dot_nn(attended, full_out) + bias_out)
    unit_two, scale_two = normed_parts(middle)
    normed_two = (unit_two * gain_two + bias_two).astype(low)
    keep = padding.astype(wide)[:, None]
    grad_result = keep * cotangent.astype(wide)
    grad_result_low = grad_result.astype(low)
    half = fc_own.shape[0]

    def up(fc_part, bias_part):
        hidden, pull = jax.vjp(quick_gelu, dot_nt(normed_two, fc_part) + bias_part)
        return hidden.astype(low), pull

    def down(pull, grads, proj_part):
        return pull(dot_nt(grads, proj_part))[0].astype(low)

    gelu_own, pull_own = up(fc_own, bias_fc[:half])
    gelu_other, pull_other = up(fc_other, bias_fc[half:])
    gelu_own, gelu_other, pair_proj = lax.optimization_barrier((gelu_own, gelu_other, pair_proj))
    proj_own = jnp.concatenate([part_proj, pair_proj], axis=0)
    proj_other = rings.swap(proj_own)
    proj_cut = dot_tn(gelu_other, after(grad_result_low, proj_own)).astype(low)
    proj_sent = rings.swap(proj_cut)
    grad_hidden_own = down(pull_own, after(grad_result_low, proj_cut), proj_own)
    grad_hidden_other = down(pull_other, after(grad_result_low, grad_hidden_own), proj_other)
    fc_cut = dot_tn(grad_hidden_other, normed_two).astype(low)
    fc_sent = rings.swap(fc_cut)
    gelu_own, proj_sent = lax.optimization_barrier((after(gelu_own, fc_cut), proj_sent))
    (proj_kept,), (proj_cut,) = rings.cut(
        added([dot_tn(gelu_own, grad_result_low)], [proj_sent])
    )
    proj_sent = rings.pair(proj_cut, last)
    gelu_own = after(gelu_own, proj_cut)
    up_own, up_other = dot_nn(gelu_own, proj_own), dot_nn(gelu_other, proj_other)
    output = (keep * (middle + up_own + up_other + bias_proj)).astype(low)
    grad_hidden_own, fc_sent, output = lax.optimization_barrier((grad_hidden_own, fc_sent, output))
    (fc_kept,), (fc_cut,) = rings.cut(added([dot_tn(grad_hidden_own, normed_two)], [fc_sent]))
    fc_sent = rings.pair(fc_cut, last)
    grad_hidden_own = after(grad_hidden_own, fc_cut)
    down_own, down_other = dot_nn(grad_hidden_own, fc_own), dot_nn(grad_hidden_other, fc_other)
    down_own, proj_sent = lax.optimization_barrier((after(down_own, down_other), proj_sent))
    for stage in reversed(range(last)):
        (proj_kept,), (proj_cut,) = rings.cut(added([proj_kept], [proj_sent]))
        proj_sent = rings.pair(proj_cut, stage)
    grad_norm_two = after(down_own, proj_cut) + down_other
    grad_middle = grad_result + norm_back(unit_two, scale_two, gain_two, grad_norm_two)
    grad_branch = grad_middle.astype(low)
    grad_attended = dot_nt(grad_branch, full_out).astype(low)

    def total(values):
        return jnp.sum(values.astype(wide), axis=0)

    hidden_sums = jnp.concatenate([total(grad_hidden_own), total(grad_hidden_other)])
    hidden_sums = jnp.sum(jnp.where(chosen, hidden_sums.reshape(size, 1, -1), 0.0), axis=0)
    near, far = slice(0, width // 2), slice(width // 2, width)
    w_restored = dot_nn(reorder, w_first[:, :mixed_half]).astype(low)

    def product(lines, grads):
        return dot_tn(normed_turned[:, lines], grads)

    early_sums = jnp.concatenate(
        [
            total(grad_branch),
            total(grad_norm_two * unit_two),
            total(grad_norm_two),
            total(grad_result),
            hidden_sums.reshape(-1),
        ]
    )
    early_all = lax.all_gather(early_sums.reshape(-1, width), "dev", axis=0)
    attended_turned = dot_nn(attended, reorder).astype(low)
    grad_attended, fc_sent = lax.optimization_barrier((grad_attended, fc_sent))
    for stage in reversed(range(last)):
        (fc_kept,), (fc_cut,) = rings.cut(added([fc_kept], [fc_sent]))
        fc_sent = rings.pair(fc_cut, stage)
    mlp_kept, mlp_sent = [fc_kept, proj_kept], [fc_sent, proj_sent]
    grad_attended = after(grad_attended, fc_cut, early_sums, attended_turned)
    first = attend_back(firsts, mixed_first, grad_attended, first_lse, 0)

    first, mlp_sent = lax.optimization_barrier((first, mlp_sent))
    mlp_kept, mlp_cut = rings.quarters(added(mlp_kept, mlp_sent))
    mlp_sent = rings.turned(mlp_cut)
    first_cut = joined(
        [product(far, after(first, mlp_cut)), dot_tn(attended_turned[:, far], grad_branch)]
    )
    first_sent = rings.swap(first_cut)
    first_kept = [
        product(near, after(first, first_cut)),
        dot_tn(attended_turned[:, near], grad_branch),
    ]
    grad_attended, first_kept = lax.optimization_barrier((grad_attended, first_kept))
    second = attend_back(firsts, mixed_second, grad_attended, second_lse, 1)

    second, first_sent, mlp_sent, early_all = lax.optimization_barrier(
        (second, first_sent, mlp_sent, early_all)
    )
    first_kept, first_cut = rings.cut(quarters_added(first_kept, [first_sent]))
    first_cut = joined(first_cut)
    first_sent = rings.pair(first_cut, last)
    second_cut = product(far, after(second, first_cut)).astype(low)
    second_sent = [rings.swap(second_cut)]
    second_kept = [product(near, after(second, second_cut))]
    second_sent, first_sent, second_kept = lax.optimization_barrier(
        (second_sent, first_sent, second_kept)
    )
    second_kept, second_cut = rings.cut(added(second_kept, second_sent))
    second_sent = rings.pairs(second_cut, last)
    for stage in reversed(range(last)):
        first_kept, first_cut = rings.cut(quarters_added(first_kept, [first_sent]))
        first_cut = joined(first_cut)
        first_sent = rings.pair(first_cut, stage)
    grad_ext, late_sums = into_norm(
        first, after(second, second_cut, first_cut), w_restored, w_second, ext_tokens
    )
    head, tail = shifted(grad_ext[rows + RIM :], 1), shifted(grad_ext[:RIM], -1)
    first_sent, second_sent, late_sums = lax.optimization_barrier(
        (first_sent, second_sent, late_sums)
    )
    for stage in reversed(range(last)):
        second_kept, second_cut = rings.cut(added(second_kept, second_sent))
        second_sent = rings.pairs(second_cut, stage)
    first_kept, first_cut = rings.quarters(quarters_added(first_kept, [first_sent]))
    first_sent = rings.turned(first_cut)
    grad_fc, grad_proj = quarters_added(mlp_kept, mlp_sent)
    grad_own, grad_fc, grad_proj, second_sent = lax.optimization_barrier(
        (after(grad_ext, second_cut, first_cut)[RIM : RIM + rows], grad_fc, grad_proj, second_sent)
    )
    second_kept, second_cut = rings.quarters(added(second_kept, second_sent))
    second_sent = rings.turned(second_cut)
    grad_norm_one = (
        after(grad_own, second_cut).astype(wide)
        + jnp.pad(head.astype(wide), ((0, rows - RIM), (0, 0)))
        + jnp.pad(tail.astype(wide), ((rows - RIM, 0), (0, 0)))
    )
    unit_own, scale_own = normed_parts(tokens.astype(wide))
    grad_tokens = (grad_middle + norm_back(unit_own, scale_own, gain_one, grad_norm_one)).astype(low)

    grad_tokens, second_sent = lax.optimization_barrier((grad_tokens, second_sent))
    grad_first, grad_out = quarters_added(first_kept, first_sent)
    (grad_second,) = quarters_added(second_kept, second_sent)
    me = lax.axis_index("dev")

    def share(sums, at, count):
        return lax.dynamic_slice_in_dim(sums[at : at + count].reshape(-1), me * (count * feat_rows), count * feat_rows)

    late, early = rings.all_sum(late_sums), jnp.sum(early_all, axis=0)
    small_outs = (
        share(late, 0, 1),
        share(late, 1, 1),
        share(late, 2, 2),
        share(early, 0, 1),
        share(early, 1, 1),
        share(early, 2, 1),
        share(early, 4, early.shape[0] - 4),
        share(early, 3, 1),
    )
    grad_mixed = jnp.concatenate([grad_first, grad_second], axis=1)
    columns = [part for which in range(3) for part in ungrouped(grad_mixed, which)]
    return (
        output,
        grad_tokens,
        small_outs[0],
        small_outs[1],
        jnp.concatenate(columns, axis=1),
        small_outs[2],
        grad_out,
        small_outs[3],
        small_outs[4],
        small_outs[5],
        grad_fc,
        small_outs[6],
        grad_proj,
        small_outs[7],
    )


def solution(mesh):
    row = P("dev", None)
    line = P("dev")
    return jax.shard_map(
        shards,
        mesh=mesh,
        in_specs=(row, row, line, line, line, line, row, line, row, line, line, line, row, line, row, line),
        out_specs=(row, row, line, line, row, line, row, line, line, line, row, line, row, line),
        check_vma=False,
    )
```
